128 devices in a mesh: gx: 8 (over x, core), gy: 16 (over z, y).
Axes of the slice: x: 4, y: 4, z: 4, core: 2. Of those that a mesh axis runs over, the one named last changes fastest.
Arguments:
- potential_heat: float32 [3, 384, 12288], P(None, 'gx', 'gy'), may hold values from -6 to 6
- easterly_speed: float32 [3, 384, 12288], P(None, 'gx', 'gy'), may hold values from -6 to 6
- poleward_speed: float32 [3, 384, 12288], P(None, 'gx', 'gy'), may hold values from -6 to 6
- sea_elevation: float32 [384, 12288], P('gx', 'gy'), may hold values from -6 to 6
- averaged_easterly_speed: float32 [384, 12288], P('gx', 'gy'), may hold values from -6 to 6
- averaged_poleward_speed: float32 [384, 12288], P('gx', 'gy'), may hold values from -6 to 6
- seafloor_distance: float32 [384, 12288], P('gx', 'gy'), may hold values from 0.5 to 2
- marine_indicator: int32 [384, 12288], P('gx', 'gy'), may hold values from 0 to 1, as said below
- hilbert_tile_sequence: int32 [1024], replicated, may hold values from -1 to 2047, as said below
Outputs:
- temp_next: float32 [3, 48, 49152], P(None, None, ('gx', 'gy'))
- zonal_next: float32 [3, 48, 49152], P(None, None, ('gx', 'gy'))
- merid_next: float32 [3, 48, 49152], P(None, None, ('gx', 'gy'))
- surface_next: float32 [48, 49152], P(None, ('gx', 'gy'))
- east_next: float32 [48, 49152], P(None, ('gx', 'gy'))
- north_next: float32 [48, 49152], P(None, ('gx', 'gy'))
The draws below stay inside these ranges and needn't reach their ends.
Inputs may be any that keep to these rules, and one draw needn't show every extreme that they name: Slot s = (device index times 8) plus slot, with device index = gx index times the size of gy plus gy index, holds block hilbert_tile_sequence[s] = latitude row times 256 plus longitude column, or -1 if empty. Every block that hilbert_tile_sequence lists appears exactly once. A device's blocks all lie in the latitude row equal to its gx index, fill its first slots, and number at least one and at most 8; some device holds 8. `marine_indicator`: zero throughout every block that hilbert_tile_sequence does not list.
All inputs are finite; a program needn't handle non-finite values.
Results may differ from the reference program's by a relative error of at most 0.0003.
Values sent between devices are 32-bit elements; how exact they have to be, the bound alone decides.
No kernel may reach another device: no remote copies, remote signals or barrier semaphores. Data moves between devices by JAX's collectives and lax.ppermute only.
A program may use at most 128 MiB of HBM per device.

```python
import math
import jax
import jax.numpy as jnp

BLOCK = 48
VERTICAL_LAYERS = 3
BAND = 16
SLOTS = 8
BLOCKS_X = 256
BLOCKS_Y = 8
LONGITUDE_SPAN = 12288
LATITUDE_SPAN = 384
CURVE_SLOTS = 1024


def curve_layout(key):
    row_devices = BLOCKS_X // BAND
    count_key, full_key, score_key, curve_key = jax.random.split(jax.random.fold_in(key, 7), 4)
    first_half = jax.random.randint(count_key, (BLOCKS_Y, row_devices // 2), SLOTS // 2, SLOTS + 1)
    counts = jnp.stack([first_half, 3 * SLOTS // 2 - first_half], axis=-1).reshape(BLOCKS_Y, row_devices)
    full_row = jax.random.randint(full_key, (), 0, BLOCKS_Y)
    counts = jnp.where(jnp.arange(BLOCKS_Y)[:, None] == full_row, SLOTS, counts)
    scores = jax.random.randint(score_key, (BLOCKS_Y, row_devices, BAND), 0, 1 << 20) * BAND + jnp.arange(BAND)
    ranks = jnp.argsort(jnp.argsort(scores, axis=-1), axis=-1)
    ocean = (ranks < counts[..., None]).reshape(BLOCKS_Y, BLOCKS_X).astype(jnp.int32)
    curve_scores = jax.random.randint(curve_key, (BLOCKS_Y, BLOCKS_X), 0, 1 << 18) * BLOCKS_X + jnp.arange(BLOCKS_X)
    curve_scores = jnp.where(ocean == 1, curve_scores, (1 << 18) * BLOCKS_X + jnp.arange(BLOCKS_X))
    order_rank = jnp.argsort(jnp.argsort(curve_scores, axis=1), axis=1)
    total = jnp.sum(ocean, axis=1, keepdims=True)
    portion = order_rank * row_devices // total
    first_rank = (portion * total + row_devices - 1) // row_devices
    target = (jnp.arange(BLOCKS_Y)[:, None] * row_devices + portion) * SLOTS + order_rank - first_rank
    target = jnp.where(ocean == 1, target, CURVE_SLOTS)
    table = jnp.full((CURVE_SLOTS + 1,), -1, jnp.int32)
    table = table.at[target.reshape(-1)].set(jnp.arange(BLOCKS_Y * BLOCKS_X, dtype=jnp.int32))
    return (ocean, table[:CURVE_SLOTS])


def draw_hilbert_tile_sequence(key, part):
    ocean, table = curve_layout(key)
    return table


def draw_marine_indicator(key, part):
    ocean, table = curve_layout(key)
    chances = jax.random.randint(jax.random.fold_in(key, 13), (LATITUDE_SPAN, LONGITUDE_SPAN), 0, 100)
    blockwise = jnp.repeat(jnp.repeat(ocean, BLOCK, axis=0), BLOCK, axis=1)
    return (blockwise * (chances < 88)).astype(jnp.int32)


def shard_levels(rng, dims, cuts, smallest, high):
    loudness, own = 1.0, jax.random.fold_in(rng, 6)
    for dim, shards_of in cuts:
        draws = jnp.exp(jax.random.uniform(jax.random.fold_in(own, dim), (shards_of,), jnp.float32, smallest / len(cuts), high / len(cuts)))
        loudness = loudness * jnp.repeat(draws, dims[dim] // shards_of).reshape([-1 if axis == dim else 1 for axis in range(len(dims))])
    return loudness


def scatter_about(rng, extent, deviation, bound, cuts=(), kind=jnp.bfloat16):
    loudness = shard_levels(rng, extent, cuts, -0.22, 0.18) if cuts else 1.0
    entries = jax.random.normal(rng, extent, jnp.float32) * deviation * loudness
    return jnp.minimum(jnp.maximum(entries, -bound), bound).astype(kind)


def setup_inputs(seed: int = 0) -> dict:
    key_of = jax.random.split(jax.random.key(seed), 10)
    return {
        "potential_heat": scatter_about(key_of[0], (VERTICAL_LAYERS, LATITUDE_SPAN, LONGITUDE_SPAN), 1.0, 6.0, ((1, 8), (2, 16)), jnp.float32),
        "easterly_speed": scatter_about(key_of[1], (VERTICAL_LAYERS, LATITUDE_SPAN, LONGITUDE_SPAN), 1.0, 6.0, ((1, 8), (2, 16)), jnp.float32),
        "poleward_speed": scatter_about(key_of[2], (VERTICAL_LAYERS, LATITUDE_SPAN, LONGITUDE_SPAN), 1.0, 6.0, ((1, 8), (2, 16)), jnp.float32),
        "sea_elevation": scatter_about(key_of[3], (LATITUDE_SPAN, LONGITUDE_SPAN), 1.0, 6.0, ((0, 8), (1, 16)), jnp.float32),
        "averaged_easterly_speed": scatter_about(key_of[4], (LATITUDE_SPAN, LONGITUDE_SPAN), 1.0, 6.0, ((0, 8), (1, 16)), jnp.float32),
        "averaged_poleward_speed": scatter_about(key_of[5], (LATITUDE_SPAN, LONGITUDE_SPAN), 1.0, 6.0, ((0, 8), (1, 16)), jnp.float32),
        "seafloor_distance": jnp.clip(jnp.exp(math.log(2.0) - 1.3862944 * jax.random.uniform(key_of[6], (LATITUDE_SPAN, LONGITUDE_SPAN), jnp.float32) ** shard_levels(key_of[6], (LATITUDE_SPAN, LONGITUDE_SPAN), ((0, 8), (1, 16)), -0.2, 0.2)), 0.5, 2.0),
        "marine_indicator": draw_marine_indicator(jax.random.fold_in(key_of[9], 71), 0),
        "hilbert_tile_sequence": draw_hilbert_tile_sequence(jax.random.fold_in(key_of[9], 71), 0),
    }


transport_factor = 0.4
spreading_factor = 0.1
time_coef = 0.3
viscous_coef = 0.1
quadratic_state_equation = 0.1
coriolis_amp = 0.5
surface_coef = 0.5
gravity_coef = 0.5


def shift_axis(field, amount, dimension_choice):
    if amount == 0:
        return field
    length = field.shape[dimension_choice]
    blank_shape = list(field.shape)
    blank_shape[dimension_choice] = abs(amount)
    blank = jnp.zeros(tuple(blank_shape), field.dtype)
    if amount > 0:
        kept = lax_slice(field, amount, length, dimension_choice)
        return jnp.concatenate([kept, blank], axis=dimension_choice)
    kept = lax_slice(field, 0, length + amount, dimension_choice)
    return jnp.concatenate([blank, kept], axis=dimension_choice)


def lax_slice(field, start, stop, dimension_choice):
    index = [slice(None)] * field.ndim
    index[dimension_choice] = slice(start, stop)
    return field[tuple(index)]


def adjacent_value(field, north, east):
    field = shift_axis(field, east, field.ndim - 1)
    return shift_axis(field, north, field.ndim - 2)


def easterly_biharmonic(field, displacement_helper):
    return (8.0 * (displacement_helper(field, 0, 1) - displacement_helper(field, 0, -1)) - (displacement_helper(field, 0, 2) - displacement_helper(field, 0, -2))) / 12.0


def poleward_biharmonic(field, displacement_helper):
    return (8.0 * (displacement_helper(field, 1, 0) - displacement_helper(field, -1, 0)) - (displacement_helper(field, 2, 0) - displacement_helper(field, -2, 0))) / 12.0


def east_centred(field, displacement_helper):
    return (displacement_helper(field, 0, 1) - displacement_helper(field, 0, -1)) * 0.5


def north_centred(field, displacement_helper):
    return (displacement_helper(field, 1, 0) - displacement_helper(field, -1, 0)) * 0.5


def second_difference(field, displacement_helper):
    return (displacement_helper(field, 0, 1) + displacement_helper(field, 0, -1)) + (displacement_helper(field, 1, 0) + displacement_helper(field, -1, 0)) - 4.0 * field


def sheared_tendencies(marine_heat_values, westeast_watery, southnorth_watery, displacement_helper):
    transport_tendency = westeast_watery * easterly_biharmonic(marine_heat_values, displacement_helper) + southnorth_watery * poleward_biharmonic(marine_heat_values, displacement_helper)
    spreading_tendency = second_difference(marine_heat_values, displacement_helper)
    density_anomaly = marine_heat_values - quadratic_state_equation * marine_heat_values * marine_heat_values
    pressure = jnp.cumsum(density_anomaly, axis=0)
    pressure = pressure - jnp.mean(pressure, axis=0)
    return (transport_tendency, spreading_tendency, east_centred(pressure, displacement_helper), north_centred(pressure, displacement_helper),
            second_difference(westeast_watery, displacement_helper), second_difference(southnorth_watery, displacement_helper))


def barotropic_pass(height_now, flow_east, flow_north, depth_field, push_east, push_north, marine_points, displacement_helper):
    height_now = marine_points * (height_now - surface_coef * (east_centred(depth_field * flow_east, displacement_helper) + north_centred(depth_field * flow_north, displacement_helper)))
    east_new = marine_points * (flow_east - gravity_coef * east_centred(height_now, displacement_helper) + push_east)
    north_new = marine_points * (flow_north - gravity_coef * north_centred(height_now, displacement_helper) + push_north)
    return height_now, east_new, north_new


def to_curve(field, plan):
    leading = field.shape[:-2]
    blocks = field.reshape(leading + (BLOCKS_Y, BLOCK, BLOCKS_X, BLOCK))
    blocks = jnp.swapaxes(blocks, -4, -3).reshape(leading + (BLOCK, BLOCKS_Y * BLOCKS_X, BLOCK))
    chosen = jnp.take(blocks, jnp.clip(plan, 0, BLOCKS_Y * BLOCKS_X - 1), axis=-2)
    chosen = jnp.where((plan >= 0)[:, None], chosen, 0.0)
    return chosen.reshape(leading + (BLOCK, CURVE_SLOTS * BLOCK))


def reference(potential_heat, easterly_speed, poleward_speed, sea_elevation, averaged_easterly_speed, averaged_poleward_speed, seafloor_distance, marine_indicator, hilbert_tile_sequence):
    marine_points = marine_indicator.astype(jnp.float32)
    north_pos = jnp.arange(LATITUDE_SPAN).astype(jnp.float32)[:, None]
    coriolis = coriolis_amp * (2.0 * (north_pos + 0.5) / LATITUDE_SPAN - 1.0)
    marine_heat_values = potential_heat * marine_points
    westeast_watery = easterly_speed * marine_points
    southnorth_watery = poleward_speed * marine_points
    transport_tendency, spreading_tendency, easterly_gradient_force, poleward_gradient_force, easterly_friction, poleward_friction = sheared_tendencies(marine_heat_values, westeast_watery, southnorth_watery, adjacent_value)
    updated_heat_tracer = marine_points * (marine_heat_values - transport_factor * transport_tendency + spreading_factor * spreading_tendency)
    zonal_new = marine_points * (westeast_watery + time_coef * (coriolis * southnorth_watery - easterly_gradient_force) + viscous_coef * easterly_friction)
    merid_new = marine_points * (southnorth_watery + time_coef * (-coriolis * westeast_watery - poleward_gradient_force) + viscous_coef * poleward_friction)
    push_east = jnp.mean(zonal_new - westeast_watery, axis=0)
    push_north = jnp.mean(merid_new - southnorth_watery, axis=0)
    height_now = sea_elevation * marine_points
    flow_east = averaged_easterly_speed * marine_points
    flow_north = averaged_poleward_speed * marine_points
    for sweep_index in range(2):
        height_now, flow_east, flow_north = barotropic_pass(height_now, flow_east, flow_north, seafloor_distance, push_east, push_north, marine_points, adjacent_value)
    return (to_curve(updated_heat_tracer, hilbert_tile_sequence), to_curve(zonal_new, hilbert_tile_sequence), to_curve(merid_new, hilbert_tile_sequence),
            to_curve(height_now, hilbert_tile_sequence), to_curve(flow_east, hilbert_tile_sequence), to_curve(flow_north, hilbert_tile_sequence))
```

```python
import functools

import jax
import jax.numpy as jnp
from jax import lax
from jax.experimental import pallas as pl
from jax.experimental.pallas import tpu as pltpu
from jax.sharding import PartitionSpec as P

BLOCK = 48
SLOTS = 8
ROW_DEVICES = 16
GRID_ROWS = 8
LAT = 384
PLANES = 14
WET = 13
LANES = 128
PIECE = 112

F32 = jnp.float32
I32 = jnp.int32


def iota(shape, dim):
    return lax.broadcasted_iota(I32, shape, dim)


def roll(x, shift, axis):
    return pltpu.roll(x, shift % x.shape[axis], axis)


def plane_of(refs, p):
    if p < 9:
        return refs[p // 3], (p % 3,)
    return refs[3 + p - 9], ()


def read_plane(refs, p, rows, lanes):
    ref, lead = plane_of(refs, p)
    x = ref[lead + (rows, lanes)]
    return x.astype(F32) if p == WET else x


def halo_tile(north, south, p):
    low = iota(north.shape, 0) < 4
    if p < 7:
        return jnp.where(low, north, roll(south, 4, 0))
    return jnp.where(low, roll(north, 4, 0), south)


def edge_kernel(*refs):
    tab_ref = refs[0]
    bottoms, tops, lefts, rights = (refs[1 + 8 * i : 9 + 8 * i] for i in range(4))
    row_a, row_b, col_e, col_w, idx = refs[33:]
    gx, gy = lax.axis_index("gx"), lax.axis_index("gy")
    even = gx % 2 == 0
    for m in range(7):
        low = iota((8, 768), 0) < 4
        full = slice(None)
        t0, t1 = (read_plane(tops, q, full, full) for q in (m, m + 7))
        b0, b1 = (read_plane(bottoms, q, full, full) for q in (m, m + 7))
        top = jnp.where(low, roll(t0, 4, 0), t1)
        bottom = jnp.where(low, b0, roll(b1, 4, 0))
        row_a[8 * m : 8 * m + 8] = jnp.where(even, top, bottom)
        row_b[8 * m : 8 * m + 8] = jnp.where(even, bottom, top)
    lane = iota((BLOCK, LANES), 1)
    east = jnp.zeros((BLOCK, LANES), F32)
    west = jnp.zeros((BLOCK, LANES), F32)
    for p in range(PLANES):
        here = (lane >= 4 * p) & (lane < 4 * p + 4)
        e = read_plane(rights, p, slice(None), slice(None))
        w = read_plane(lefts, p, slice(None), slice(None))
        east = jnp.where(here, roll(e, 4 * p + 4, 1), east)
        west = jnp.where(here, roll(w, 4 * p, 1), west)
    col_e[...] = east
    col_w[...] = west

    square = (LANES, LANES)
    g = tab_ref[pl.ds(gx, 1), :].astype(F32)
    g_lane = jnp.broadcast_to(g, square)
    diagonal = iota(square, 0) == iota(square, 1)
    g_sub = jnp.sum(jnp.where(diagonal, g_lane, 0.0), axis=1, keepdims=True)
    g_sub = jnp.broadcast_to(g_sub, square)
    d_lane = jnp.floor(g_lane * (1.0 / 16.0))
    d_sub = jnp.floor(g_sub * (1.0 / 16.0))
    same = d_lane == d_sub
    rank_lane = jnp.sum(jnp.where(same & (g_sub < g_lane), 1.0, 0.0), axis=0, keepdims=True)
    rank_sub = jnp.sum(jnp.where(same & (g_lane < g_sub), 1.0, 0.0), axis=1, keepdims=True)
    first = (gx * ROW_DEVICES).astype(F32)
    source = jnp.floor(g * (1.0 / 16.0)) - first
    place = jnp.where(g >= 0.0, source * 16.0 + rank_lane, 0.0)
    me = (gx * ROW_DEVICES + gy).astype(F32)
    c_lane = iota(square, 1).astype(F32)
    mine = (d_sub == me) & (jnp.broadcast_to(rank_sub, square) == c_lane)
    order = jnp.sum(jnp.where(mine, g_sub - d_sub * 16.0, 0.0), axis=0, keepdims=True)
    count = jnp.zeros(square, F32)
    for r in range(GRID_ROWS):
        owner = jnp.floor(tab_ref[r : r + 1, :].astype(F32) * (1.0 / 16.0))
        count += jnp.where(jnp.broadcast_to(owner, square) == iota(square, 0).astype(F32), 1.0, 0.0)
    most = jnp.max(jnp.sum(count, axis=1, keepdims=True), axis=0, keepdims=True)
    most = jnp.broadcast_to(most, (1, LANES))
    sub = iota((8, LANES), 0)
    table = jnp.where(sub == 0, place, jnp.where(sub == 1, order, most))
    idx[...] = table.astype(I32)


def column_kernel(a0, b0, a5, b5, col_e, col_w, col_a, col_b):
    gx, gy = lax.axis_index("gx"), lax.axis_index("gy")
    even_row, even = gx % 2 == 0, gy % 2 == 0
    lane = iota((8, LANES), 1)
    east = jnp.zeros((8, LANES), F32)
    west = jnp.zeros((8, LANES), F32)
    for p in range(PLANES):
        rows = slice(8 * (p % 7), 8 * (p % 7) + 8)
        here = (lane >= 4 * p) & (lane < 4 * p + 4)
        w = halo_tile(
            jnp.where(even_row, a0[rows], b0[rows]), jnp.where(even_row, b0[rows], a0[rows]), p
        )
        e = halo_tile(
            jnp.where(even_row, a5[rows], b5[rows]), jnp.where(even_row, b5[rows], a5[rows]), p
        )
        east = jnp.where(here, roll(e, 4 * p + 4, 1), east)
        west = jnp.where(here, roll(w, 4 * p, 1), west)
    e_own, w_own = col_e[...], col_w[...]
    col_a[0:48] = jnp.where(even, e_own, w_own)
    col_b[0:48] = jnp.where(even, w_own, e_own)
    col_a[48:56] = jnp.where(even, east, west)
    col_b[48:56] = jnp.where(even, west, east)


HT = 56
WIDTH = 896
T0, U0, V0, PR = 0, 3, 6, 9
E0, P0, Q0, DEPTH, WETS, DP, GX, GY = 12, 13, 14, 15, 16, 17, 18, 19
FIELDS = 20


def pack_tiles(r):
    lane = iota(r[0].shape, 1)
    t0 = jnp.where(lane < 48, r[0], jnp.where(lane < 96, r[1], r[2]))
    t1 = jnp.where(
        lane < 16, r[2], jnp.where(lane < 64, r[3], jnp.where(lane < 112, r[4], r[5]))
    )
    t2 = jnp.where(lane < 32, r[5], jnp.where(lane < 80, r[6], r[7]))
    return t0, t1, t2


def step_kernel(rounds, *refs):
    idx = refs[0]
    raw = refs[1:9]
    row_a, row_b, col_a, col_b = refs[9:13]
    send = refs[13]
    ext, res = refs[14:]
    gx, gy = lax.axis_index("gx"), lax.axis_index("gy")
    even_row, even = gx % 2 == 0, gy % 2 == 0

    def place_strip(t, planes):
        lanes = slice(128 * t, 128 * t + 128)
        wet = planes(WET)
        ext[WETS, :, lanes] = wet
        heat = [planes(q) * wet for q in range(3)]
        for q in range(3):
            ext[T0 + q, :, lanes] = heat[q]
        run = None
        sums = []
        for q in range(3):
            b = heat[q] - 0.1 * heat[q] * heat[q]
            run = b if run is None else run + b
            sums.append(run)
        mean = (sums[0] + sums[1] + sums[2]) / 3.0
        for q in range(3):
            ext[PR + q, :, lanes] = sums[q] - mean
        for q in range(3):
            ext[U0 + q, :, lanes] = planes(3 + q) * wet
            ext[V0 + q, :, lanes] = planes(6 + q) * wet
        ext[E0, :, lanes] = planes(9) * wet
        east = planes(10) * wet
        depth = planes(12)
        ext[P0, :, lanes] = east
        ext[Q0, :, lanes] = planes(11) * wet
        ext[DEPTH, :, lanes] = depth
        ext[DP, :, lanes] = depth * east

    for t in range(6):
        lanes = slice(128 * t, 128 * t + 128)

        def planes(p, lanes=lanes):
            rows = slice(8 * (p % 7), 8 * (p % 7) + 8)
            a, b = row_a[rows, lanes], row_b[rows, lanes]
            halo = halo_tile(jnp.where(even_row, a, b), jnp.where(even_row, b, a), p)
            return jnp.concatenate([read_plane(raw, p, slice(None), lanes), halo], axis=0)

        place_strip(t, planes)

    def side(p):
        a, b = col_a[...], col_b[...]
        from_east = roll(jnp.where(even, a, b), -4 * p, 1)
        from_west = roll(jnp.where(even, b, a), 124 - 4 * p, 1)
        lane = iota((HT, LANES), 1)
        return jnp.where(lane < 4, from_east, jnp.where(lane >= 124, from_west, 0.0))

    place_strip(6, side)

    lane = iota((HT, LANES), 1)
    row = iota((HT, LANES), 0)
    north = gx * BLOCK + row - jnp.where(row >= 52, HT, 0)
    coriolis = 0.5 * (2.0 * (north.astype(F32) + 0.5) / LAT - 1.0)

    def at(t):
        return pl.ds(pl.multiple_of(t * LANES, LANES), LANES)

    def strips(t):
        before = jnp.where(t == 0, 6, t - 1)
        after = jnp.where(t == 6, 0, t + 1)
        return at(t), at(before), at(after)

    def east_of(field, here, after, k, x):
        return roll(jnp.where(lane < k, ext[field, :, after], x), -k, 1)

    def west_of(field, here, before, k, x):
        return roll(jnp.where(lane >= 128 - k, ext[field, :, before], x), k, 1)

    @pl.loop(0, 7)
    def levels(t):
        here, before, after = strips(t)
        wet = ext[WETS, :, here]
        gain_x = jnp.zeros((HT, LANES), F32)
        gain_y = jnp.zeros((HT, LANES), F32)

        def around(field):
            x = ext[field, :, here]
            return (
                x,
                east_of(field, here, after, 1, x),
                west_of(field, here, before, 1, x),
                roll(x, -1, 0),
                roll(x, 1, 0),
            )

        for q in range(3):
            u, ue, uw, un, us = around(U0 + q)
            v, ve, vw, vn, vs = around(V0 + q)
            x, xe, xw, xn, xs = around(T0 + q)
            xee = east_of(T0 + q, here, after, 2, x)
            xww = west_of(T0 + q, here, before, 2, x)
            dx = (8.0 * (xe - xw) - (xee - xww)) * (1.0 / 12.0)
            dy = (8.0 * (xn - xs) - (roll(x, -2, 0) - roll(x, 2, 0))) * (1.0 / 12.0)
            lap = (xe + xw) + (xn + xs) - 4.0 * x
            heat = wet * (x - 0.4 * (u * dx + v * dy) + 0.1 * lap)
            res[48 * q : 48 * q + 48, here] = heat[:48]
            _, pe, pw, pn, ps = around(PR + q)
            lap_u = (ue + uw) + (un + us) - 4.0 * u
            lap_v = (ve + vw) + (vn + vs) - 4.0 * v
            new_u = wet * (u + 0.3 * (coriolis * v - (pe - pw) * 0.5) + 0.1 * lap_u)
            new_v = wet * (v + 0.3 * (-coriolis * u - (pn - ps) * 0.5) + 0.1 * lap_v)
            res[144 + 48 * q : 192 + 48 * q, here] = new_u[:48]
            res[288 + 48 * q : 336 + 48 * q, here] = new_v[:48]
            gain_x += new_u - u
            gain_y += new_v - v
        ext[GX, :, here] = gain_x / 3.0
        ext[GY, :, here] = gain_y / 3.0

    for sweep in range(2):
        last = sweep == 1

        @pl.loop(0, 7)
        def height(t):
            here, before, after = strips(t)
            flux = ext[DP, :, here]
            div = (east_of(DP, here, after, 1, flux) - west_of(DP, here, before, 1, flux)) * 0.5
            cross = ext[DEPTH, :, here] * ext[Q0, :, here]
            div += (roll(cross, -1, 0) - roll(cross, 1, 0)) * 0.5
            new = ext[WETS, :, here] * (ext[E0, :, here] - 0.5 * div)
            ext[E0, :, here] = new
            if last:
                res[432:480, here] = new[:48]

        @pl.loop(0, 7)
        def flow(t):
            here, before, after = strips(t)
            wet = ext[WETS, :, here]
            e = ext[E0, :, here]
            ex = (east_of(E0, here, after, 1, e) - west_of(E0, here, before, 1, e)) * 0.5
            ey = (roll(e, -1, 0) - roll(e, 1, 0)) * 0.5
            new_p = wet * (ext[P0, :, here] - 0.5 * ex + ext[GX, :, here])
            new_q = wet * (ext[Q0, :, here] - 0.5 * ey + ext[GY, :, here])
            if last:
                res[480:528, here] = new_p[:48]
                res[528:576, here] = new_q[:48]
            else:
                ext[P0, :, here] = new_p
                ext[Q0, :, here] = new_q
                ext[DP, :, here] = ext[DEPTH, :, here] * new_p

    offsets = [48 * idx[1, c] for c in range(8 * rounds)]

    @pl.loop(0, 8)
    def cut(q):
        pair = 2 * q
        main = pl.ds(pl.multiple_of(64 * q, 64), 64)
        rest = pl.ds(pl.multiple_of(512 + 8 * q, 8), 8)
        for h in range(rounds):
            for rows, n in ((main, 64), (rest, 8)):
                lanes = iota((n, LANES), 1)
                moved = []
                for c in range(8):
                    off = offsets[8 * h + c]
                    tile, inner = off // LANES, off % LANES
                    x = jnp.where(
                        lanes >= inner, res[rows, at(tile)], res[rows, at(tile + 1)]
                    )
                    moved.append(pltpu.roll(x, (48 * c + 2 * LANES - inner) % LANES, 1))
                tiles = pack_tiles(moved)
                base = PIECE * h
                if n == 64:
                    for i in range(3):
                        spot = slice(base + 32 * i, base + 32 * i + 32)
                        send[pair, spot] = tiles[i][:32]
                        send[pair + 1, spot] = tiles[i][32:]
                else:
                    low = iota((8, LANES), 0) < 4
                    a, b, c = tiles
                    s0, s1 = slice(base + 96, base + 104), slice(base + 104, base + 112)
                    send[pair, s0] = jnp.where(low, a, roll(b, 4, 0))
                    send[pair, s1] = c
                    send[pair + 1, s0] = jnp.where(low, roll(a, 4, 0), b)
                    send[pair + 1, s1] = roll(c, 4, 0)


def route_kernel(rounds, idx, got, send):
    low = iota((8, LANES), 0) < 4

    @pl.loop(0, ROW_DEVICES)
    def target(d):
        main, rest = [], []
        for s in range(SLOTS):
            place = idx[0, d * SLOTS + s]
            source, rank = place // 16, place % 16
            base = (rank // 8) * PIECE if rounds > 1 else 0
            off = 48 * (rank % 8)
            tile, inner = off // LANES, off % LANES
            turn = (48 * s + 2 * LANES - inner) % LANES
            first = pl.ds(pl.multiple_of(base + 32 * tile, 8), 32)
            after = pl.ds(pl.multiple_of(base + 32 * jnp.minimum(tile + 1, 2), 8), 32)
            x = jnp.where(
                iota((32, LANES), 1) >= inner, got[source, first, :], got[source, after, :]
            )
            main.append(pltpu.roll(x, turn, 1))
            ha = got[source, pl.ds(pl.multiple_of(base + 96, 8), 8), :]
            hb = got[source, pl.ds(pl.multiple_of(base + 104, 8), 8), :]
            hr = roll(ha, 4, 0)
            now = jnp.where(tile == 0, ha, jnp.where(tile == 1, hr, hb))
            then = jnp.where(tile == 0, hr, hb)
            x = jnp.where(iota((8, LANES), 1) >= inner, now, then)
            rest.append(pltpu.roll(x, turn, 1))
        tiles = pack_tiles(main)
        for i in range(3):
            send[d, 32 * i : 32 * i + 32] = tiles[i]
        a, b, c = pack_tiles(rest)
        send[d, 96:104] = jnp.where(low, a, roll(b, 4, 0))
        send[d, 104:112] = c


def settle_kernel(tab, got, heat, zonal, merid, height, east, north):
    gx, gy = lax.axis_index("gx"), lax.axis_index("gy")
    used = jnp.int32(0)
    for s in range(SLOTS):
        used += (tab[gx, gy * SLOTS + s] >= 0).astype(I32)
    lane = iota((8, LANES), 1)
    low = iota((8, LANES), 0) < 4
    outs = (heat, zonal, merid, height, east, north)

    def put(tile_row, i, x):
        x = jnp.where(lane + LANES * i < used * BLOCK, x, 0.0)
        plane, rows = tile_row // 6, slice(8 * (tile_row % 6), 8 * (tile_row % 6) + 8)
        lanes = slice(LANES * i, LANES * i + LANES)
        if plane < 9:
            outs[plane // 3][plane % 3, rows, lanes] = x
        else:
            outs[plane - 6][rows, lanes] = x

    for k in range(ROW_DEVICES):
        for i in range(3):
            for t in range(4):
                put(4 * k + t, i, got[k, 32 * i + 8 * t : 32 * i + 8 * t + 8, :])
    for q in range(8):
        a0, a1 = got[2 * q, 96:104, :], got[2 * q + 1, 96:104, :]
        b0, b1 = got[2 * q, 104:112, :], got[2 * q + 1, 104:112, :]
        put(64 + q, 0, jnp.where(low, a0, roll(a1, 4, 0)))
        put(64 + q, 1, jnp.where(low, roll(a0, 4, 0), a1))
        put(64 + q, 2, jnp.where(low, b0, roll(b1, 4, 0)))


def f32(*shape):
    return jax.ShapeDtypeStruct(shape, F32)


VM = pl.BlockSpec(memory_space=pltpu.VMEM)
SM = pl.BlockSpec(memory_space=pltpu.SMEM)


def shards(heat, zonal, merid, height, east, north, depth, marine, sequence):
    raw = (heat, zonal, merid, height, east, north, depth, marine)
    tab = sequence.reshape(GRID_ROWS, LANES)

    def spec(x, block, where):
        if x.ndim == 3:
            return pl.BlockSpec((3,) + block, lambda i: (0,) + where)
        return pl.BlockSpec(block, lambda i: where)

    corners = (
        ((8, 768), (0, 0)),
        ((8, 768), (5, 0)),
        ((BLOCK, LANES), (0, 0)),
        ((BLOCK, LANES), (0, 5)),
    )
    whole = lambda *shape: pl.BlockSpec(shape, lambda i: (0,) * len(shape))
    row_a, row_b, col_e, col_w, idx = pl.pallas_call(
        edge_kernel,
        grid=(1,),
        in_specs=[whole(GRID_ROWS, LANES)]
        + [spec(x, block, where) for block, where in corners for x in raw],
        out_specs=(whole(56, 768), whole(56, 768), whole(48, 128), whole(48, 128), whole(8, 128)),
        out_shape=(
            f32(56, 768),
            f32(56, 768),
            f32(48, 128),
            f32(48, 128),
            jax.ShapeDtypeStruct((8, 128), I32),
        ),
        name="edges",
    )(tab, *(x for _ in corners for x in raw))

    def swaps(axis, size, first, second):
        near = [(i, i ^ 1) for i in range(size)]
        far = [(i, i + 1) for i in range(1, size - 1, 2)]
        far += [(j, i) for i, j in far]
        return lax.ppermute(first, axis, near), lax.ppermute(second, axis, far)

    row_a, row_b = swaps("gx", GRID_ROWS, row_a, row_b)
    left = pl.BlockSpec((56, 128), lambda i: (0, 0))
    right = pl.BlockSpec((56, 128), lambda i: (0, 5))
    col_a, col_b = pl.pallas_call(
        column_kernel,
        grid=(1,),
        in_specs=[left, left, right, right, whole(48, 128), whole(48, 128)],
        out_specs=(whole(56, 128), whole(56, 128)),
        out_shape=(f32(56, 128), f32(56, 128)),
        name="columns",
    )(row_a, row_b, row_a, row_b, col_e, col_w)
    col_a, col_b = swaps("gy", ROW_DEVICES, col_a, col_b)

    def tail(rounds):
        send = pl.pallas_call(
            functools.partial(step_kernel, rounds),
            in_specs=[SM] + [VM] * 12,
            out_specs=VM,
            out_shape=f32(ROW_DEVICES, rounds * PIECE, LANES),
            scratch_shapes=[
                pltpu.VMEM((FIELDS, HT, WIDTH), F32),
                pltpu.VMEM((576, WIDTH), F32),
            ],
            name="step",
        )(idx, *raw, row_a, row_b, col_a, col_b)
        got = lax.all_to_all(send, "gy", 0, 0, tiled=True)
        send = pl.pallas_call(
            functools.partial(route_kernel, rounds),
            in_specs=[SM, VM],
            out_specs=VM,
            out_shape=f32(ROW_DEVICES, PIECE, LANES),
            name="route",
        )(idx, got)
        got = lax.all_to_all(send, "gy", 0, 0, tiled=True)
        return pl.pallas_call(
            settle_kernel,
            in_specs=[SM, VM],
            out_specs=(VM,) * 6,
            out_shape=(f32(3, 48, 384),) * 3 + (f32(48, 384),) * 3,
            name="settle",
        )(tab, got)

    return tail(2)


def solution(mesh):
    level, flat = P(None, "gx", "gy"), P("gx", "gy")
    return jax.shard_map(
        shards,
        mesh=mesh,
        in_specs=(level,) * 3 + (flat,) * 5 + (P(),),
        out_specs=(P(None, None, ("gx", "gy")),) * 3 + (P(None, ("gx", "gy")),) * 3,
        check_vma=False,
    )
```

```python
import functools

import jax
import jax.numpy as jnp
from jax import lax
from jax.experimental import pallas as pl
from jax.experimental.pallas import tpu as pltpu
from jax.sharding import PartitionSpec as P

BLOCK = 48
SLOTS = 8
ROW_DEVICES = 16
GRID_ROWS = 8
LAT = 384
PLANES = 14
WET = 13
LANES = 128
PIECE = 112

F32 = jnp.float32
I32 = jnp.int32


def iota(shape, dim):
    return lax.broadcasted_iota(I32, shape, dim)


def roll(x, shift, axis):
    return pltpu.roll(x, shift % x.shape[axis], axis)


def plane_of(refs, p):
    if p < 9:
        return refs[p // 3], (p % 3,)
    return refs[3 + p - 9], ()


def read_plane(refs, p, rows, lanes):
    ref, lead = plane_of(refs, p)
    x = ref[lead + (rows, lanes)]
    return x.astype(F32) if p == WET else x


def halo_tile(north, south, p):
    low = iota(north.shape, 0) < 4
    if p < 7:
        return jnp.where(low, north, roll(south, 4, 0))
    return jnp.where(low, roll(north, 4, 0), south)


def edge_kernel(*refs):
    tab_ref = refs[0]
    bottoms, tops, lefts, rights = (refs[1 + 8 * i : 9 + 8 * i] for i in range(4))
    row_a, row_b, col_e, col_w, idx = refs[33:]
    gx, gy = lax.axis_index("gx"), lax.axis_index("gy")
    even = gx % 2 == 0
    for m in range(7):
        low = iota((8, 768), 0) < 4
        full = slice(None)
        t0, t1 = (read_plane(tops, q, full, full) for q in (m, m + 7))
        b0, b1 = (read_plane(bottoms, q, full, full) for q in (m, m + 7))
        top = jnp.where(low, roll(t0, 4, 0), t1)
        bottom = jnp.where(low, b0, roll(b1, 4, 0))
        row_a[8 * m : 8 * m + 8] = jnp.where(even, top, bottom)
        row_b[8 * m : 8 * m + 8] = jnp.where(even, bottom, top)
    lane = iota((BLOCK, LANES), 1)
    east = jnp.zeros((BLOCK, LANES), F32)
    west = jnp.zeros((BLOCK, LANES), F32)
    for p in range(PLANES):
        here = (lane >= 4 * p) & (lane < 4 * p + 4)
        e = read_plane(rights, p, slice(None), slice(None))
        w = read_plane(lefts, p, slice(None), slice(None))
        east = jnp.where(here, roll(e, 4 * p + 4, 1), east)
        west = jnp.where(here, roll(w, 4 * p, 1), west)
    col_e[...] = east
    col_w[...] = west

    square = (LANES, LANES)
    g = tab_ref[pl.ds(gx, 1), :].astype(F32)
    g_lane = jnp.broadcast_to(g, square)
    diagonal = iota(square, 0) == iota(square, 1)
    g_sub = jnp.sum(jnp.where(diagonal, g_lane, 0.0), axis=1, keepdims=True)
    g_sub = jnp.broadcast_to(g_sub, square)
    d_lane = jnp.floor(g_lane * (1.0 / 16.0))
    d_sub = jnp.floor(g_sub * (1.0 / 16.0))
    same = d_lane == d_sub
    rank_lane = jnp.sum(jnp.where(same & (g_sub < g_lane), 1.0, 0.0), axis=0, keepdims=True)
    rank_sub = jnp.sum(jnp.where(same & (g_lane < g_sub), 1.0, 0.0), axis=1, keepdims=True)
    first = (gx * ROW_DEVICES).astype(F32)
    source = jnp.floor(g * (1.0 / 16.0)) - first
    listed = g >= 0.0
    half = jnp.where(rank_lane >= 8.0, 1.0, 0.0)
    place = jnp.where(listed, source * 2.0 + half, 0.0)
    off = jnp.where(listed, 48.0 * (rank_lane - 8.0 * half), 0.0)
    tile = jnp.floor(off * (1.0 / LANES))
    me = (gx * ROW_DEVICES + gy).astype(F32)
    c_lane = iota(square, 1).astype(F32)
    mine = (d_sub == me) & (jnp.broadcast_to(rank_sub, square) == c_lane)
    order = jnp.sum(jnp.where(mine, g_sub - d_sub * 16.0, 0.0), axis=0, keepdims=True)
    count = jnp.zeros(square, F32)
    for r in range(GRID_ROWS):
        owner = jnp.floor(tab_ref[r : r + 1, :].astype(F32) * (1.0 / 16.0))
        count += jnp.where(jnp.broadcast_to(owner, square) == iota(square, 0).astype(F32), 1.0, 0.0)
    most = jnp.max(jnp.sum(count, axis=1, keepdims=True), axis=0, keepdims=True)
    most = jnp.broadcast_to(most, (1, LANES))
    sub = iota((8, LANES), 0)
    table = jnp.where(sub == 3, order, most)
    table = jnp.where(sub == 2, off - LANES * tile, table)
    table = jnp.where(sub == 1, 32.0 * tile, table)
    table = jnp.where(sub == 0, place, table)
    idx[...] = table.astype(I32)


def column_kernel(a0, b0, a5, b5, col_e, col_w, col_a, col_b):
    gx, gy = lax.axis_index("gx"), lax.axis_index("gy")
    even_row, even = gx % 2 == 0, gy % 2 == 0
    lane = iota((8, LANES), 1)
    east = jnp.zeros((8, LANES), F32)
    west = jnp.zeros((8, LANES), F32)
    for p in range(PLANES):
        rows = slice(8 * (p % 7), 8 * (p % 7) + 8)
        here = (lane >= 4 * p) & (lane < 4 * p + 4)
        w = halo_tile(
            jnp.where(even_row, a0[rows], b0[rows]), jnp.where(even_row, b0[rows], a0[rows]), p
        )
        e = halo_tile(
            jnp.where(even_row, a5[rows], b5[rows]), jnp.where(even_row, b5[rows], a5[rows]), p
        )
        east = jnp.where(here, roll(e, 4 * p + 4, 1), east)
        west = jnp.where(here, roll(w, 4 * p, 1), west)
    e_own, w_own = col_e[...], col_w[...]
    col_a[0:48] = jnp.where(even, e_own, w_own)
    col_b[0:48] = jnp.where(even, w_own, e_own)
    col_a[48:56] = jnp.where(even, east, west)
    col_b[48:56] = jnp.where(even, west, east)


HT = 56
STRIP = 72
STRIPS = 7
T0, U0, V0 = 0, 3, 6
XE, XW, YN, YS = 9, 12, 15, 18
E0, P0, Q0, DEPTH, WETS, QUARTER, DP, DQ, GX, GY = range(21, 31)
FIELDS = 31


def pack_tiles(r):
    lane = iota(r[0].shape, 1)
    t0 = jnp.where(lane < 48, r[0], jnp.where(lane < 96, r[1], r[2]))
    t1 = jnp.where(
        lane < 16, r[2], jnp.where(lane < 64, r[3], jnp.where(lane < 112, r[4], r[5]))
    )
    t2 = jnp.where(lane < 32, r[5], jnp.where(lane < 80, r[6], r[7]))
    return t0, t1, t2


def step_kernel(rounds, *refs):
    idx = refs[0]
    raw = refs[1:9]
    row_a, row_b, col_a, col_b = refs[9:13]
    send = refs[13]
    ext, res = refs[14:]
    gx, gy = lax.axis_index("gx"), lax.axis_index("gy")
    even_row, even = gx % 2 == 0, gy % 2 == 0

    def put(field, t, x, ring=False):
        ext[field, t, 8:64] = x
        if ring:
            ext[field, t, 0:8] = x[48:56]
            ext[field, t, 64:72] = x[0:8]

    def mid(field, t, rows=HT):
        return ext[field, t, 8 : 8 + rows]

    def up(field, t, k=1, rows=HT):
        return ext[field, t, 8 + k : 8 + k + rows]

    def down(field, t, k=1, rows=HT):
        return ext[field, t, 8 - k : 8 - k + rows]

    def right(field, t, x, k=1, rows=HT):
        after = (t + 1) % STRIPS if isinstance(t, int) else jnp.where(t == 6, 0, t + 1)
        lane = iota((rows, LANES), 1)
        return roll(jnp.where(lane < k, mid(field, after, rows), x), -k, 1)

    def left(field, t, x, k=1, rows=HT):
        before = (t - 1) % STRIPS if isinstance(t, int) else jnp.where(t == 0, 6, t - 1)
        lane = iota((rows, LANES), 1)
        return roll(jnp.where(lane >= LANES - k, mid(field, before, rows), x), k, 1)

    def place_strip(t, planes):
        wet = planes(WET)
        put(WETS, t, wet)
        put(QUARTER, t, 0.25 * wet)
        sums = []
        for q in range(3):
            heat = planes(q) * wet
            put(T0 + q, t, heat, ring=True)
            b = heat - 0.1 * heat * heat
            sums.append(sums[-1] + b if sums else b)
        mean = (sums[0] + sums[1] + sums[2]) * (1.0 / 3.0)
        for q in range(3):
            push = 0.15 * (sums[q] - mean)
            u, v = planes(3 + q) * wet, planes(6 + q) * wet
            put(U0 + q, t, u, ring=True)
            put(V0 + q, t, v)
            u, v = 0.1 * u, 0.1 * v
            put(XE + q, t, u - push)
            put(XW + q, t, u + push)
            put(YN + q, t, v - push, ring=True)
            put(YS + q, t, v + push, ring=True)
        put(E0, t, planes(9) * wet)
        east, north = planes(10) * wet, planes(11) * wet
        depth = 0.25 * planes(12)
        put(P0, t, east)
        put(Q0, t, north)
        put(DEPTH, t, depth)
        put(DP, t, depth * east)
        put(DQ, t, depth * north, ring=True)

    for t in range(6):
        lanes = slice(128 * t, 128 * t + 128)

        def planes(p, lanes=lanes):
            rows = slice(8 * (p % 7), 8 * (p % 7) + 8)
            a, b = row_a[rows, lanes], row_b[rows, lanes]
            halo = halo_tile(jnp.where(even_row, a, b), jnp.where(even_row, b, a), p)
            return jnp.concatenate([read_plane(raw, p, slice(None), lanes), halo], axis=0)

        place_strip(t, planes)

    def side(p):
        a, b = col_a[...], col_b[...]
        from_east = roll(jnp.where(even, a, b), -4 * p, 1)
        from_west = roll(jnp.where(even, b, a), 124 - 4 * p, 1)
        lane = iota((HT, LANES), 1)
        return jnp.where(lane < 4, from_east, jnp.where(lane >= 124, from_west, 0.0))

    place_strip(6, side)

    row = iota((HT, LANES), 0)
    north = gx * BLOCK + row - jnp.where(row >= 52, HT, 0)
    turn = 0.15 * (2.0 * (north.astype(F32) + 0.5) / LAT - 1.0)

    @pl.loop(0, 6)
    def tracer(t):
        wet = mid(WETS, t, 48)
        for q in range(3):
            f = T0 + q
            x = mid(f, t, 48)
            xe, xw = right(f, t, x, 1, 48), left(f, t, x, 1, 48)
            xee, xww = right(f, t, x, 2, 48), left(f, t, x, 2, 48)
            xn, xs = up(f, t, 1, 48), down(f, t, 1, 48)
            xnn, xss = up(f, t, 2, 48), down(f, t, 2, 48)
            dx = (3.2 / 12.0) * (xw - xe) + (0.4 / 12.0) * (xee - xww)
            dy = (3.2 / 12.0) * (xs - xn) + (0.4 / 12.0) * (xnn - xss)
            ring = 0.1 * ((xe + xw) + (xn + xs))
            new = 0.6 * x + ring + (mid(U0 + q, t, 48) * dx + mid(V0 + q, t, 48) * dy)
            res[t, 48 * q : 48 * q + 48] = wet * new

    @pl.loop(0, STRIPS)
    def motion(t):
        wet = mid(WETS, t)
        gain_x = gain_y = None
        for q in range(3):
            u, v = mid(U0 + q, t), mid(V0 + q, t)
            side_x = right(XE + q, t, mid(XE + q, t)) + left(XW + q, t, mid(XW + q, t))
            side_y = up(YN + q, t) + down(YS + q, t)
            ring_u = 0.1 * (up(U0 + q, t) + down(U0 + q, t))
            ring_v = 0.1 * (right(V0 + q, t, v) + left(V0 + q, t, v))
            new_u = wet * ((0.6 * u + turn * v) + (side_x + ring_u))
            new_v = wet * ((0.6 * v - turn * u) + (side_y + ring_v))
            res[t, 144 + 48 * q : 192 + 48 * q] = new_u[:48]
            res[t, 288 + 48 * q : 336 + 48 * q] = new_v[:48]
            du, dv = new_u - u, new_v - v
            gain_x = du if gain_x is None else gain_x + du
            gain_y = dv if gain_y is None else gain_y + dv
        put(GX, t, gain_x * (1.0 / 3.0))
        put(GY, t, gain_y * (1.0 / 3.0))

    for last in (False, True):
        for t in range(STRIPS):
            flux = mid(DP, t)
            div = (right(DP, t, flux) - left(DP, t, flux)) + (up(DQ, t) - down(DQ, t))
            new = mid(E0, t) - mid(WETS, t) * div
            put(E0, t, new, ring=True)
            if last:
                res[t, 432:480] = new[:48]
        for t in range(STRIPS):
            e, quarter = mid(E0, t), mid(QUARTER, t)
            ex = right(E0, t, e) - left(E0, t, e)
            ey = up(E0, t) - down(E0, t)
            new_p = (mid(P0, t) + mid(GX, t)) - quarter * ex
            new_q = (mid(Q0, t) + mid(GY, t)) - quarter * ey
            if last:
                res[t, 480:528] = new_p[:48]
                res[t, 528:576] = new_q[:48]
            else:
                put(P0, t, new_p)
                put(Q0, t, new_q)
                put(DP, t, mid(DEPTH, t) * new_p)
                put(DQ, t, mid(DEPTH, t) * new_q, ring=True)

    spots = []
    for c in range(8 * rounds):
        off = 48 * idx[3, c]
        inner = off & 127
        spots.append((off >> 7, inner, (48 * c + 256 - inner) & 127))

    @pl.loop(0, 8)
    def cut(q):
        pair = 2 * q
        main = pl.ds(pl.multiple_of(64 * q, 64), 64)
        rest = pl.ds(pl.multiple_of(512 + 8 * q, 8), 8)
        for h in range(rounds):
            for rows, n in ((main, 64), (rest, 8)):
                lanes = iota((n, LANES), 1)
                moved = []
                for tile, inner, shift in spots[8 * h : 8 * h + 8]:
                    x = jnp.where(lanes >= inner, res[tile, rows], res[tile + 1, rows])
                    moved.append(pltpu.roll(x, shift, 1))
                tiles = pack_tiles(moved)
                base = PIECE * h
                if n == 64:
                    for i in range(3):
                        spot = slice(base + 32 * i, base + 32 * i + 32)
                        send[pair, spot] = tiles[i][:32]
                        send[pair + 1, spot] = tiles[i][32:]
                else:
                    low = iota((8, LANES), 0) < 4
                    a, b, c = tiles
                    s0, s1 = slice(base + 96, base + 104), slice(base + 104, base + 112)
                    send[pair, s0] = jnp.where(low, a, roll(b, 4, 0))
                    send[pair, s1] = c
                    send[pair + 1, s0] = jnp.where(low, roll(a, 4, 0), b)
                    send[pair + 1, s1] = roll(c, 4, 0)


def route_kernel(rounds, idx, got, send):
    low = iota((8, LANES), 0) < 4
    wide, flat = iota((32, LANES), 1), iota((8, LANES), 1)

    @pl.loop(0, ROW_DEVICES // 4)
    def targets(four):
        for j in range(4):
            d = four * 4 + j
            main, rest = [], []
            for s in range(SLOTS):
                slot = d * SLOTS + s
                place, row, inner = idx[0, slot], idx[1, slot], idx[2, slot]
                base = PIECE * (place if rounds > 1 else place >> 1)
                shift = (48 * s + 256 - inner) & 127
                first = pl.ds(pl.multiple_of(base + row, 8), 32)
                after = pl.ds(pl.multiple_of(base + jnp.minimum(row + 32, 64), 8), 32)
                x = jnp.where(wide >= inner, got[first, :], got[after, :])
                main.append(pltpu.roll(x, shift, 1))
                ha = got[pl.ds(pl.multiple_of(base + 96, 8), 8), :]
                hb = got[pl.ds(pl.multiple_of(base + 104, 8), 8), :]
                hr = roll(ha, 4, 0)
                now = jnp.where(row == 0, ha, jnp.where(row == 32, hr, hb))
                then = jnp.where(row == 0, hr, hb)
                x = jnp.where(flat >= inner, now, then)
                rest.append(pltpu.roll(x, shift, 1))
            tiles = pack_tiles(main)
            for i in range(3):
                send[d, 32 * i : 32 * i + 32] = tiles[i]
            a, b, c = pack_tiles(rest)
            send[d, 96:104] = jnp.where(low, a, roll(b, 4, 0))
            send[d, 104:112] = c


def settle_kernel(tab, got, heat, zonal, merid, height, east, north):
    gx, gy = lax.axis_index("gx"), lax.axis_index("gy")
    used = jnp.int32(0)
    for s in range(SLOTS):
        used += (tab[gx, gy * SLOTS + s] >= 0).astype(I32)
    lane = iota((8, LANES), 1)
    low = iota((8, LANES), 0) < 4
    outs = (heat, zonal, merid, height, east, north)

    def put(tile_row, i, x):
        x = jnp.where(lane + LANES * i < used * BLOCK, x, 0.0)
        plane, rows = tile_row // 6, slice(8 * (tile_row % 6), 8 * (tile_row % 6) + 8)
        lanes = slice(LANES * i, LANES * i + LANES)
        if plane < 9:
            outs[plane // 3][plane % 3, rows, lanes] = x
        else:
            outs[plane - 6][rows, lanes] = x

    for k in range(ROW_DEVICES):
        for i in range(3):
            for t in range(4):
                put(4 * k + t, i, got[k, 32 * i + 8 * t : 32 * i + 8 * t + 8, :])
    for q in range(8):
        a0, a1 = got[2 * q, 96:104, :], got[2 * q + 1, 96:104, :]
        b0, b1 = got[2 * q, 104:112, :], got[2 * q + 1, 104:112, :]
        put(64 + q, 0, jnp.where(low, a0, roll(a1, 4, 0)))
        put(64 + q, 1, jnp.where(low, roll(a0, 4, 0), a1))
        put(64 + q, 2, jnp.where(low, b0, roll(b1, 4, 0)))


def f32(*shape):
    return jax.ShapeDtypeStruct(shape, F32)


VM = pl.BlockSpec(memory_space=pltpu.VMEM)
SM = pl.BlockSpec(memory_space=pltpu.SMEM)


def shards(heat, zonal, merid, height, east, north, depth, marine, sequence):
    raw = (heat, zonal, merid, height, east, north, depth, marine)
    tab = sequence.reshape(GRID_ROWS, LANES)

    def spec(x, block, where):
        if x.ndim == 3:
            return pl.BlockSpec((3,) + block, lambda i: (0,) + where)
        return pl.BlockSpec(block, lambda i: where)

    corners = (
        ((8, 768), (0, 0)),
        ((8, 768), (5, 0)),
        ((BLOCK, LANES), (0, 0)),
        ((BLOCK, LANES), (0, 5)),
    )
    whole = lambda *shape: pl.BlockSpec(shape, lambda i: (0,) * len(shape))
    row_a, row_b, col_e, col_w, idx = pl.pallas_call(
        edge_kernel,
        grid=(1,),
        in_specs=[whole(GRID_ROWS, LANES)]
        + [spec(x, block, where) for block, where in corners for x in raw],
        out_specs=(whole(56, 768), whole(56, 768), whole(48, 128), whole(48, 128), whole(8, 128)),
        out_shape=(
            f32(56, 768),
            f32(56, 768),
            f32(48, 128),
            f32(48, 128),
            jax.ShapeDtypeStruct((8, 128), I32),
        ),
        compiler_params=pltpu.CompilerParams(vmem_limit_bytes=6 << 20),
        name="edges",
    )(tab, *(x for _ in corners for x in raw))

    def swaps(axis, size, first, second):
        near = [(i, i ^ 1) for i in range(size)]
        far = [(i, i + 1) for i in range(1, size - 1, 2)]
        far += [(j, i) for i, j in far]
        return lax.ppermute(first, axis, near), lax.ppermute(second, axis, far)

    row_a, row_b = swaps("gx", GRID_ROWS, row_a, row_b)
    left = pl.BlockSpec((56, 128), lambda i: (0, 0))
    right = pl.BlockSpec((56, 128), lambda i: (0, 5))
    col_a, col_b = pl.pallas_call(
        column_kernel,
        grid=(1,),
        in_specs=[left, left, right, right, whole(48, 128), whole(48, 128)],
        out_specs=(whole(56, 128), whole(56, 128)),
        out_shape=(f32(56, 128), f32(56, 128)),
        compiler_params=pltpu.CompilerParams(vmem_limit_bytes=4 << 20),
        name="columns",
    )(row_a, row_b, row_a, row_b, col_e, col_w)
    col_a, col_b = swaps("gy", ROW_DEVICES, col_a, col_b)

    def tail(rounds):
        send = pl.pallas_call(
            functools.partial(step_kernel, rounds),
            in_specs=[SM] + [VM] * 12,
            out_specs=VM,
            out_shape=f32(ROW_DEVICES, rounds * PIECE, LANES),
            scratch_shapes=[
                pltpu.VMEM((FIELDS, STRIPS, STRIP, LANES), F32),
                pltpu.VMEM((STRIPS, 576, LANES), F32),
            ],
            compiler_params=pltpu.CompilerParams(vmem_limit_bytes=24 << 20),
        name="step",
        )(idx, *raw, row_a, row_b, col_a, col_b)
        got = lax.all_to_all(send, "gy", 0, 0, tiled=True)
        send = pl.pallas_call(
            functools.partial(route_kernel, rounds),
            in_specs=[SM, VM],
            out_specs=VM,
            out_shape=f32(ROW_DEVICES, PIECE, LANES),
            compiler_params=pltpu.CompilerParams(vmem_limit_bytes=8 << 20),
        name="route",
        )(idx, got.reshape(ROW_DEVICES * rounds * PIECE, LANES))
        got = lax.all_to_all(send, "gy", 0, 0, tiled=True)
        return pl.pallas_call(
            settle_kernel,
            in_specs=[SM, VM],
            out_specs=(VM,) * 6,
            out_shape=(f32(3, 48, 384),) * 3 + (f32(48, 384),) * 3,
            compiler_params=pltpu.CompilerParams(vmem_limit_bytes=6 << 20),
        name="settle",
        )(tab, got)

    return lax.cond(idx[4, 0] > 8, lambda: tail(2), lambda: tail(1))


def solution(mesh):
    level, flat = P(None, "gx", "gy"), P("gx", "gy")
    return jax.shard_map(
        shards,
        mesh=mesh,
        in_specs=(level,) * 3 + (flat,) * 5 + (P(),),
        out_specs=(P(None, None, ("gx", "gy")),) * 3 + (P(None, ("gx", "gy")),) * 3,
        check_vma=False,
    )
```

```python
import functools

import jax
import jax.numpy as jnp
from jax import lax
from jax.experimental import pallas as pl
from jax.experimental.pallas import tpu as pltpu
from jax.sharding import PartitionSpec as P

BLOCK = 48
SLOTS = 8
ROW_DEVICES = 16
GRID_ROWS = 8
LAT = 384
PLANES = 14
WET = 13
LANES = 128
PIECE = 112

F32 = jnp.float32
I32 = jnp.int32


def iota(shape, dim):
    return lax.broadcasted_iota(I32, shape, dim)


def roll(x, shift, axis):
    return pltpu.roll(x, shift % x.shape[axis], axis)


def plane_of(refs, p):
    if p < 9:
        return refs[p // 3], (p % 3,)
    return refs[3 + p - 9], ()


def read_plane(refs, p, rows, lanes):
    ref, lead = plane_of(refs, p)
    x = ref[lead + (rows, lanes)]
    return x.astype(F32) if p == WET else x


def halo_tile(north, south, p):
    low = iota(north.shape, 0) < 4
    if p < 7:
        return jnp.where(low, north, roll(south, 4, 0))
    return jnp.where(low, roll(north, 4, 0), south)


def edge_kernel(*refs):
    bottoms, tops, lefts, rights = (refs[8 * i : 8 * i + 8] for i in range(4))
    row_a, row_b, col_e, col_w = refs[32:]
    gx, gy = lax.axis_index("gx"), lax.axis_index("gy")
    even = gx % 2 == 0
    for m in range(7):
        low = iota((8, 768), 0) < 4
        full = slice(None)
        t0, t1 = (read_plane(tops, q, full, full) for q in (m, m + 7))
        b0, b1 = (read_plane(bottoms, q, full, full) for q in (m, m + 7))
        top = jnp.where(low, roll(t0, 4, 0), t1)
        bottom = jnp.where(low, b0, roll(b1, 4, 0))
        row_a[8 * m : 8 * m + 8] = jnp.where(even, top, bottom)
        row_b[8 * m : 8 * m + 8] = jnp.where(even, bottom, top)
    lane = iota((BLOCK, LANES), 1)
    east = jnp.zeros((BLOCK, LANES), F32)
    west = jnp.zeros((BLOCK, LANES), F32)
    for p in range(PLANES):
        here = (lane >= 4 * p) & (lane < 4 * p + 4)
        e = read_plane(rights, p, slice(None), slice(None))
        w = read_plane(lefts, p, slice(None), slice(None))
        east = jnp.where(here, roll(e, 4 * p + 4, 1), east)
        west = jnp.where(here, roll(w, 4 * p, 1), west)
    col_e[...] = east
    col_w[...] = west


def place_kernel(tab_ref, idx):
    gx, gy = lax.axis_index("gx"), lax.axis_index("gy")
    square = (LANES, LANES)
    g = tab_ref[pl.ds(gx, 1), :].astype(F32)
    g_lane = jnp.broadcast_to(g, square)
    diagonal = iota(square, 0) == iota(square, 1)
    g_sub = jnp.sum(jnp.where(diagonal, g_lane, 0.0), axis=1, keepdims=True)
    g_sub = jnp.broadcast_to(g_sub, square)
    d_lane = jnp.floor(g_lane * (1.0 / 16.0))
    d_sub = jnp.floor(g_sub * (1.0 / 16.0))
    same = d_lane == d_sub
    rank_lane = jnp.sum(jnp.where(same & (g_sub < g_lane), 1.0, 0.0), axis=0, keepdims=True)
    rank_sub = jnp.sum(jnp.where(same & (g_lane < g_sub), 1.0, 0.0), axis=1, keepdims=True)
    first = (gx * ROW_DEVICES).astype(F32)
    source = jnp.floor(g * (1.0 / 16.0)) - first
    listed = g >= 0.0
    half = jnp.where(rank_lane >= 8.0, 1.0, 0.0)
    half = jnp.where(listed, half, 0.0)
    place = jnp.where(listed, source, 0.0)
    off = jnp.where(listed, 48.0 * (rank_lane - 8.0 * half), 0.0)
    tile = jnp.floor(off * (1.0 / LANES))
    own = (iota((1, LANES), 1) // SLOTS == gy) & listed
    used = jnp.sum(jnp.where(own, float(BLOCK), 0.0), axis=1, keepdims=True)
    used = jnp.broadcast_to(used, (1, LANES))
    me = (gx * ROW_DEVICES + gy).astype(F32)
    c_lane = iota(square, 1).astype(F32)
    mine = (d_sub == me) & (jnp.broadcast_to(rank_sub, square) == c_lane)
    order = jnp.sum(jnp.where(mine, g_sub - d_sub * 16.0, 0.0), axis=0, keepdims=True)
    count = jnp.zeros(square, F32)
    for r in range(GRID_ROWS):
        owner = jnp.floor(tab_ref[r : r + 1, :].astype(F32) * (1.0 / 16.0))
        count += jnp.where(jnp.broadcast_to(owner, square) == iota(square, 0).astype(F32), 1.0, 0.0)
    most = jnp.max(jnp.sum(count, axis=1, keepdims=True), axis=0, keepdims=True)
    most = jnp.broadcast_to(most, (1, LANES))
    sub = iota((8, LANES), 0)
    table = jnp.where(sub == 3, order, most)
    table = jnp.where(sub == 0, place * PIECE + 36.0 * tile, table)
    table = jnp.where(sub == 1, place * PIECE + 36.0 * jnp.minimum(tile + 1.0, 2.0), table)
    table = jnp.where(sub == 2, off - LANES * tile, table)
    table = jnp.where(sub == 5, used, table)
    table = jnp.where(sub == 6, half, table)
    idx[...] = table.astype(I32)


def column_kernel(a0, b0, a5, b5, col_e, col_w, col_a, col_b):
    gx, gy = lax.axis_index("gx"), lax.axis_index("gy")
    even_row, even = gx % 2 == 0, gy % 2 == 0
    lane = iota((8, LANES), 1)
    east = jnp.zeros((8, LANES), F32)
    west = jnp.zeros((8, LANES), F32)
    for p in range(PLANES):
        rows = slice(8 * (p % 7), 8 * (p % 7) + 8)
        here = (lane >= 4 * p) & (lane < 4 * p + 4)
        w = halo_tile(
            jnp.where(even_row, a0[rows], b0[rows]), jnp.where(even_row, b0[rows], a0[rows]), p
        )
        e = halo_tile(
            jnp.where(even_row, a5[rows], b5[rows]), jnp.where(even_row, b5[rows], a5[rows]), p
        )
        east = jnp.where(here, roll(e, 4 * p + 4, 1), east)
        west = jnp.where(here, roll(w, 4 * p, 1), west)
    e_own, w_own = col_e[...], col_w[...]
    col_a[0:48] = jnp.where(even, e_own, w_own)
    col_b[0:48] = jnp.where(even, w_own, e_own)
    col_a[48:56] = jnp.where(even, east, west)
    col_b[48:56] = jnp.where(even, west, east)


HT = 56
STRIP = 72
STRIPS = 7
T0, U0, V0 = 0, 3, 6
XE, XW, YN, YS = 9, 12, 15, 18
E0, P0, Q0, DEPTH, WETS, QUARTER, DP, DQ, GX, GY = range(21, 31)
FIELDS = 31


def pack_tiles(r):
    lane = iota(r[0].shape, 1)
    t0 = jnp.where(lane < 48, r[0], jnp.where(lane < 96, r[1], r[2]))
    t1 = jnp.where(
        lane < 16, r[2], jnp.where(lane < 64, r[3], jnp.where(lane < 112, r[4], r[5]))
    )
    t2 = jnp.where(lane < 32, r[5], jnp.where(lane < 80, r[6], r[7]))
    return t0, t1, t2


class Step:
    def __init__(self, ext, res):
        self.ext, self.res = ext, res
        self.gx, self.gy = lax.axis_index("gx"), lax.axis_index("gy")

    def put(self, field, t, x, first=8):
        self.ext[field, t, first : first + x.shape[0]] = x

    def mid(self, field, t, first=8, rows=HT):
        return self.ext[field, t, first : first + rows]

    def right(self, field, t, x, k=1, first=8):
        after = (t + 1) % STRIPS if isinstance(t, int) else jnp.where(t == 6, 0, t + 1)
        lane = iota(x.shape, 1)
        y = self.mid(field, after, first, x.shape[0])
        return roll(jnp.where(lane < k, y, x), -k, 1)

    def left(self, field, t, x, k=1, first=8):
        before = (t - 1) % STRIPS if isinstance(t, int) else jnp.where(t == 0, 6, t - 1)
        lane = iota(x.shape, 1)
        y = self.mid(field, before, first, x.shape[0])
        return roll(jnp.where(lane >= LANES - k, y, x), k, 1)

    def place(self, t, planes, part):
        def put(field, x, ring=False):
            if part == "halo":
                self.put(field, t, x, 56)
                if ring:
                    self.put(field, t, x, 0)
            else:
                self.put(field, t, x)
                if ring:
                    self.put(field, t, x[0:8], 64)
                    if part == "all":
                        self.put(field, t, x[48:56], 0)

        wet = planes(WET)
        put(WETS, wet)
        put(QUARTER, 0.25 * wet)
        sums = []
        for q in range(3):
            heat = planes(q) * wet
            put(T0 + q, heat, ring=True)
            b = heat - 0.1 * heat * heat
            sums.append(sums[-1] + b if sums else b)
        mean = (sums[0] + sums[1] + sums[2]) * (1.0 / 3.0)
        for q in range(3):
            push = 0.15 * (sums[q] - mean)
            u, v = planes(3 + q) * wet, planes(6 + q) * wet
            put(U0 + q, u, ring=True)
            put(V0 + q, v)
            u, v = 0.1 * u, 0.1 * v
            put(XE + q, u - push)
            put(XW + q, u + push)
            put(YN + q, v - push, ring=True)
            put(YS + q, v + push, ring=True)
        put(E0, planes(9) * wet)
        east, north = planes(10) * wet, planes(11) * wet
        depth = 0.25 * planes(12)
        put(P0, east)
        put(Q0, north)
        put(DEPTH, depth)
        put(DP, depth * east)
        put(DQ, depth * north, ring=True)

    def tracer(self, t, first, rows):
        mid = functools.partial(self.mid, t=t, rows=rows)
        wet = mid(WETS, first=first)
        for q in range(3):
            f = T0 + q
            x = mid(f, first=first)
            xe, xw = self.right(f, t, x, 1, first), self.left(f, t, x, 1, first)
            xee, xww = self.right(f, t, x, 2, first), self.left(f, t, x, 2, first)
            xn, xs = mid(f, first=first + 1), mid(f, first=first - 1)
            xnn, xss = mid(f, first=first + 2), mid(f, first=first - 2)
            dx = (3.2 / 12.0) * (xw - xe) + (0.4 / 12.0) * (xee - xww)
            dy = (3.2 / 12.0) * (xs - xn) + (0.4 / 12.0) * (xnn - xss)
            ring = 0.1 * ((xe + xw) + (xn + xs))
            u, v = mid(U0 + q, first=first), mid(V0 + q, first=first)
            new = 0.6 * x + ring + (u * dx + v * dy)
            self.res[t, 48 * q + first - 8 : 48 * q + first - 8 + rows] = wet * new

    def motion(self, t, first, rows):
        row = iota((rows, LANES), 0) + (first - 8)
        north = self.gx * BLOCK + row - jnp.where(row >= 52, HT, 0)
        turn = 0.15 * (2.0 * (north.astype(F32) + 0.5) / LAT - 1.0)
        mid = functools.partial(self.mid, t=t, rows=rows)
        wet = mid(WETS, first=first)
        kept = min(rows, 56 - first)
        gain_x = gain_y = None
        for q in range(3):
            u, v = mid(U0 + q, first=first), mid(V0 + q, first=first)
            xe, xw = mid(XE + q, first=first), mid(XW + q, first=first)
            side_x = self.right(XE + q, t, xe, 1, first) + self.left(XW + q, t, xw, 1, first)
            side_y = mid(YN + q, first=first + 1) + mid(YS + q, first=first - 1)
            ring_u = 0.1 * (mid(U0 + q, first=first + 1) + mid(U0 + q, first=first - 1))
            ring_v = 0.1 * (
                self.right(V0 + q, t, v, 1, first) + self.left(V0 + q, t, v, 1, first)
            )
            new_u = wet * ((0.6 * u + turn * v) + (side_x + ring_u))
            new_v = wet * ((0.6 * v - turn * u) + (side_y + ring_v))
            spot = 144 + 48 * q + first - 8
            self.res[t, spot : spot + kept] = new_u[:kept]
            self.res[t, spot + 144 : spot + 144 + kept] = new_v[:kept]
            du, dv = new_u - u, new_v - v
            gain_x = du if gain_x is None else gain_x + du
            gain_y = dv if gain_y is None else gain_y + dv
        self.put(GX, t, gain_x * (1.0 / 3.0), first)
        self.put(GY, t, gain_y * (1.0 / 3.0), first)

    def passes(self):
        mid, put = self.mid, self.put
        for last in (False, True):
            for t in range(STRIPS):
                flux = mid(DP, t)
                div = (self.right(DP, t, flux) - self.left(DP, t, flux)) + (
                    mid(DQ, t, 9) - mid(DQ, t, 7)
                )
                new = mid(E0, t) - mid(WETS, t) * div
                put(E0, t, new)
                put(E0, t, new[48:56], 0)
                put(E0, t, new[0:8], 64)
                if last:
                    self.res[t, 432:480] = new[:48]
            for t in range(STRIPS):
                e, quarter = mid(E0, t), mid(QUARTER, t)
                ex = self.right(E0, t, e) - self.left(E0, t, e)
                ey = mid(E0, t, 9) - mid(E0, t, 7)
                new_p = (mid(P0, t) + mid(GX, t)) - quarter * ex
                new_q = (mid(Q0, t) + mid(GY, t)) - quarter * ey
                if last:
                    self.res[t, 480:528] = new_p[:48]
                    self.res[t, 528:576] = new_q[:48]
                else:
                    cross = mid(DEPTH, t) * new_q
                    put(P0, t, new_p)
                    put(Q0, t, new_q)
                    put(DP, t, mid(DEPTH, t) * new_p)
                    put(DQ, t, cross)
                    put(DQ, t, cross[48:56], 0)
                    put(DQ, t, cross[0:8], 64)


def cut_pieces(rounds, idx, res, send):
    spots = []
    for c in range(8 * rounds):
        off = 48 * idx[3, c]
        inner = off & 127
        spots.append((off >> 7, inner, (48 * c + 256 - inner) & 127))

    def cut(q):
        pair = 2 * q
        for h in range(rounds):
            done = []
            for start, n in ((64 * q, 64), (512 + 8 * q, 8)):
                rows = pl.ds(start, n) if isinstance(q, int) else pl.ds(pl.multiple_of(start, 8), n)
                lanes = iota((n, LANES), 1)
                moved = []
                for tile, inner, shift in spots[8 * h : 8 * h + 8]:
                    x = jnp.where(lanes >= inner, res[tile, rows], res[tile + 1, rows])
                    moved.append(pltpu.roll(x, shift, 1))
                done.append(pack_tiles(moved))
            mains, rests = done
            for i in range(3):
                base = PIECE * h + 36 * i
                send[pair, base + 32 : base + 40] = rests[i]
                send[pair + 1, base + 28 : base + 36] = rests[i]
            for i in range(3):
                base = PIECE * h + 36 * i
                send[pair, base : base + 32] = mains[i][:32]
                send[pair + 1, base : base + 32] = mains[i][32:]

    if rounds == 1:
        for q in range(8):
            cut(q)
    else:
        pl.loop(0, 8)(cut)


def interior_kernel(*refs):
    raw = refs[:8]
    step = Step(*refs[8:])

    @pl.loop(0, 6)
    def fill(t):
        lanes = pl.ds(pl.multiple_of(t * LANES, LANES), LANES)
        step.place(t, lambda p: read_plane(raw, p, slice(None), lanes), "own")

    @pl.loop(1, 5)
    def inner(t):
        step.tracer(t, 16, 32)
        step.motion(t, 16, 32)


def middle_kernel(row_a, row_b, ext_in, res_in, ext, res):
    step = Step(ext, res)
    even_row = step.gx % 2 == 0
    for t in range(6):
        lanes = slice(LANES * t, LANES * t + LANES)

        def planes(p, lanes=lanes):
            rows = slice(8 * (p % 7), 8 * (p % 7) + 8)
            a, b = row_a[rows, lanes], row_b[rows, lanes]
            return halo_tile(jnp.where(even_row, a, b), jnp.where(even_row, b, a), p)

        step.place(t, planes, "halo")

    @pl.loop(1, 5)
    def edge(t):
        step.tracer(t, 8, 8)
        step.tracer(t, 48, 8)
        step.motion(t, 8, 8)
        step.motion(t, 48, 16)


def finish_kernel(col_a, col_b, idx, ext_in, res_in, ext, res, send, table, sem):
    copy = pltpu.make_async_copy(idx, table, sem)
    copy.start()
    step = Step(ext, res)
    even = step.gy % 2 == 0

    def side(p):
        a, b = col_a[...], col_b[...]
        from_east = roll(jnp.where(even, a, b), -4 * p, 1)
        from_west = roll(jnp.where(even, b, a), 124 - 4 * p, 1)
        lane = iota((HT, LANES), 1)
        return jnp.where(lane < 4, from_east, jnp.where(lane >= 124, from_west, 0.0))

    step.place(6, side, "all")
    for t in (0, 5):
        step.tracer(t, 8, 48)
    for t in (0, 5, 6):
        step.motion(t, 8, 56)
    step.passes()
    copy.wait()
    cut_pieces(1, table, res, send)


def cut_kernel(idx, res, send):
    cut_pieces(2, idx, res, send)


def route_kernel(rounds, idx, got, send):
    lane = iota((36, LANES), 1)

    @pl.loop(0, 2)
    def targets(part):
        for j in range(8):
            d = part * 8 + j
            moved = []
            for s in range(SLOTS):
                slot = d * SLOTS + s
                first, after, inner = idx[0, slot], idx[1, slot], idx[2, slot]
                if rounds > 1:
                    first, after = (
                        x + PIECE * (x // PIECE) + PIECE * idx[6, slot] for x in (first, after)
                    )
                near = got[pl.ds(first, 36), :]
                far = got[pl.ds(after, 36), :]
                x = jnp.where(lane >= inner, near, far)
                moved.append(pltpu.roll(x, (48 * s + 256 - inner) & 127, 1))
            for i, x in enumerate(pack_tiles(moved)):
                send[d, 36 * i : 36 * i + 36] = x


def settle_kernel(idx, got, heat, zonal, merid, height, east, north):
    used = jnp.broadcast_to(idx[5:6, :], (8, LANES))
    lane = iota((8, LANES), 1)
    low = iota((8, LANES), 0) < 4
    outs = (heat, zonal, merid, height, east, north)

    def put(tile_row, i, x):
        x = jnp.where(lane + LANES * i < used, x, 0.0)
        plane, rows = tile_row // 6, slice(8 * (tile_row % 6), 8 * (tile_row % 6) + 8)
        lanes = slice(LANES * i, LANES * i + LANES)
        if plane < 9:
            outs[plane // 3][plane % 3, rows, lanes] = x
        else:
            outs[plane - 6][rows, lanes] = x

    for i in range(3):
        for k in range(ROW_DEVICES):
            for t in range(4):
                put(4 * k + t, i, got[k, 36 * i + 8 * t : 36 * i + 8 * t + 8, :])
        for q in range(8):
            a = got[2 * q, 36 * i + 32 : 36 * i + 40, :]
            b = got[2 * q + 1, 36 * i + 28 : 36 * i + 36, :]
            put(64 + q, i, jnp.where(low, a, b))


def f32(*shape):
    return jax.ShapeDtypeStruct(shape, F32)


def cost(us):
    return pl.CostEstimate(flops=us * 1_000_000, bytes_accessed=us * 2_000_000, transcendentals=0)


VM = pl.BlockSpec(memory_space=pltpu.VMEM)
SM = pl.BlockSpec(memory_space=pltpu.SMEM)


def shards(heat, zonal, merid, height, east, north, depth, marine, sequence):
    raw = (heat, zonal, merid, height, east, north, depth, marine)
    tab = sequence.reshape(GRID_ROWS, LANES)

    def spec(x, block, where):
        if x.ndim == 3:
            return pl.BlockSpec((3,) + block, lambda i: (0,) + where)
        return pl.BlockSpec(block, lambda i: where)

    corners = (
        ((8, 768), (0, 0)),
        ((8, 768), (5, 0)),
        ((BLOCK, LANES), (0, 0)),
        ((BLOCK, LANES), (0, 5)),
    )
    whole = lambda *shape: pl.BlockSpec(shape, lambda i: (0,) * len(shape))
    row_a, row_b, col_e, col_w = pl.pallas_call(
        edge_kernel,
        grid=(1,),
        in_specs=[spec(x, block, where) for block, where in corners for x in raw],
        out_specs=(whole(56, 768), whole(56, 768), whole(48, 128), whole(48, 128)),
        out_shape=(f32(56, 768), f32(56, 768), f32(48, 128), f32(48, 128)),
        compiler_params=pltpu.CompilerParams(vmem_limit_bytes=6 << 20),
        cost_estimate=cost(1),
        name="edges",
    )(*(x for _ in corners for x in raw))

    def call(kernel, name, operands, ins, outs, shapes, mega=8, us=1, **more):
        more = {"in_specs": ins, "out_specs": outs, **more}
        return pl.pallas_call(
            kernel,
            out_shape=shapes,
            compiler_params=pltpu.CompilerParams(vmem_limit_bytes=mega << 20),
            cost_estimate=cost(us),
            name=name,
            **more,
        )(*operands)

    idx = call(
        place_kernel, "places", (tab,), [VM], VM, jax.ShapeDtypeStruct((8, LANES), I32), mega=4
    )
    fields = (f32(FIELDS, STRIPS, STRIP, LANES), f32(STRIPS, 576, LANES))
    ext, res = call(interior_kernel, "interior", raw, [VM] * 8, (VM, VM), fields, us=2)

    def swaps(axis, size, first, second):
        near = [(i, i ^ 1) for i in range(size)]
        far = [(i, i + 1) for i in range(1, size - 1, 2)]
        far += [(j, i) for i, j in far]
        return lax.ppermute(first, axis, near), lax.ppermute(second, axis, far)

    row_a, row_b = swaps("gx", GRID_ROWS, row_a, row_b)
    left = pl.BlockSpec((56, 128), lambda i: (0, 0))
    right = pl.BlockSpec((56, 128), lambda i: (0, 5))
    col_a, col_b = call(
        column_kernel,
        "columns",
        (row_a, row_b, row_a, row_b, col_e, col_w),
        None,
        None,
        (f32(56, 128), f32(56, 128)),
        mega=4,
        grid=(1,),
        in_specs=[left, left, right, right, whole(48, 128), whole(48, 128)],
        out_specs=(whole(56, 128), whole(56, 128)),
    )
    ext, res = call(
        middle_kernel,
        "middle",
        (row_a, row_b, ext, res),
        [VM] * 4,
        (VM, VM),
        fields,
        us=2,
        input_output_aliases={2: 0, 3: 1},
    )
    col_a, col_b = swaps("gy", ROW_DEVICES, col_a, col_b)
    _, res, send = call(
        finish_kernel,
        "finish",
        (col_a, col_b, idx, ext, res),
        [VM] * 5,
        (VM,) * 3,
        fields + (f32(ROW_DEVICES, PIECE, LANES),),
        us=4,
        input_output_aliases={3: 0, 4: 1},
        scratch_shapes=[pltpu.SMEM((8, LANES), I32), pltpu.SemaphoreType.DMA],
    )

    def deliver(rounds, send):
        got = lax.all_to_all(send, "gy", 0, 0, tiled=True)
        got = got.reshape(ROW_DEVICES * rounds * PIECE, LANES)
        piece = f32(ROW_DEVICES, PIECE, LANES)
        send = call(
            functools.partial(route_kernel, rounds), "route", (idx, got), [SM, VM], VM, piece
        )
        got = lax.all_to_all(send, "gy", 0, 0, tiled=True)
        shapes = (f32(3, 48, 384),) * 3 + (f32(48, 384),) * 3
        return call(settle_kernel, "settle", (idx, got), [VM, VM], (VM,) * 6, shapes)

    def crowded():
        both = f32(ROW_DEVICES, 2 * PIECE, LANES)
        return deliver(2, call(cut_kernel, "cut", (idx, res), [SM, VM], VM, both))

    return lax.cond(idx[4, 0] > 8, crowded, lambda: deliver(1, send))


def solution(mesh):
    level, flat = P(None, "gx", "gy"), P("gx", "gy")
    return jax.shard_map(
        shards,
        mesh=mesh,
        in_specs=(level,) * 3 + (flat,) * 5 + (P(),),
        out_specs=(P(None, None, ("gx", "gy")),) * 3 + (P(None, ("gx", "gy")),) * 3,
        check_vma=False,
    )
```

```python
import functools

import jax
import jax.numpy as jnp
from jax import lax
from jax.experimental import pallas as pl
from jax.experimental.pallas import tpu as pltpu
from jax.sharding import PartitionSpec as P

BLOCK = 48
SLOTS = 8
ROW_DEVICES = 16
GRID_ROWS = 8
LAT = 384
PLANES = 14
WET = 13
LANES = 128
PIECE = 112

F32 = jnp.float32
I32 = jnp.int32


def iota(shape, dim):
    return lax.broadcasted_iota(I32, shape, dim)


def roll(x, shift, axis):
    return pltpu.roll(x, shift % x.shape[axis], axis)


def plane_of(refs, p):
    if p < 9:
        return refs[p // 3], (p % 3,)
    return refs[3 + p - 9], ()


def read_plane(refs, p, rows, lanes):
    ref, lead = plane_of(refs, p)
    x = ref[lead + (rows, lanes)]
    return x.astype(F32) if p == WET else x


def halo_tile(north, south, p):
    low = iota(north.shape, 0) < 4
    if p < 7:
        return jnp.where(low, north, roll(south, 4, 0))
    return jnp.where(low, roll(north, 4, 0), south)


EDGES = (
    (slice(0, 8), slice(None)),
    (slice(40, 48), slice(None)),
    (slice(None), slice(0, 128)),
    (slice(None), slice(640, 768)),
)


def edge_kernel(*refs):
    raw = refs[:8]
    row_a, row_b, col_e, col_w = refs[8:12]
    parts, sem = refs[12:44], refs[44]
    bottoms, tops, lefts, rights = (parts[8 * i : 8 * i + 8] for i in range(4))
    copies = []
    for i, (rows, lanes) in enumerate(EDGES):
        for j, x in enumerate(raw):
            where = (slice(None),) * (len(x.shape) - 2) + (rows, lanes)
            n = 8 * i + j
            copies.append(pltpu.make_async_copy(x.at[where], parts[n], sem.at[n]))
            copies[-1].start()
    for copy in copies:
        copy.wait()
    gx, gy = lax.axis_index("gx"), lax.axis_index("gy")
    even = gx % 2 == 0
    for m in range(7):
        low = iota((8, 768), 0) < 4
        full = slice(None)
        t0, t1 = (read_plane(tops, q, full, full) for q in (m, m + 7))
        b0, b1 = (read_plane(bottoms, q, full, full) for q in (m, m + 7))
        top = jnp.where(low, roll(t0, 4, 0), t1)
        bottom = jnp.where(low, b0, roll(b1, 4, 0))
        row_a[8 * m : 8 * m + 8] = jnp.where(even, top, bottom)
        row_b[8 * m : 8 * m + 8] = jnp.where(even, bottom, top)
    lane = iota((BLOCK, LANES), 1)
    east = jnp.zeros((BLOCK, LANES), F32)
    west = jnp.zeros((BLOCK, LANES), F32)
    for p in range(PLANES):
        here = (lane >= 4 * p) & (lane < 4 * p + 4)
        e = read_plane(rights, p, slice(None), slice(None))
        w = read_plane(lefts, p, slice(None), slice(None))
        east = jnp.where(here, roll(e, 4 * p + 4, 1), east)
        west = jnp.where(here, roll(w, 4 * p, 1), west)
    col_e[...] = east
    col_w[...] = west


def place_kernel(tab_ref, after, idx):
    gx, gy = lax.axis_index("gx"), lax.axis_index("gy")
    square = (LANES, LANES)
    g = tab_ref[pl.ds(gx, 1), :].astype(F32)
    g_lane = jnp.broadcast_to(g, square)
    diagonal = iota(square, 0) == iota(square, 1)
    g_sub = jnp.sum(jnp.where(diagonal, g_lane, 0.0), axis=1, keepdims=True)
    g_sub = jnp.broadcast_to(g_sub, square)
    d_lane = jnp.floor(g_lane * (1.0 / 16.0))
    d_sub = jnp.floor(g_sub * (1.0 / 16.0))
    same = d_lane == d_sub
    rank_lane = jnp.sum(jnp.where(same & (g_sub < g_lane), 1.0, 0.0), axis=0, keepdims=True)
    rank_sub = jnp.sum(jnp.where(same & (g_lane < g_sub), 1.0, 0.0), axis=1, keepdims=True)
    first = (gx * ROW_DEVICES).astype(F32)
    source = jnp.floor(g * (1.0 / 16.0)) - first
    listed = g >= 0.0
    half = jnp.where(rank_lane >= 8.0, 1.0, 0.0)
    half = jnp.where(listed, half, 0.0)
    place = jnp.where(listed, source, 0.0)
    off = jnp.where(listed, 48.0 * (rank_lane - 8.0 * half), 0.0)
    tile = jnp.floor(off * (1.0 / LANES))
    own = (iota((1, LANES), 1) // SLOTS == gy) & listed
    used = jnp.sum(jnp.where(own, float(BLOCK), 0.0), axis=1, keepdims=True)
    used = jnp.broadcast_to(used, (1, LANES))
    me = (gx * ROW_DEVICES + gy).astype(F32)
    c_lane = iota(square, 1).astype(F32)
    mine = (d_sub == me) & (jnp.broadcast_to(rank_sub, square) == c_lane)
    order = jnp.sum(jnp.where(mine, g_sub - d_sub * 16.0, 0.0), axis=0, keepdims=True)
    count = jnp.zeros(square, F32)
    for r in range(GRID_ROWS):
        owner = jnp.floor(tab_ref[r : r + 1, :].astype(F32) * (1.0 / 16.0))
        count += jnp.where(jnp.broadcast_to(owner, square) == iota(square, 0).astype(F32), 1.0, 0.0)
    most = jnp.max(jnp.sum(count, axis=1, keepdims=True), axis=0, keepdims=True)
    most = jnp.broadcast_to(most, (1, LANES))
    sub = iota((8, LANES), 0)
    table = jnp.where(sub == 3, order, most)
    table = jnp.where(sub == 0, place * PIECE + 36.0 * tile, table)
    table = jnp.where(sub == 1, place * PIECE + 36.0 * jnp.minimum(tile + 1.0, 2.0), table)
    table = jnp.where(sub == 2, off - LANES * tile, table)
    table = jnp.where(sub == 5, used, table)
    table = jnp.where(sub == 6, half, table)
    idx[...] = table.astype(I32)


def column_kernel(row_a, row_b, col_e, col_w, after, mark, col_a, col_b):
    gx, gy = lax.axis_index("gx"), lax.axis_index("gy")
    even_row, even = gx % 2 == 0, gy % 2 == 0
    lane = iota((8, LANES), 1)
    east = jnp.zeros((8, LANES), F32)
    west = jnp.zeros((8, LANES), F32)
    for p in range(PLANES):
        rows = slice(8 * (p % 7), 8 * (p % 7) + 8)
        here = (lane >= 4 * p) & (lane < 4 * p + 4)
        w, e = (
            halo_tile(jnp.where(even_row, a, b), jnp.where(even_row, b, a), p)
            for a, b in (
                (row_a[rows, i : i + LANES], row_b[rows, i : i + LANES]) for i in (0, 640)
            )
        )
        east = jnp.where(here, roll(e, 4 * p + 4, 1), east)
        west = jnp.where(here, roll(w, 4 * p, 1), west)
    e_own, w_own = col_e[...], col_w[...]
    col_a[0:48] = jnp.where(even, e_own, w_own)
    col_b[0:48] = jnp.where(even, w_own, e_own)
    col_a[48:56] = jnp.where(even, east, west)
    col_b[48:56] = jnp.where(even, west, east)


HT = 56
STRIP = 72
STRIPS = 7
T0, U0, V0 = 0, 3, 6
XE, XW, YN, YS = 9, 12, 15, 18
E0, P0, Q0, DEPTH, WETS, QUARTER, DP, DQ, GX, GY = range(21, 31)
FIELDS = 31


def pack_tiles(r):
    lane = iota(r[0].shape, 1)
    t0 = jnp.where(lane < 48, r[0], jnp.where(lane < 96, r[1], r[2]))
    t1 = jnp.where(
        lane < 16, r[2], jnp.where(lane < 64, r[3], jnp.where(lane < 112, r[4], r[5]))
    )
    t2 = jnp.where(lane < 32, r[5], jnp.where(lane < 80, r[6], r[7]))
    return t0, t1, t2


class Step:
    def __init__(self, ext, res):
        self.ext, self.res = ext, res
        self.gx, self.gy = lax.axis_index("gx"), lax.axis_index("gy")

    def put(self, field, t, x, first=8):
        self.ext[field, t, first : first + x.shape[0]] = x

    def mid(self, field, t, first=8, rows=HT):
        return self.ext[field, t, first : first + rows]

    def right(self, field, t, x, k=1, first=8):
        after = (t + 1) % STRIPS if isinstance(t, int) else jnp.where(t == 6, 0, t + 1)
        lane = iota(x.shape, 1)
        y = self.mid(field, after, first, x.shape[0])
        return roll(jnp.where(lane < k, y, x), -k, 1)

    def left(self, field, t, x, k=1, first=8):
        before = (t - 1) % STRIPS if isinstance(t, int) else jnp.where(t == 0, 6, t - 1)
        lane = iota(x.shape, 1)
        y = self.mid(field, before, first, x.shape[0])
        return roll(jnp.where(lane >= LANES - k, y, x), k, 1)

    def place(self, t, planes, part):
        def put(field, x, ring=False):
            if part == "halo":
                self.put(field, t, x, 56)
                if ring:
                    self.put(field, t, x, 0)
            else:
                self.put(field, t, x)
                if ring:
                    self.put(field, t, x[0:8], 64)
                    if part == "all":
                        self.put(field, t, x[48:56], 0)

        wet = planes(WET)
        put(WETS, wet)
        put(QUARTER, 0.25 * wet)
        sums = []
        for q in range(3):
            heat = planes(q) * wet
            put(T0 + q, heat, ring=True)
            b = heat - 0.1 * heat * heat
            sums.append(sums[-1] + b if sums else b)
        mean = (sums[0] + sums[1] + sums[2]) * (1.0 / 3.0)
        for q in range(3):
            push = 0.15 * (sums[q] - mean)
            u, v = planes(3 + q) * wet, planes(6 + q) * wet
            put(U0 + q, u, ring=True)
            put(V0 + q, v)
            u, v = 0.1 * u, 0.1 * v
            put(XE + q, u - push)
            put(XW + q, u + push)
            put(YN + q, v - push, ring=True)
            put(YS + q, v + push, ring=True)
        put(E0, planes(9) * wet)
        east, north = planes(10) * wet, planes(11) * wet
        depth = 0.25 * planes(12)
        put(P0, east)
        put(Q0, north)
        put(DEPTH, depth)
        put(DP, depth * east)
        put(DQ, depth * north, ring=True)

    def tracer(self, t, first, rows):
        mid = functools.partial(self.mid, t=t, rows=rows)
        wet = mid(WETS, first=first)
        for q in range(3):
            f = T0 + q
            x = mid(f, first=first)
            xe, xw = self.right(f, t, x, 1, first), self.left(f, t, x, 1, first)
            xee, xww = self.right(f, t, x, 2, first), self.left(f, t, x, 2, first)
            xn, xs = mid(f, first=first + 1), mid(f, first=first - 1)
            xnn, xss = mid(f, first=first + 2), mid(f, first=first - 2)
            dx = (3.2 / 12.0) * (xw - xe) + (0.4 / 12.0) * (xee - xww)
            dy = (3.2 / 12.0) * (xs - xn) + (0.4 / 12.0) * (xnn - xss)
            ring = 0.1 * ((xe + xw) + (xn + xs))
            u, v = mid(U0 + q, first=first), mid(V0 + q, first=first)
            new = 0.6 * x + ring + (u * dx + v * dy)
            self.res[t, 48 * q + first - 8 : 48 * q + first - 8 + rows] = wet * new

    def motion(self, t, first, rows):
        row = iota((rows, LANES), 0) + (first - 8)
        north = self.gx * BLOCK + row - jnp.where(row >= 52, HT, 0)
        turn = 0.15 * (2.0 * (north.astype(F32) + 0.5) / LAT - 1.0)
        mid = functools.partial(self.mid, t=t, rows=rows)
        wet = mid(WETS, first=first)
        kept = min(rows, 56 - first)
        gain_x = gain_y = None
        for q in range(3):
            u, v = mid(U0 + q, first=first), mid(V0 + q, first=first)
            xe, xw = mid(XE + q, first=first), mid(XW + q, first=first)
            side_x = self.right(XE + q, t, xe, 1, first) + self.left(XW + q, t, xw, 1, first)
            side_y = mid(YN + q, first=first + 1) + mid(YS + q, first=first - 1)
            ring_u = 0.1 * (mid(U0 + q, first=first + 1) + mid(U0 + q, first=first - 1))
            ring_v = 0.1 * (
                self.right(V0 + q, t, v, 1, first) + self.left(V0 + q, t, v, 1, first)
            )
            new_u = wet * ((0.6 * u + turn * v) + (side_x + ring_u))
            new_v = wet * ((0.6 * v - turn * u) + (side_y + ring_v))
            spot = 144 + 48 * q + first - 8
            self.res[t, spot : spot + kept] = new_u[:kept]
            self.res[t, spot + 144 : spot + 144 + kept] = new_v[:kept]
            du, dv = new_u - u, new_v - v
            gain_x = du if gain_x is None else gain_x + du
            gain_y = dv if gain_y is None else gain_y + dv
        self.put(GX, t, gain_x * (1.0 / 3.0), first)
        self.put(GY, t, gain_y * (1.0 / 3.0), first)

    def passes(self):
        mid, put = self.mid, self.put
        for last in (False, True):
            for t in range(STRIPS):
                flux = mid(DP, t)
                div = (self.right(DP, t, flux) - self.left(DP, t, flux)) + (
                    mid(DQ, t, 9) - mid(DQ, t, 7)
                )
                new = mid(E0, t) - mid(WETS, t) * div
                put(E0, t, new)
                put(E0, t, new[48:56], 0)
                put(E0, t, new[0:8], 64)
                if last:
                    self.res[t, 432:480] = new[:48]
            for t in range(STRIPS):
                e, quarter = mid(E0, t), mid(QUARTER, t)
                ex = self.right(E0, t, e) - self.left(E0, t, e)
                ey = mid(E0, t, 9) - mid(E0, t, 7)
                new_p = (mid(P0, t) + mid(GX, t)) - quarter * ex
                new_q = (mid(Q0, t) + mid(GY, t)) - quarter * ey
                if last:
                    self.res[t, 480:528] = new_p[:48]
                    self.res[t, 528:576] = new_q[:48]
                else:
                    cross = mid(DEPTH, t) * new_q
                    put(P0, t, new_p)
                    put(Q0, t, new_q)
                    put(DP, t, mid(DEPTH, t) * new_p)
                    put(DQ, t, cross)
                    put(DQ, t, cross[48:56], 0)
                    put(DQ, t, cross[0:8], 64)


def cut_pieces(rounds, idx, res, send):
    spots = []
    for c in range(8 * rounds):
        off = 48 * idx[3, c]
        inner = off & 127
        spots.append((off >> 7, inner, (48 * c + 256 - inner) & 127))

    def cut(q):
        pair = 2 * q
        for h in range(rounds):
            done = []
            for start, n in ((64 * q, 64), (512 + 8 * q, 8)):
                rows = pl.ds(start, n) if isinstance(q, int) else pl.ds(pl.multiple_of(start, 8), n)
                lanes = iota((n, LANES), 1)
                moved = []
                for tile, inner, shift in spots[8 * h : 8 * h + 8]:
                    x = jnp.where(lanes >= inner, res[tile, rows], res[tile + 1, rows])
                    moved.append(pltpu.roll(x, shift, 1))
                done.append(pack_tiles(moved))
            mains, rests = done
            for i in range(3):
                base = PIECE * h + 36 * i
                send[pair, base + 32 : base + 40] = rests[i]
                send[pair + 1, base + 28 : base + 36] = rests[i]
            for i in range(3):
                base = PIECE * h + 36 * i
                send[pair, base : base + 32] = mains[i][:32]
                send[pair + 1, base : base + 32] = mains[i][32:]

    if rounds == 1:
        for q in range(8):
            cut(q)
    else:
        pl.loop(0, 8)(cut)


def interior_kernel(*refs):
    raw = refs[:8]
    step = Step(*refs[9:11])
    refs[11][...] = jnp.zeros((8, LANES), F32)

    @pl.loop(0, 6)
    def fill(t):
        lanes = pl.ds(pl.multiple_of(t * LANES, LANES), LANES)
        step.place(t, lambda p: read_plane(raw, p, slice(None), lanes), "own")

    @pl.loop(1, 5)
    def inner(t):
        step.tracer(t, 16, 32)
        step.motion(t, 16, 32)


def middle_kernel(row_a, row_b, ext_in, res_in, ext, res):
    step = Step(ext, res)
    even_row = step.gx % 2 == 0
    for t in range(6):
        lanes = slice(LANES * t, LANES * t + LANES)

        def planes(p, lanes=lanes):
            rows = slice(8 * (p % 7), 8 * (p % 7) + 8)
            a, b = row_a[rows, lanes], row_b[rows, lanes]
            return halo_tile(jnp.where(even_row, a, b), jnp.where(even_row, b, a), p)

        step.place(t, planes, "halo")

    @pl.loop(1, 5)
    def edge(t):
        step.tracer(t, 8, 8)
        step.tracer(t, 48, 8)
        step.motion(t, 8, 8)
        step.motion(t, 48, 16)


def finish_kernel(col_a, col_b, idx, ext_in, res_in, ext, res, send, table, sem):
    copy = pltpu.make_async_copy(idx, table, sem)
    copy.start()
    step = Step(ext, res)
    even = step.gy % 2 == 0

    def side(p):
        a, b = col_a[...], col_b[...]
        from_east = roll(jnp.where(even, a, b), -4 * p, 1)
        from_west = roll(jnp.where(even, b, a), 124 - 4 * p, 1)
        lane = iota((HT, LANES), 1)
        return jnp.where(lane < 4, from_east, jnp.where(lane >= 124, from_west, 0.0))

    step.place(6, side, "all")
    for t in (0, 5):
        step.tracer(t, 8, 48)
    for t in (0, 5, 6):
        step.motion(t, 8, 56)
    step.passes()
    copy.wait()
    cut_pieces(1, table, res, send)


def cut_kernel(idx, res, send):
    cut_pieces(2, idx, res, send)


def route_kernel(rounds, idx, got, send):
    lane = iota((36, LANES), 1)

    @pl.loop(0, 2)
    def targets(part):
        for j in range(8):
            d = part * 8 + j
            moved = []
            for s in range(SLOTS):
                slot = d * SLOTS + s
                first, after, inner = idx[0, slot], idx[1, slot], idx[2, slot]
                if rounds > 1:
                    first, after = (
                        x + PIECE * (x // PIECE) + PIECE * idx[6, slot] for x in (first, after)
                    )
                near = got[pl.ds(first, 36), :]
                far = got[pl.ds(after, 36), :]
                x = jnp.where(lane >= inner, near, far)
                moved.append(pltpu.roll(x, (48 * s + 256 - inner) & 127, 1))
            for i, x in enumerate(pack_tiles(moved)):
                send[d, 36 * i : 36 * i + 36] = x


def settle_kernel(idx, got, heat, zonal, merid, height, east, north):
    used = jnp.broadcast_to(idx[5:6, :], (8, LANES))
    lane = iota((8, LANES), 1)
    low = iota((8, LANES), 0) < 4
    outs = (heat, zonal, merid, height, east, north)

    def put(tile_row, i, x):
        x = jnp.where(lane + LANES * i < used, x, 0.0)
        plane, rows = tile_row // 6, slice(8 * (tile_row % 6), 8 * (tile_row % 6) + 8)
        lanes = slice(LANES * i, LANES * i + LANES)
        if plane < 9:
            outs[plane // 3][plane % 3, rows, lanes] = x
        else:
            outs[plane - 6][rows, lanes] = x

    for i in range(3):
        for k in range(ROW_DEVICES):
            for t in range(4):
                put(4 * k + t, i, got[k, 36 * i + 8 * t : 36 * i + 8 * t + 8, :])
        for q in range(8):
            a = got[2 * q, 36 * i + 32 : 36 * i + 40, :]
            b = got[2 * q + 1, 36 * i + 28 : 36 * i + 36, :]
            put(64 + q, i, jnp.where(low, a, b))


def f32(*shape):
    return jax.ShapeDtypeStruct(shape, F32)


def cost(us):
    return pl.CostEstimate(flops=us * 1_000_000, bytes_accessed=us * 2_000_000, transcendentals=0)


VM = pl.BlockSpec(memory_space=pltpu.VMEM)
SM = pl.BlockSpec(memory_space=pltpu.SMEM)


def shards(heat, zonal, merid, height, east, north, depth, marine, sequence):
    raw = (heat, zonal, merid, height, east, north, depth, marine)
    tab = sequence.reshape(GRID_ROWS, LANES)

    def call(kernel, name, operands, ins, outs, shapes, mega=8, us=1, **more):
        more = {"in_specs": ins, "out_specs": outs, **more}
        return pl.pallas_call(
            kernel,
            out_shape=shapes,
            compiler_params=pltpu.CompilerParams(vmem_limit_bytes=mega << 20),
            cost_estimate=cost(us),
            name=name,
            **more,
        )(*operands)

    def part(x, height, width):
        return pltpu.VMEM(x.shape[:-2] + (height, width), x.dtype)

    scratch = [part(x, 8, 768) for _ in range(2) for x in raw]
    scratch += [part(x, BLOCK, LANES) for _ in range(2) for x in raw]
    row_a, row_b, col_e, col_w = call(
        edge_kernel,
        "edges",
        raw,
        [pl.BlockSpec(memory_space=pltpu.HBM)] * 8,
        (VM,) * 4,
        (f32(56, 768), f32(56, 768), f32(48, 128), f32(48, 128)),
        mega=4,
        scratch_shapes=scratch + [pltpu.SemaphoreType.DMA((32,))],
    )
    idx = call(
        place_kernel,
        "places",
        (tab, col_e),
        [VM, VM],
        VM,
        jax.ShapeDtypeStruct((8, LANES), I32),
        mega=4,
    )
    full = (idx[4:5, 0:1] > 8).astype(I32)
    fields = (f32(FIELDS, STRIPS, STRIP, LANES), f32(STRIPS, 576, LANES))
    ext, res, mark = call(
        interior_kernel,
        "interior",
        raw + (col_e,),
        [VM] * 9,
        (VM,) * 3,
        fields + (f32(8, LANES),),
        us=2,
    )

    def swaps(axis, size, first, second):
        near = [(i, i ^ 1) for i in range(size)]
        far = [(i, i + 1) for i in range(1, size - 1, 2)]
        far += [(j, i) for i, j in far]
        return lax.ppermute(first, axis, near), lax.ppermute(second, axis, far)

    row_a, row_b = swaps("gx", GRID_ROWS, row_a, row_b)
    col_a, col_b = call(
        column_kernel,
        "columns",
        (row_a, row_b, col_e, col_w, full, mark),
        [VM] * 6,
        (VM, VM),
        (f32(56, 128), f32(56, 128)),
        mega=4,
    )
    ext, res = call(
        middle_kernel,
        "middle",
        (row_a, row_b, ext, res),
        [VM] * 4,
        (VM, VM),
        fields,
        us=2,
        input_output_aliases={2: 0, 3: 1},
    )
    col_a, col_b = swaps("gy", ROW_DEVICES, col_a, col_b)
    _, res, send = call(
        finish_kernel,
        "finish",
        (col_a, col_b, idx, ext, res),
        [VM] * 5,
        (VM,) * 3,
        fields + (f32(ROW_DEVICES, PIECE, LANES),),
        us=4,
        input_output_aliases={3: 0, 4: 1},
        scratch_shapes=[pltpu.SMEM((8, LANES), I32), pltpu.SemaphoreType.DMA],
    )

    def deliver(rounds, send):
        got = lax.all_to_all(send, "gy", 0, 0, tiled=True)
        got = got.reshape(ROW_DEVICES * rounds * PIECE, LANES)
        piece = f32(ROW_DEVICES, PIECE, LANES)
        send = call(
            functools.partial(route_kernel, rounds), "route", (idx, got), [SM, VM], VM, piece
        )
        got = lax.all_to_all(send, "gy", 0, 0, tiled=True)
        shapes = (f32(3, 48, 384),) * 3 + (f32(48, 384),) * 3
        return call(settle_kernel, "settle", (idx, got), [VM, VM], (VM,) * 6, shapes)

    def crowded():
        both = f32(ROW_DEVICES, 2 * PIECE, LANES)
        return deliver(2, call(cut_kernel, "cut", (idx, res), [SM, VM], VM, both))

    return lax.cond(full[0, 0] > 0, crowded, lambda: deliver(1, send))


def solution(mesh):
    level, flat = P(None, "gx", "gy"), P("gx", "gy")
    return jax.shard_map(
        shards,
        mesh=mesh,
        in_specs=(level,) * 3 + (flat,) * 5 + (P(),),
        out_specs=(P(None, None, ("gx", "gy")),) * 3 + (P(None, ("gx", "gy")),) * 3,
        check_vma=False,
    )
```

```python
import functools

import jax
import jax.numpy as jnp
from jax import lax
from jax.experimental import pallas as pl
from jax.experimental.pallas import tpu as pltpu
from jax.sharding import PartitionSpec as P

BLOCK = 48
SLOTS = 8
ROW_DEVICES = 16
GRID_ROWS = 8
LAT = 384
PLANES = 14
WET = 13
LANES = 128
PIECE = 112

F32 = jnp.float32
I32 = jnp.int32


def iota(shape, dim):
    return lax.broadcasted_iota(I32, shape, dim)


def roll(x, shift, axis):
    return pltpu.roll(x, shift % x.shape[axis], axis)


def plane_of(refs, p):
    if p < 9:
        return refs[p // 3], (p % 3,)
    return refs[3 + p - 9], ()


def read_plane(refs, p, rows, lanes):
    ref, lead = plane_of(refs, p)
    x = ref[lead + (rows, lanes)]
    return x.astype(F32) if p == WET else x


def halo_tile(north, south, p):
    low = iota(north.shape, 0) < 4
    if p < 7:
        return jnp.where(low, north, roll(south, 4, 0))
    return jnp.where(low, roll(north, 4, 0), south)


EDGES = (
    (slice(0, 8), slice(None)),
    (slice(40, 48), slice(None)),
    (slice(None), slice(0, 128)),
    (slice(None), slice(640, 768)),
)


def edge_kernel(*refs):
    raw = refs[:8]
    row_a, row_b, col_e, col_w = refs[8:12]
    parts, sem = refs[12:44], refs[44]
    bottoms, tops, lefts, rights = (parts[8 * i : 8 * i + 8] for i in range(4))
    copies = []
    for i, (rows, lanes) in enumerate(EDGES):
        for j, x in enumerate(raw):
            where = (slice(None),) * (len(x.shape) - 2) + (rows, lanes)
            n = 8 * i + j
            copies.append(pltpu.make_async_copy(x.at[where], parts[n], sem.at[n]))
            copies[-1].start()
    for copy in copies:
        copy.wait()
    gx, gy = lax.axis_index("gx"), lax.axis_index("gy")
    even = gx % 2 == 0
    for m in range(7):
        low = iota((8, 768), 0) < 4
        full = slice(None)
        t0, t1 = (read_plane(tops, q, full, full) for q in (m, m + 7))
        b0, b1 = (read_plane(bottoms, q, full, full) for q in (m, m + 7))
        top = jnp.where(low, roll(t0, 4, 0), t1)
        bottom = jnp.where(low, b0, roll(b1, 4, 0))
        row_a[8 * m : 8 * m + 8] = jnp.where(even, top, bottom)
        row_b[8 * m : 8 * m + 8] = jnp.where(even, bottom, top)
    lane = iota((BLOCK, LANES), 1)
    east = jnp.zeros((BLOCK, LANES), F32)
    west = jnp.zeros((BLOCK, LANES), F32)
    for p in range(PLANES):
        here = (lane >= 4 * p) & (lane < 4 * p + 4)
        e = read_plane(rights, p, slice(None), slice(None))
        w = read_plane(lefts, p, slice(None), slice(None))
        east = jnp.where(here, roll(e, 4 * p + 4, 1), east)
        west = jnp.where(here, roll(w, 4 * p, 1), west)
    col_e[...] = east
    col_w[...] = west


def place_kernel(tab_ref, after, idx, full):
    gx, gy = lax.axis_index("gx"), lax.axis_index("gy")
    square = (LANES, LANES)
    g = tab_ref[pl.ds(gx, 1), :].astype(F32)
    g_lane = jnp.broadcast_to(g, square)
    diagonal = iota(square, 0) == iota(square, 1)
    g_sub = jnp.sum(jnp.where(diagonal, g_lane, 0.0), axis=1, keepdims=True)
    g_sub = jnp.broadcast_to(g_sub, square)
    d_lane = jnp.floor(g_lane * (1.0 / 16.0))
    d_sub = jnp.floor(g_sub * (1.0 / 16.0))
    same = d_lane == d_sub
    rank_lane = jnp.sum(jnp.where(same & (g_sub < g_lane), 1.0, 0.0), axis=0, keepdims=True)
    rank_sub = jnp.sum(jnp.where(same & (g_lane < g_sub), 1.0, 0.0), axis=1, keepdims=True)
    first = (gx * ROW_DEVICES).astype(F32)
    source = jnp.floor(g * (1.0 / 16.0)) - first
    listed = g >= 0.0
    half = jnp.where(rank_lane >= 8.0, 1.0, 0.0)
    half = jnp.where(listed, half, 0.0)
    place = jnp.where(listed, source, 0.0)
    off = jnp.where(listed, 48.0 * (rank_lane - 8.0 * half), 0.0)
    tile = jnp.floor(off * (1.0 / LANES))
    own = (iota((1, LANES), 1) // SLOTS == gy) & listed
    used = jnp.sum(jnp.where(own, float(BLOCK), 0.0), axis=1, keepdims=True)
    used = jnp.broadcast_to(used, (1, LANES))
    me = (gx * ROW_DEVICES + gy).astype(F32)
    c_lane = iota(square, 1).astype(F32)
    mine = (d_sub == me) & (jnp.broadcast_to(rank_sub, square) == c_lane)
    order = jnp.sum(jnp.where(mine, g_sub - d_sub * 16.0, 0.0), axis=0, keepdims=True)
    count = jnp.zeros(square, F32)
    for r in range(GRID_ROWS):
        owner = jnp.floor(tab_ref[r : r + 1, :].astype(F32) * (1.0 / 16.0))
        count += jnp.where(jnp.broadcast_to(owner, square) == iota(square, 0).astype(F32), 1.0, 0.0)
    most = jnp.max(jnp.sum(count, axis=1, keepdims=True), axis=0, keepdims=True)
    most = jnp.broadcast_to(most, (1, LANES))
    sub = iota((8, LANES), 0)
    table = jnp.where(sub == 3, order, most)
    table = jnp.where(sub == 0, place * PIECE + 36.0 * tile, table)
    table = jnp.where(sub == 1, place * PIECE + 36.0 * jnp.minimum(tile + 1.0, 2.0), table)
    table = jnp.where(sub == 2, off - LANES * tile, table)
    table = jnp.where(sub == 5, used, table)
    table = jnp.where(sub == 6, half, table)
    idx[...] = table.astype(I32)
    full[...] = most[:, :1].astype(I32)


def column_kernel(row_a, row_b, col_e, col_w, after, mark, col_a, col_b):
    gx, gy = lax.axis_index("gx"), lax.axis_index("gy")
    even_row, even = gx % 2 == 0, gy % 2 == 0
    lane = iota((8, LANES), 1)
    east = jnp.zeros((8, LANES), F32)
    west = jnp.zeros((8, LANES), F32)
    for p in range(PLANES):
        rows = slice(8 * (p % 7), 8 * (p % 7) + 8)
        here = (lane >= 4 * p) & (lane < 4 * p + 4)
        w, e = (
            halo_tile(jnp.where(even_row, a, b), jnp.where(even_row, b, a), p)
            for a, b in (
                (row_a[rows, i : i + LANES], row_b[rows, i : i + LANES]) for i in (0, 640)
            )
        )
        east = jnp.where(here, roll(e, 4 * p + 4, 1), east)
        west = jnp.where(here, roll(w, 4 * p, 1), west)
    e_own, w_own = col_e[...], col_w[...]
    col_a[0:48] = jnp.where(even, e_own, w_own)
    col_b[0:48] = jnp.where(even, w_own, e_own)
    col_a[48:56] = jnp.where(even, east, west)
    col_b[48:56] = jnp.where(even, west, east)


HT = 56
STRIP = 72
STRIPS = 7
T0, U0, V0 = 0, 3, 6
XE, XW, YN, YS = 9, 12, 15, 18
E0, P0, Q0, DEPTH, WETS, QUARTER, DP, DQ, GX, GY = range(21, 31)
FIELDS = 31


def pack_tiles(r):
    lane = iota(r[0].shape, 1)
    t0 = jnp.where(lane < 48, r[0], jnp.where(lane < 96, r[1], r[2]))
    t1 = jnp.where(
        lane < 16, r[2], jnp.where(lane < 64, r[3], jnp.where(lane < 112, r[4], r[5]))
    )
    t2 = jnp.where(lane < 32, r[5], jnp.where(lane < 80, r[6], r[7]))
    return t0, t1, t2


class Step:
    def __init__(self, ext, res):
        self.ext, self.res = ext, res
        self.gx, self.gy = lax.axis_index("gx"), lax.axis_index("gy")

    def put(self, field, t, x, first=8):
        self.ext[field, t, first : first + x.shape[0]] = x

    def mid(self, field, t, first=8, rows=HT):
        return self.ext[field, t, first : first + rows]

    def right(self, field, t, x, k=1, first=8):
        after = (t + 1) % STRIPS if isinstance(t, int) else jnp.where(t == 6, 0, t + 1)
        lane = iota(x.shape, 1)
        y = self.mid(field, after, first, x.shape[0])
        return roll(jnp.where(lane < k, y, x), -k, 1)

    def left(self, field, t, x, k=1, first=8):
        before = (t - 1) % STRIPS if isinstance(t, int) else jnp.where(t == 0, 6, t - 1)
        lane = iota(x.shape, 1)
        y = self.mid(field, before, first, x.shape[0])
        return roll(jnp.where(lane >= LANES - k, y, x), k, 1)

    def place(self, t, planes, part):
        def put(field, x, ring=False):
            if part == "halo":
                self.put(field, t, x, 56)
                if ring:
                    self.put(field, t, x, 0)
            else:
                self.put(field, t, x)
                if ring:
                    self.put(field, t, x[0:8], 64)
                    if part == "all":
                        self.put(field, t, x[48:56], 0)

        wet = planes(WET)
        put(WETS, wet)
        put(QUARTER, 0.25 * wet)
        sums = []
        for q in range(3):
            heat = planes(q) * wet
            put(T0 + q, heat, ring=True)
            b = heat - 0.1 * heat * heat
            sums.append(sums[-1] + b if sums else b)
        mean = (sums[0] + sums[1] + sums[2]) * (1.0 / 3.0)
        for q in range(3):
            push = 0.15 * (sums[q] - mean)
            u, v = planes(3 + q) * wet, planes(6 + q) * wet
            put(U0 + q, u, ring=True)
            put(V0 + q, v)
            u, v = 0.1 * u, 0.1 * v
            put(XE + q, u - push)
            put(XW + q, u + push)
            put(YN + q, v - push, ring=True)
            put(YS + q, v + push, ring=True)
        put(E0, planes(9) * wet)
        east, north = planes(10) * wet, planes(11) * wet
        depth = 0.25 * planes(12)
        put(P0, east)
        put(Q0, north)
        put(DEPTH, depth)
        put(DP, depth * east)
        put(DQ, depth * north, ring=True)

    def tracer(self, t, first, rows):
        mid = functools.partial(self.mid, t=t, rows=rows)
        wet = mid(WETS, first=first)
        for q in range(3):
            f = T0 + q
            x = mid(f, first=first)
            xe, xw = self.right(f, t, x, 1, first), self.left(f, t, x, 1, first)
            xee, xww = self.right(f, t, x, 2, first), self.left(f, t, x, 2, first)
            xn, xs = mid(f, first=first + 1), mid(f, first=first - 1)
            xnn, xss = mid(f, first=first + 2), mid(f, first=first - 2)
            dx = (3.2 / 12.0) * (xw - xe) + (0.4 / 12.0) * (xee - xww)
            dy = (3.2 / 12.0) * (xs - xn) + (0.4 / 12.0) * (xnn - xss)
            ring = 0.1 * ((xe + xw) + (xn + xs))
            u, v = mid(U0 + q, first=first), mid(V0 + q, first=first)
            new = 0.6 * x + ring + (u * dx + v * dy)
            self.res[t, 48 * q + first - 8 : 48 * q + first - 8 + rows] = wet * new

    def motion(self, t, first, rows):
        row = iota((rows, LANES), 0) + (first - 8)
        north = self.gx * BLOCK + row - jnp.where(row >= 52, HT, 0)
        turn = 0.15 * (2.0 * (north.astype(F32) + 0.5) / LAT - 1.0)
        mid = functools.partial(self.mid, t=t, rows=rows)
        wet = mid(WETS, first=first)
        kept = min(rows, 56 - first)
        gain_x = gain_y = None
        for q in range(3):
            u, v = mid(U0 + q, first=first), mid(V0 + q, first=first)
            xe, xw = mid(XE + q, first=first), mid(XW + q, first=first)
            side_x = self.right(XE + q, t, xe, 1, first) + self.left(XW + q, t, xw, 1, first)
            side_y = mid(YN + q, first=first + 1) + mid(YS + q, first=first - 1)
            ring_u = 0.1 * (mid(U0 + q, first=first + 1) + mid(U0 + q, first=first - 1))
            ring_v = 0.1 * (
                self.right(V0 + q, t, v, 1, first) + self.left(V0 + q, t, v, 1, first)
            )
            new_u = wet * ((0.6 * u + turn * v) + (side_x + ring_u))
            new_v = wet * ((0.6 * v - turn * u) + (side_y + ring_v))
            spot = 144 + 48 * q + first - 8
            self.res[t, spot : spot + kept] = new_u[:kept]
            self.res[t, spot + 144 : spot + 144 + kept] = new_v[:kept]
            du, dv = new_u - u, new_v - v
            gain_x = du if gain_x is None else gain_x + du
            gain_y = dv if gain_y is None else gain_y + dv
        self.put(GX, t, gain_x * (1.0 / 3.0), first)
        self.put(GY, t, gain_y * (1.0 / 3.0), first)

    def passes(self):
        mid, put = self.mid, self.put
        for last in (False, True):
            for t in range(STRIPS):
                flux = mid(DP, t)
                div = (self.right(DP, t, flux) - self.left(DP, t, flux)) + (
                    mid(DQ, t, 9) - mid(DQ, t, 7)
                )
                new = mid(E0, t) - mid(WETS, t) * div
                put(E0, t, new)
                put(E0, t, new[48:56], 0)
                put(E0, t, new[0:8], 64)
                if last:
                    self.res[t, 432:480] = new[:48]
            for t in range(STRIPS):
                e, quarter = mid(E0, t), mid(QUARTER, t)
                ex = self.right(E0, t, e) - self.left(E0, t, e)
                ey = mid(E0, t, 9) - mid(E0, t, 7)
                new_p = (mid(P0, t) + mid(GX, t)) - quarter * ex
                new_q = (mid(Q0, t) + mid(GY, t)) - quarter * ey
                if last:
                    self.res[t, 480:528] = new_p[:48]
                    self.res[t, 528:576] = new_q[:48]
                else:
                    cross = mid(DEPTH, t) * new_q
                    put(P0, t, new_p)
                    put(Q0, t, new_q)
                    put(DP, t, mid(DEPTH, t) * new_p)
                    put(DQ, t, cross)
                    put(DQ, t, cross[48:56], 0)
                    put(DQ, t, cross[0:8], 64)


def cut_pieces(rounds, idx, res, send):
    spots = []
    for c in range(8 * rounds):
        off = 48 * idx[3, c]
        inner = off & 127
        spots.append((off >> 7, inner, (48 * c + 256 - inner) & 127))

    def cut(q):
        pair = 2 * q
        for h in range(rounds):
            done = []
            for start, n in ((64 * q, 64), (512 + 8 * q, 8)):
                rows = pl.ds(start, n) if isinstance(q, int) else pl.ds(pl.multiple_of(start, 8), n)
                lanes = iota((n, LANES), 1)
                moved = []
                for tile, inner, shift in spots[8 * h : 8 * h + 8]:
                    x = jnp.where(lanes >= inner, res[tile, rows], res[tile + 1, rows])
                    moved.append(pltpu.roll(x, shift, 1))
                done.append(pack_tiles(moved))
            mains, rests = done
            for i in range(3):
                base = PIECE * h + 36 * i
                send[pair, base + 32 : base + 40] = rests[i]
                send[pair + 1, base + 28 : base + 36] = rests[i]
            for i in range(3):
                base = PIECE * h + 36 * i
                send[pair, base : base + 32] = mains[i][:32]
                send[pair + 1, base : base + 32] = mains[i][32:]

    if rounds == 1:
        for q in range(8):
            cut(q)
    else:
        pl.loop(0, 8)(cut)


def interior_kernel(*refs):
    raw = refs[:8]
    step = Step(*refs[9:11])
    refs[11][...] = jnp.zeros((8, LANES), F32)

    @pl.loop(0, 6)
    def fill(t):
        lanes = pl.ds(pl.multiple_of(t * LANES, LANES), LANES)
        step.place(t, lambda p: read_plane(raw, p, slice(None), lanes), "own")

    @pl.loop(1, 5)
    def inner(t):
        step.tracer(t, 16, 32)
        step.motion(t, 16, 32)


def middle_kernel(row_a, row_b, ext_in, res_in, ext, res):
    step = Step(ext, res)
    even_row = step.gx % 2 == 0
    for t in range(6):
        lanes = slice(LANES * t, LANES * t + LANES)

        def planes(p, lanes=lanes):
            rows = slice(8 * (p % 7), 8 * (p % 7) + 8)
            a, b = row_a[rows, lanes], row_b[rows, lanes]
            return halo_tile(jnp.where(even_row, a, b), jnp.where(even_row, b, a), p)

        step.place(t, planes, "halo")

    @pl.loop(1, 5)
    def edge(t):
        step.tracer(t, 8, 8)
        step.tracer(t, 48, 8)
        step.motion(t, 8, 8)
        step.motion(t, 48, 16)


def finish_kernel(col_a, col_b, idx, ext_in, res_in, ext, res, send, table, sem):
    copy = pltpu.make_async_copy(idx, table, sem)
    copy.start()
    step = Step(ext, res)
    even = step.gy % 2 == 0

    def side(p):
        a, b = col_a[...], col_b[...]
        from_east = roll(jnp.where(even, a, b), -4 * p, 1)
        from_west = roll(jnp.where(even, b, a), 124 - 4 * p, 1)
        lane = iota((HT, LANES), 1)
        return jnp.where(lane < 4, from_east, jnp.where(lane >= 124, from_west, 0.0))

    step.place(6, side, "all")
    for t in (0, 5):
        step.tracer(t, 8, 48)
    for t in (0, 5, 6):
        step.motion(t, 8, 56)
    step.passes()
    copy.wait()
    cut_pieces(1, table, res, send)


def cut_kernel(idx, res, send):
    cut_pieces(2, idx, res, send)


def route_kernel(rounds, idx, got, send):
    lane = iota((36, LANES), 1)

    @pl.loop(0, 2)
    def targets(part):
        for j in range(8):
            d = part * 8 + j
            moved = []
            for s in range(SLOTS):
                slot = d * SLOTS + s
                first, after, inner = idx[0, slot], idx[1, slot], idx[2, slot]
                if rounds > 1:
                    first, after = (
                        x + PIECE * (x // PIECE) + PIECE * idx[6, slot] for x in (first, after)
                    )
                near = got[pl.ds(first, 36), :]
                far = got[pl.ds(after, 36), :]
                x = jnp.where(lane >= inner, near, far)
                moved.append(pltpu.roll(x, (48 * s + 256 - inner) & 127, 1))
            for i, x in enumerate(pack_tiles(moved)):
                send[d, 36 * i : 36 * i + 36] = x


def settle_kernel(idx, got, heat, zonal, merid, height, east, north):
    used = jnp.broadcast_to(idx[5:6, :], (8, LANES))
    lane = iota((8, LANES), 1)
    low = iota((8, LANES), 0) < 4
    outs = (heat, zonal, merid, height, east, north)

    def put(tile_row, i, x):
        x = jnp.where(lane + LANES * i < used, x, 0.0)
        plane, rows = tile_row // 6, slice(8 * (tile_row % 6), 8 * (tile_row % 6) + 8)
        lanes = slice(LANES * i, LANES * i + LANES)
        if plane < 9:
            outs[plane // 3][plane % 3, rows, lanes] = x
        else:
            outs[plane - 6][rows, lanes] = x

    for i in range(3):
        for k in range(ROW_DEVICES):
            for t in range(4):
                put(4 * k + t, i, got[k, 36 * i + 8 * t : 36 * i + 8 * t + 8, :])
        for q in range(8):
            a = got[2 * q, 36 * i + 32 : 36 * i + 40, :]
            b = got[2 * q + 1, 36 * i + 28 : 36 * i + 36, :]
            put(64 + q, i, jnp.where(low, a, b))


def f32(*shape):
    return jax.ShapeDtypeStruct(shape, F32)


def cost(us):
    return pl.CostEstimate(flops=us * 1_000_000, bytes_accessed=us * 2_000_000, transcendentals=0)


VM = pl.BlockSpec(memory_space=pltpu.VMEM)
SM = pl.BlockSpec(memory_space=pltpu.SMEM)


def shards(heat, zonal, merid, height, east, north, depth, marine, sequence):
    raw = (heat, zonal, merid, height, east, north, depth, marine)
    tab = sequence.reshape(GRID_ROWS, LANES)

    def call(kernel, name, operands, ins, outs, shapes, mega=8, us=0, **more):
        more = {"in_specs": ins, "out_specs": outs, **more}
        return pl.pallas_call(
            kernel,
            out_shape=shapes,
            compiler_params=pltpu.CompilerParams(vmem_limit_bytes=mega << 20 if mega < 64 else 67_043_328),
            cost_estimate=cost(us) if us else None,
            name=name,
            **more,
        )(*operands)

    def part(x, height, width):
        return pltpu.VMEM(x.shape[:-2] + (height, width), x.dtype)

    scratch = [part(x, 8, 768) for _ in range(2) for x in raw]
    scratch += [part(x, BLOCK, LANES) for _ in range(2) for x in raw]
    row_a, row_b, col_e, col_w = call(
        edge_kernel,
        "edges",
        [pltpu.with_memory_space_constraint(x, pltpu.HBM) for x in raw],
        [pl.BlockSpec(memory_space=pltpu.HBM)] * 8,
        (VM,) * 4,
        (f32(56, 768), f32(56, 768), f32(48, 128), f32(48, 128)),
        mega=4,
        scratch_shapes=scratch + [pltpu.SemaphoreType.DMA((32,))],
    )
    idx, most = call(
        place_kernel,
        "places",
        (tab, col_e),
        [VM, VM],
        (VM, VM),
        (jax.ShapeDtypeStruct((8, LANES), I32), jax.ShapeDtypeStruct((1, 1), I32)),
        mega=4,
    )
    full = (most > 8).astype(I32)
    fields = (f32(FIELDS, STRIPS, STRIP, LANES), f32(STRIPS, 576, LANES))
    ext, res, mark = call(
        interior_kernel,
        "interior",
        raw + (col_e,),
        [VM] * 9,
        (VM,) * 3,
        fields + (f32(8, LANES),),
        us=2,
    )

    def swaps(axis, size, first, second):
        near = [(i, i ^ 1) for i in range(size)]
        far = [(i, i + 1) for i in range(1, size - 1, 2)]
        far += [(j, i) for i, j in far]
        return lax.ppermute(first, axis, near), lax.ppermute(second, axis, far)

    row_a, row_b = swaps("gx", GRID_ROWS, row_a, row_b)
    col_a, col_b = call(
        column_kernel,
        "columns",
        (row_a, row_b, col_e, col_w, full, mark),
        [VM] * 6,
        (VM, VM),
        (f32(56, 128), f32(56, 128)),
        mega=4,
    )
    ext, res = call(
        middle_kernel,
        "middle",
        (row_a, row_b, ext, res),
        [VM] * 4,
        (VM, VM),
        fields,
        us=2,
        input_output_aliases={2: 0, 3: 1},
    )
    col_a, col_b = swaps("gy", ROW_DEVICES, col_a, col_b)
    _, res, send = call(
        finish_kernel,
        "finish",
        (col_a, col_b, idx, ext, res),
        [VM] * 5,
        (VM,) * 3,
        fields + (f32(ROW_DEVICES, PIECE, LANES),),
        us=4,
        input_output_aliases={3: 0, 4: 1},
        scratch_shapes=[pltpu.SMEM((8, LANES), I32), pltpu.SemaphoreType.DMA],
    )

    def deliver(rounds, send):
        got = lax.all_to_all(send, "gy", 0, 0, tiled=True)
        got = got.reshape(ROW_DEVICES * rounds * PIECE, LANES)
        piece = f32(ROW_DEVICES, PIECE, LANES)
        send = call(
            functools.partial(route_kernel, rounds), "route", (idx, got), [SM, VM], VM, piece
        )
        got = lax.all_to_all(send, "gy", 0, 0, tiled=True)
        shapes = (f32(3, 48, 384),) * 3 + (f32(48, 384),) * 3
        return call(settle_kernel, "settle", (idx, got), [VM, VM], (VM,) * 6, shapes)

    def crowded():
        both = f32(ROW_DEVICES, 2 * PIECE, LANES)
        return deliver(2, call(cut_kernel, "cut", (idx, res), [SM, VM], VM, both))

    return lax.cond(full[0, 0] > 0, crowded, lambda: deliver(1, send))


def solution(mesh):
    level, flat = P(None, "gx", "gy"), P("gx", "gy")
    return jax.shard_map(
        shards,
        mesh=mesh,
        in_specs=(level,) * 3 + (flat,) * 5 + (P(),),
        out_specs=(P(None, None, ("gx", "gy")),) * 3 + (P(None, ("gx", "gy")),) * 3,
        check_vma=False,
    )
```

```python
import functools

import jax
import jax.numpy as jnp
from jax import lax
from jax.experimental import pallas as pl
from jax.experimental.pallas import tpu as pltpu
from jax.sharding import PartitionSpec as P

BLOCK = 48
SLOTS = 8
ROW_DEVICES = 16
GRID_ROWS = 8
LAT = 384
PLANES = 14
WET = 13
LANES = 128
PIECE = 112

F32 = jnp.float32
I32 = jnp.int32


def iota(shape, dim):
    return lax.broadcasted_iota(I32, shape, dim)


def roll(x, shift, axis):
    return pltpu.roll(x, shift % x.shape[axis], axis)


def plane_of(refs, p):
    if p < 9:
        return refs[p // 3], (p % 3,)
    return refs[3 + p - 9], ()


def read_plane(refs, p, rows, lanes):
    ref, lead = plane_of(refs, p)
    x = ref[lead + (rows, lanes)]
    return x.astype(F32) if p == WET else x


def halo_tile(north, south, p):
    low = iota(north.shape, 0) < 4
    if p < 7:
        return jnp.where(low, north, roll(south, 4, 0))
    return jnp.where(low, roll(north, 4, 0), south)


EDGES = (
    (slice(0, 8), slice(None)),
    (slice(40, 48), slice(None)),
    (slice(None), slice(0, 128)),
    (slice(None), slice(640, 768)),
)


def edge_kernel(*refs):
    raw = refs[:8]
    row_a, row_b, col_e, col_w = refs[8:12]
    parts, sem = refs[12:44], refs[44]
    bottoms, tops, lefts, rights = (parts[8 * i : 8 * i + 8] for i in range(4))
    copies = []
    for i, (rows, lanes) in enumerate(EDGES):
        for j, x in enumerate(raw):
            where = (slice(None),) * (len(x.shape) - 2) + (rows, lanes)
            n = 8 * i + j
            copies.append(pltpu.make_async_copy(x.at[where], parts[n], sem.at[n]))
            copies[-1].start()
    for copy in copies:
        copy.wait()
    gx, gy = lax.axis_index("gx"), lax.axis_index("gy")
    even = gx % 2 == 0
    for m in range(7):
        low = iota((8, 768), 0) < 4
        full = slice(None)
        t0, t1 = (read_plane(tops, q, full, full) for q in (m, m + 7))
        b0, b1 = (read_plane(bottoms, q, full, full) for q in (m, m + 7))
        top = jnp.where(low, roll(t0, 4, 0), t1)
        bottom = jnp.where(low, b0, roll(b1, 4, 0))
        row_a[8 * m : 8 * m + 8] = jnp.where(even, top, bottom)
        row_b[8 * m : 8 * m + 8] = jnp.where(even, bottom, top)
    lane = iota((BLOCK, LANES), 1)
    east = jnp.zeros((BLOCK, LANES), F32)
    west = jnp.zeros((BLOCK, LANES), F32)
    for p in range(PLANES):
        here = (lane >= 4 * p) & (lane < 4 * p + 4)
        e = read_plane(rights, p, slice(None), slice(None))
        w = read_plane(lefts, p, slice(None), slice(None))
        east = jnp.where(here, roll(e, 4 * p + 4, 1), east)
        west = jnp.where(here, roll(w, 4 * p, 1), west)
    col_e[...] = east
    col_w[...] = west


def place_tables(tab_ref, idx, full):
    gx, gy = lax.axis_index("gx"), lax.axis_index("gy")
    square = (LANES, LANES)
    g = tab_ref[pl.ds(gx, 1), :].astype(F32)
    g_lane = jnp.broadcast_to(g, square)
    diagonal = iota(square, 0) == iota(square, 1)
    g_sub = jnp.sum(jnp.where(diagonal, g_lane, 0.0), axis=1, keepdims=True)
    g_sub = jnp.broadcast_to(g_sub, square)
    d_lane = jnp.floor(g_lane * (1.0 / 16.0))
    d_sub = jnp.floor(g_sub * (1.0 / 16.0))
    same = d_lane == d_sub
    rank_lane = jnp.sum(jnp.where(same & (g_sub < g_lane), 1.0, 0.0), axis=0, keepdims=True)
    rank_sub = jnp.sum(jnp.where(same & (g_lane < g_sub), 1.0, 0.0), axis=1, keepdims=True)
    first = (gx * ROW_DEVICES).astype(F32)
    source = jnp.floor(g * (1.0 / 16.0)) - first
    listed = g >= 0.0
    half = jnp.where(rank_lane >= 8.0, 1.0, 0.0)
    half = jnp.where(listed, half, 0.0)
    place = jnp.where(listed, source, 0.0)
    off = jnp.where(listed, 48.0 * (rank_lane - 8.0 * half), 0.0)
    tile = jnp.floor(off * (1.0 / LANES))
    own = (iota((1, LANES), 1) // SLOTS == gy) & listed
    used = jnp.sum(jnp.where(own, float(BLOCK), 0.0), axis=1, keepdims=True)
    used = jnp.broadcast_to(used, (1, LANES))
    me = (gx * ROW_DEVICES + gy).astype(F32)
    c_lane = iota(square, 1).astype(F32)
    mine = (d_sub == me) & (jnp.broadcast_to(rank_sub, square) == c_lane)
    order = jnp.sum(jnp.where(mine, g_sub - d_sub * 16.0, 0.0), axis=0, keepdims=True)
    count = jnp.zeros(square, F32)
    for r in range(GRID_ROWS):
        owner = jnp.floor(tab_ref[r : r + 1, :].astype(F32) * (1.0 / 16.0))
        count += jnp.where(jnp.broadcast_to(owner, square) == iota(square, 0).astype(F32), 1.0, 0.0)
    most = jnp.max(jnp.sum(count, axis=1, keepdims=True), axis=0, keepdims=True)
    most = jnp.broadcast_to(most, (1, LANES))
    sub = iota((8, LANES), 0)
    table = jnp.where(sub == 3, order, most)
    table = jnp.where(sub == 0, place * PIECE + 36.0 * tile, table)
    table = jnp.where(sub == 1, place * PIECE + 36.0 * jnp.minimum(tile + 1.0, 2.0), table)
    table = jnp.where(sub == 2, off - LANES * tile, table)
    table = jnp.where(sub == 5, used, table)
    table = jnp.where(sub == 6, half, table)
    idx[...] = table.astype(I32)
    full[...] = most[:, :1].astype(I32)


def column_kernel(row_a, row_b, col_e, col_w, after, col_a, col_b):
    gx, gy = lax.axis_index("gx"), lax.axis_index("gy")
    even_row, even = gx % 2 == 0, gy % 2 == 0
    lane = iota((8, LANES), 1)
    east = jnp.zeros((8, LANES), F32)
    west = jnp.zeros((8, LANES), F32)
    for p in range(PLANES):
        rows = slice(8 * (p % 7), 8 * (p % 7) + 8)
        here = (lane >= 4 * p) & (lane < 4 * p + 4)
        w, e = (
            halo_tile(jnp.where(even_row, a, b), jnp.where(even_row, b, a), p)
            for a, b in (
                (row_a[rows, i : i + LANES], row_b[rows, i : i + LANES]) for i in (0, 640)
            )
        )
        east = jnp.where(here, roll(e, 4 * p + 4, 1), east)
        west = jnp.where(here, roll(w, 4 * p, 1), west)
    e_own, w_own = col_e[...], col_w[...]
    col_a[0:48] = jnp.where(even, e_own, w_own)
    col_b[0:48] = jnp.where(even, w_own, e_own)
    col_a[48:56] = jnp.where(even, east, west)
    col_b[48:56] = jnp.where(even, west, east)


HT = 56
STRIP = 72
STRIPS = 7
T0, U0, V0 = 0, 3, 6
XE, XW, YN, YS = 9, 12, 15, 18
E0, P0, Q0, DEPTH, WETS, QUARTER, DP, DQ, GX, GY = range(21, 31)
FIELDS = 31


def pack_tiles(r):
    lane = iota(r[0].shape, 1)
    t0 = jnp.where(lane < 48, r[0], jnp.where(lane < 96, r[1], r[2]))
    t1 = jnp.where(
        lane < 16, r[2], jnp.where(lane < 64, r[3], jnp.where(lane < 112, r[4], r[5]))
    )
    t2 = jnp.where(lane < 32, r[5], jnp.where(lane < 80, r[6], r[7]))
    return t0, t1, t2


class Step:
    def __init__(self, ext, res):
        self.ext, self.res = ext, res
        self.gx, self.gy = lax.axis_index("gx"), lax.axis_index("gy")

    def put(self, field, t, x, first=8):
        self.ext[field, t, first : first + x.shape[0]] = x

    def mid(self, field, t, first=8, rows=HT):
        return self.ext[field, t, first : first + rows]

    def right(self, field, t, x, k=1, first=8):
        after = t if isinstance(t, int) and t in (5, 6) else t + 1
        lane = iota(x.shape, 1)
        y = self.mid(field, after, first, x.shape[0])
        return roll(jnp.where(lane < k, y, x), -k, 1)

    def left(self, field, t, x, k=1, first=8):
        before = t if isinstance(t, int) and t in (0, 6) else t - 1
        lane = iota(x.shape, 1)
        y = self.mid(field, before, first, x.shape[0])
        return roll(jnp.where(lane >= LANES - k, y, x), k, 1)

    def place(self, t, planes, part):
        def put(field, x, ring=False):
            if part == "halo":
                self.put(field, t, x, 56)
                if ring:
                    self.put(field, t, x, 0)
            else:
                self.put(field, t, x)
                if ring:
                    self.put(field, t, x[0:8], 64)
                    if part == "all":
                        self.put(field, t, x[48:56], 0)

        wet = planes(WET)
        put(WETS, wet)
        put(QUARTER, 0.25 * wet)
        sums = []
        for q in range(3):
            heat = planes(q) * wet
            put(T0 + q, heat, ring=True)
            b = heat - 0.1 * heat * heat
            sums.append(sums[-1] + b if sums else b)
        mean = (sums[0] + sums[1] + sums[2]) * (1.0 / 3.0)
        for q in range(3):
            push = 0.15 * (sums[q] - mean)
            u, v = planes(3 + q) * wet, planes(6 + q) * wet
            put(U0 + q, u, ring=True)
            put(V0 + q, v)
            u, v = 0.1 * u, 0.1 * v
            put(XE + q, u - push)
            put(XW + q, u + push)
            put(YN + q, v - push, ring=True)
            put(YS + q, v + push, ring=True)
        put(E0, planes(9) * wet)
        east, north = planes(10) * wet, planes(11) * wet
        depth = 0.25 * planes(12)
        put(P0, east)
        put(Q0, north)
        put(DEPTH, depth)
        put(DP, depth * east)
        put(DQ, depth * north, ring=True)

    def tracer(self, t, first, rows):
        mid = functools.partial(self.mid, t=t, rows=rows)
        wet = mid(WETS, first=first)
        for q in range(3):
            f = T0 + q
            x = mid(f, first=first)
            xe, xw = self.right(f, t, x, 1, first), self.left(f, t, x, 1, first)
            xee, xww = self.right(f, t, x, 2, first), self.left(f, t, x, 2, first)
            xn, xs = mid(f, first=first + 1), mid(f, first=first - 1)
            xnn, xss = mid(f, first=first + 2), mid(f, first=first - 2)
            dx = (3.2 / 12.0) * (xw - xe) + (0.4 / 12.0) * (xee - xww)
            dy = (3.2 / 12.0) * (xs - xn) + (0.4 / 12.0) * (xnn - xss)
            ring = 0.1 * ((xe + xw) + (xn + xs))
            u, v = mid(U0 + q, first=first), mid(V0 + q, first=first)
            new = 0.6 * x + ring + (u * dx + v * dy)
            self.res[t, 48 * q + first - 8 : 48 * q + first - 8 + rows] = wet * new

    def motion(self, t, first, rows):
        row = iota((rows, LANES), 0) + (first - 8)
        north = self.gx * BLOCK + row - jnp.where(row >= 52, HT, 0)
        turn = 0.15 * (2.0 * (north.astype(F32) + 0.5) / LAT - 1.0)
        mid = functools.partial(self.mid, t=t, rows=rows)
        wet = mid(WETS, first=first)
        kept = min(rows, 56 - first)
        gain_x = gain_y = None
        for q in range(3):
            u, v = mid(U0 + q, first=first), mid(V0 + q, first=first)
            xe, xw = mid(XE + q, first=first), mid(XW + q, first=first)
            side_x = self.right(XE + q, t, xe, 1, first) + self.left(XW + q, t, xw, 1, first)
            side_y = mid(YN + q, first=first + 1) + mid(YS + q, first=first - 1)
            ring_u = 0.1 * (mid(U0 + q, first=first + 1) + mid(U0 + q, first=first - 1))
            ring_v = 0.1 * (
                self.right(V0 + q, t, v, 1, first) + self.left(V0 + q, t, v, 1, first)
            )
            new_u = wet * ((0.6 * u + turn * v) + (side_x + ring_u))
            new_v = wet * ((0.6 * v - turn * u) + (side_y + ring_v))
            spot = 144 + 48 * q + first - 8
            self.res[t, spot : spot + kept] = new_u[:kept]
            self.res[t, spot + 144 : spot + 144 + kept] = new_v[:kept]
            du, dv = new_u - u, new_v - v
            gain_x = du if gain_x is None else gain_x + du
            gain_y = dv if gain_y is None else gain_y + dv
        self.put(GX, t, gain_x * (1.0 / 3.0), first)
        self.put(GY, t, gain_y * (1.0 / 3.0), first)

    def passes(self, strips):
        mid, put = self.mid, self.put
        for last in (False, True):
            for t in strips:
                flux = mid(DP, t)
                div = (self.right(DP, t, flux) - self.left(DP, t, flux)) + (
                    mid(DQ, t, 9) - mid(DQ, t, 7)
                )
                new = mid(E0, t) - mid(WETS, t) * div
                put(E0, t, new)
                put(E0, t, new[48:56], 0)
                put(E0, t, new[0:8], 64)
                if last:
                    self.res[t, 432:480] = new[:48]
            for t in strips:
                e, quarter = mid(E0, t), mid(QUARTER, t)
                ex = self.right(E0, t, e) - self.left(E0, t, e)
                ey = mid(E0, t, 9) - mid(E0, t, 7)
                new_p = (mid(P0, t) + mid(GX, t)) - quarter * ex
                new_q = (mid(Q0, t) + mid(GY, t)) - quarter * ey
                if last:
                    self.res[t, 480:528] = new_p[:48]
                    self.res[t, 528:576] = new_q[:48]
                else:
                    cross = mid(DEPTH, t) * new_q
                    put(P0, t, new_p)
                    put(Q0, t, new_q)
                    put(DP, t, mid(DEPTH, t) * new_p)
                    put(DQ, t, cross)
                    put(DQ, t, cross[48:56], 0)
                    put(DQ, t, cross[0:8], 64)


def cut_pieces(rounds, idx, res, send):
    spots = []
    for c in range(8 * rounds):
        off = 48 * idx[3, c]
        inner = off & 127
        spots.append((off >> 7, inner, (48 * c + 256 - inner) & 127))

    def cut(q):
        pair = 2 * q
        for h in range(rounds):
            done = []
            for start, n in ((64 * q, 64), (512 + 8 * q, 8)):
                rows = pl.ds(start, n) if isinstance(q, int) else pl.ds(pl.multiple_of(start, 8), n)
                lanes = iota((n, LANES), 1)
                moved = []
                for tile, inner, shift in spots[8 * h : 8 * h + 8]:
                    x = jnp.where(lanes >= inner, res[tile, rows], res[tile + 1, rows])
                    moved.append(pltpu.roll(x, shift, 1))
                done.append(pack_tiles(moved))
            mains, rests = done
            for i in range(3):
                base = PIECE * h + 36 * i
                send[pair, base + 32 : base + 40] = rests[i]
                send[pair + 1, base + 28 : base + 36] = rests[i]
            for i in range(3):
                base = PIECE * h + 36 * i
                send[pair, base : base + 32] = mains[i][:32]
                send[pair + 1, base : base + 32] = mains[i][32:]

    if rounds == 1:
        for q in range(8):
            cut(q)
    else:
        pl.loop(0, 8)(cut)


def interior_kernel(*refs):
    tab = refs[0]
    far, (ext, res, idx, most, edge) = refs[2:10], refs[10:15]
    raw, sem = refs[15:23], refs[23]
    copies = [pltpu.make_async_copy(x, y, sem.at[i]) for i, (x, y) in enumerate(zip(far, raw))]
    for copy in copies:
        copy.start()
    place_tables(tab, idx, most)
    for copy in copies:
        copy.wait()
    step = Step(ext, res)

    @pl.loop(0, 6)
    def fill(t):
        lanes = pl.ds(pl.multiple_of(t * LANES, LANES), LANES)
        step.place(t, lambda p: read_plane(raw, p, slice(None), lanes), "own")

    lane = iota((BLOCK, LANES), 1)
    for p in range(PLANES):
        east = read_plane(raw, p, slice(None), slice(640, 768))
        west = read_plane(raw, p, slice(None), slice(0, 128))
        edge[p, 0:48] = jnp.where(lane < 64, roll(east, 60, 1), roll(west, 68, 1))

    @pl.loop(1, 5)
    def inner(t):
        step.tracer(t, 16, 32)
        step.motion(t, 16, 32)


def middle_kernel(row_a, row_b, ext_in, res_in, edge_in, ext, res, edge):
    step = Step(ext, res)
    even_row = step.gx % 2 == 0
    lane = iota((8, LANES), 1)
    for t in range(6):
        lanes = slice(LANES * t, LANES * t + LANES)

        def planes(p, t=t, lanes=lanes):
            rows = slice(8 * (p % 7), 8 * (p % 7) + 8)
            a, b = row_a[rows, lanes], row_b[rows, lanes]
            x = halo_tile(jnp.where(even_row, a, b), jnp.where(even_row, b, a), p)
            if t == 0:
                edge[p, 48:56] = roll(x, 68, 1)
            if t == 5:
                edge[p, 48:56] = jnp.where(lane < 64, roll(x, 60, 1), edge[p, 48:56])
            return x

        step.place(t, planes, "halo")

    @pl.loop(1, 5)
    def rims(t):
        step.tracer(t, 8, 8)
        step.tracer(t, 48, 8)
        step.motion(t, 8, 8)
        step.motion(t, 48, 16)

    for t in (0, 5):
        step.tracer(t, 8, 48)
        step.motion(t, 8, 56)
    step.passes(range(6))


def finish_kernel(col_a, col_b, idx, edge, ext_in, res_in, ext, res, send, table, sem):
    copy = pltpu.make_async_copy(idx, table, sem)
    copy.start()
    step = Step(ext, res)
    even = step.gy % 2 == 0
    a, b = col_a[...], col_b[...]
    from_east, from_west = jnp.where(even, a, b), jnp.where(even, b, a)
    lane = iota((HT, LANES), 1)

    def planes(p):
        near = jnp.where(lane < 64, roll(from_east, 60 - 4 * p, 1), roll(from_west, 64 - 4 * p, 1))
        return jnp.where((lane >= 60) & (lane < 68), near, edge[p])

    step.place(6, planes, "all")
    step.tracer(6, 8, 48)
    step.motion(6, 8, 56)
    step.passes((6,))
    lane = iota((BLOCK, LANES), 1)
    for r in range(0, 576, BLOCK):
        rows = slice(r, r + BLOCK)
        x = res[6, rows]
        res[0, rows] = jnp.where(lane < 4, roll(x, 60, 1), res[0, rows])
        res[5, rows] = jnp.where(lane >= 124, roll(x, 68, 1), res[5, rows])
    copy.wait()
    cut_pieces(1, table, res, send)


def cut_kernel(idx, res, send):
    cut_pieces(2, idx, res, send)


def route_kernel(rounds, idx, got, send):
    lane = iota((36, LANES), 1)

    @pl.loop(0, 2)
    def targets(part):
        for j in range(8):
            d = part * 8 + j
            moved = []
            for s in range(SLOTS):
                slot = d * SLOTS + s
                first, after, inner = idx[0, slot], idx[1, slot], idx[2, slot]
                if rounds > 1:
                    first, after = (
                        x + PIECE * (x // PIECE) + PIECE * idx[6, slot] for x in (first, after)
                    )
                near = got[pl.ds(first, 36), :]
                far = got[pl.ds(after, 36), :]
                x = jnp.where(lane >= inner, near, far)
                moved.append(pltpu.roll(x, (48 * s + 256 - inner) & 127, 1))
            for i, x in enumerate(pack_tiles(moved)):
                send[d, 36 * i : 36 * i + 36] = x


def settle_kernel(idx, got, heat, zonal, merid, height, east, north):
    used = jnp.broadcast_to(idx[5:6, :], (8, LANES))
    lane = iota((8, LANES), 1)
    low = iota((8, LANES), 0) < 4
    outs = (heat, zonal, merid, height, east, north)

    def put(tile_row, i, x):
        x = jnp.where(lane + LANES * i < used, x, 0.0)
        plane, rows = tile_row // 6, slice(8 * (tile_row % 6), 8 * (tile_row % 6) + 8)
        lanes = slice(LANES * i, LANES * i + LANES)
        if plane < 9:
            outs[plane // 3][plane % 3, rows, lanes] = x
        else:
            outs[plane - 6][rows, lanes] = x

    for i in range(3):
        for k in range(ROW_DEVICES):
            for t in range(4):
                put(4 * k + t, i, got[k, 36 * i + 8 * t : 36 * i + 8 * t + 8, :])
        for q in range(8):
            a = got[2 * q, 36 * i + 32 : 36 * i + 40, :]
            b = got[2 * q + 1, 36 * i + 28 : 36 * i + 36, :]
            put(64 + q, i, jnp.where(low, a, b))


def f32(*shape):
    return jax.ShapeDtypeStruct(shape, F32)


def cost(us):
    return pl.CostEstimate(flops=us * 1_000_000, bytes_accessed=us * 2_000_000, transcendentals=0)


VM = pl.BlockSpec(memory_space=pltpu.VMEM)
SM = pl.BlockSpec(memory_space=pltpu.SMEM)


def shards(heat, zonal, merid, height, east, north, depth, marine, sequence):
    raw = (heat, zonal, merid, height, east, north, depth, marine)
    tab = sequence.reshape(GRID_ROWS, LANES)

    def call(kernel, name, operands, ins, outs, shapes, mega=8, us=0, **more):
        more = {"in_specs": ins, "out_specs": outs, **more}
        return pl.pallas_call(
            kernel,
            out_shape=shapes,
            compiler_params=pltpu.CompilerParams(vmem_limit_bytes=mega << 20 if mega < 64 else 67_043_328),
            cost_estimate=cost(us) if us else None,
            name=name,
            **more,
        )(*operands)

    def part(x, height, width):
        return pltpu.VMEM(x.shape[:-2] + (height, width), x.dtype)

    scratch = [part(x, 8, 768) for _ in range(2) for x in raw]
    scratch += [part(x, BLOCK, LANES) for _ in range(2) for x in raw]
    far = tuple(pltpu.with_memory_space_constraint(x, pltpu.HBM) for x in raw)
    hbm = [pl.BlockSpec(memory_space=pltpu.HBM)] * 8
    row_a, row_b, col_e, col_w = call(
        edge_kernel,
        "edges",
        far,
        hbm,
        (VM,) * 4,
        (f32(56, 768), f32(56, 768), f32(48, 128), f32(48, 128)),
        mega=4,
        scratch_shapes=scratch + [pltpu.SemaphoreType.DMA((32,))],
    )
    fields = (f32(FIELDS, STRIPS, STRIP, LANES), f32(STRIPS, 576, LANES))
    ints = jax.ShapeDtypeStruct((8, LANES), I32), jax.ShapeDtypeStruct((1, 1), I32)
    rim = f32(PLANES, HT, LANES)
    ext, res, idx, most, edge = call(
        interior_kernel,
        "interior",
        (tab, col_e) + far,
        [VM, VM] + hbm,
        (VM,) * 5,
        fields + ints + (rim,),
        mega=12,
        us=3,
        scratch_shapes=[pltpu.VMEM(x.shape, x.dtype) for x in raw]
        + [pltpu.SemaphoreType.DMA((8,))],
    )
    full = (most > 8).astype(I32)

    def swaps(axis, size, first, second):
        near = [(i, i ^ 1) for i in range(size)]
        far = [(i, i + 1) for i in range(1, size - 1, 2)]
        far += [(j, i) for i, j in far]
        second = lax.ppermute(second, axis, far)
        return lax.ppermute(first, axis, near), second

    row_a, row_b = swaps("gx", GRID_ROWS, row_a, row_b)
    col_a, col_b = call(
        column_kernel,
        "columns",
        (row_a, row_b, col_e, col_w, full),
        [VM] * 5,
        (VM, VM),
        (f32(56, 128), f32(56, 128)),
        mega=4,
    )
    ext, res, edge = call(
        middle_kernel,
        "middle",
        (row_a, row_b, ext, res, edge),
        [VM] * 5,
        (VM,) * 3,
        fields + (rim,),
        us=3,
        input_output_aliases={2: 0, 3: 1, 4: 2},
    )
    col_a, col_b = swaps("gy", ROW_DEVICES, col_a, col_b)
    _, res, send = call(
        finish_kernel,
        "finish",
        (col_a, col_b, idx, edge, ext, res),
        [VM] * 6,
        (VM,) * 3,
        fields + (f32(ROW_DEVICES, PIECE, LANES),),
        us=2,
        input_output_aliases={4: 0, 5: 1},
        scratch_shapes=[pltpu.SMEM((8, LANES), I32), pltpu.SemaphoreType.DMA],
    )

    def deliver(rounds, send):
        got = lax.all_to_all(send, "gy", 0, 0, tiled=True)
        got = got.reshape(ROW_DEVICES * rounds * PIECE, LANES)
        piece = f32(ROW_DEVICES, PIECE, LANES)
        send = call(
            functools.partial(route_kernel, rounds), "route", (idx, got), [SM, VM], VM, piece
        )
        got = lax.all_to_all(send, "gy", 0, 0, tiled=True)
        shapes = (f32(3, 48, 384),) * 3 + (f32(48, 384),) * 3
        return call(settle_kernel, "settle", (idx, got), [VM, VM], (VM,) * 6, shapes)

    def crowded():
        both = f32(ROW_DEVICES, 2 * PIECE, LANES)
        return deliver(2, call(cut_kernel, "cut", (idx, res), [SM, VM], VM, both))

    return lax.cond(full[0, 0] > 0, crowded, lambda: deliver(1, send))


def solution(mesh):
    level, flat = P(None, "gx", "gy"), P("gx", "gy")
    return jax.shard_map(
        shards,
        mesh=mesh,
        in_specs=(level,) * 3 + (flat,) * 5 + (P(),),
        out_specs=(P(None, None, ("gx", "gy")),) * 3 + (P(None, ("gx", "gy")),) * 3,
        check_vma=False,
    )
```

```python
import functools

import jax
import jax.numpy as jnp
from jax import lax
from jax.experimental import pallas as pl
from jax.experimental.pallas import tpu as pltpu
from jax.sharding import PartitionSpec as P

BLOCK = 48
SLOTS = 8
ROW_DEVICES = 16
GRID_ROWS = 8
LAT = 384
PLANES = 14
WET = 13
LANES = 128
PIECE = 112

F32 = jnp.float32
I32 = jnp.int32


def iota(shape, dim):
    return lax.broadcasted_iota(I32, shape, dim)


def roll(x, shift, axis):
    return pltpu.roll(x, shift % x.shape[axis], axis)


def plane_of(refs, p):
    if p < 9:
        return refs[p // 3], (p % 3,)
    return refs[3 + p - 9], ()


def read_plane(refs, p, rows, lanes):
    ref, lead = plane_of(refs, p)
    x = ref[lead + (rows, lanes)]
    return x.astype(F32) if p == WET else x


def halo_tile(north, south, p):
    low = iota(north.shape, 0) < 4
    if p < 7:
        return jnp.where(low, north, roll(south, 4, 0))
    return jnp.where(low, roll(north, 4, 0), south)


def edge_kernel(*refs):
    raw = refs[:8]
    row_a, row_b = refs[8:10]
    parts, sem = refs[10:26], refs[26]
    copies = []
    for i, rows in enumerate((slice(0, 8), slice(40, 48))):
        for j, x in enumerate(raw):
            where = (slice(None),) * (len(x.shape) - 2) + (rows, slice(None))
            n = 8 * i + j
            copies.append(pltpu.make_async_copy(x.at[where], parts[n], sem.at[n]))
            copies[-1].start()
    for copy in copies:
        copy.wait()
    bottoms, tops = parts[:8], parts[8:]
    even = lax.axis_index("gx") % 2 == 0
    low = iota((8, 768), 0) < 4
    full = slice(None)
    for m in range(7):
        t0, t1 = (read_plane(tops, q, full, full) for q in (m, m + 7))
        b0, b1 = (read_plane(bottoms, q, full, full) for q in (m, m + 7))
        top = jnp.where(low, roll(t0, 4, 0), t1)
        bottom = jnp.where(low, b0, roll(b1, 4, 0))
        row_a[8 * m : 8 * m + 8] = jnp.where(even, top, bottom)
        row_b[8 * m : 8 * m + 8] = jnp.where(even, bottom, top)


def place_tables(tab_ref, idx, full):
    gx, gy = lax.axis_index("gx"), lax.axis_index("gy")
    square = (LANES, LANES)
    g = tab_ref[pl.ds(gx, 1), :].astype(F32)
    g_lane = jnp.broadcast_to(g, square)
    diagonal = iota(square, 0) == iota(square, 1)
    g_sub = jnp.sum(jnp.where(diagonal, g_lane, 0.0), axis=1, keepdims=True)
    g_sub = jnp.broadcast_to(g_sub, square)
    d_lane = jnp.floor(g_lane * (1.0 / 16.0))
    d_sub = jnp.floor(g_sub * (1.0 / 16.0))
    same = d_lane == d_sub
    rank_lane = jnp.sum(jnp.where(same & (g_sub < g_lane), 1.0, 0.0), axis=0, keepdims=True)
    rank_sub = jnp.sum(jnp.where(same & (g_lane < g_sub), 1.0, 0.0), axis=1, keepdims=True)
    first = (gx * ROW_DEVICES).astype(F32)
    source = jnp.floor(g * (1.0 / 16.0)) - first
    listed = g >= 0.0
    half = jnp.where(rank_lane >= 8.0, 1.0, 0.0)
    half = jnp.where(listed, half, 0.0)
    place = jnp.where(listed, source, 0.0)
    off = jnp.where(listed, 48.0 * (rank_lane - 8.0 * half), 0.0)
    tile = jnp.floor(off * (1.0 / LANES))
    own = (iota((1, LANES), 1) // SLOTS == gy) & listed
    used = jnp.sum(jnp.where(own, float(BLOCK), 0.0), axis=1, keepdims=True)
    used = jnp.broadcast_to(used, (1, LANES))
    me = (gx * ROW_DEVICES + gy).astype(F32)
    c_lane = iota(square, 1).astype(F32)
    mine = (d_sub == me) & (jnp.broadcast_to(rank_sub, square) == c_lane)
    order = jnp.sum(jnp.where(mine, g_sub - d_sub * 16.0, 0.0), axis=0, keepdims=True)
    count = jnp.zeros(square, F32)
    for r in range(GRID_ROWS):
        owner = jnp.floor(tab_ref[r : r + 1, :].astype(F32) * (1.0 / 16.0))
        count += jnp.where(jnp.broadcast_to(owner, square) == iota(square, 0).astype(F32), 1.0, 0.0)
    most = jnp.max(jnp.sum(count, axis=1, keepdims=True), axis=0, keepdims=True)
    most = jnp.broadcast_to(most, (1, LANES))
    sub = iota((8, LANES), 0)
    table = jnp.where(sub == 3, order, most)
    table = jnp.where(sub == 0, place * PIECE + 36.0 * tile, table)
    table = jnp.where(sub == 1, place * PIECE + 36.0 * jnp.minimum(tile + 1.0, 2.0), table)
    table = jnp.where(sub == 2, off - LANES * tile, table)
    table = jnp.where(sub == 5, used, table)
    table = jnp.where(sub == 6, half, table)
    idx[...] = table.astype(I32)
    full[...] = most[:, :1].astype(I32)


def column_kernel(row_a, row_b, col_e, col_w, col_a, col_b):
    gx, gy = lax.axis_index("gx"), lax.axis_index("gy")
    even_row, even = gx % 2 == 0, gy % 2 == 0
    lane = iota((8, LANES), 1)
    east = jnp.zeros((8, LANES), F32)
    west = jnp.zeros((8, LANES), F32)
    for p in range(PLANES):
        rows = slice(8 * (p % 7), 8 * (p % 7) + 8)
        here = (lane >= 4 * p) & (lane < 4 * p + 4)
        w, e = (
            halo_tile(jnp.where(even_row, a, b), jnp.where(even_row, b, a), p)
            for a, b in (
                (row_a[rows, i : i + LANES], row_b[rows, i : i + LANES]) for i in (0, 640)
            )
        )
        east = jnp.where(here, roll(e, 4 * p + 4, 1), east)
        west = jnp.where(here, roll(w, 4 * p, 1), west)
    e_own, w_own = col_e[...], col_w[...]
    col_a[0:48] = jnp.where(even, e_own, w_own)
    col_b[0:48] = jnp.where(even, w_own, e_own)
    col_a[48:56] = jnp.where(even, east, west)
    col_b[48:56] = jnp.where(even, west, east)


HT = 56
STRIP = 72
STRIPS = 7
T0, U0, V0 = 0, 3, 6
XE, XW, YN, YS = 9, 12, 15, 18
E0, P0, Q0, DEPTH, WETS, QUARTER, DP, DQ, GX, GY = range(21, 31)
FIELDS = 31


def pack_tiles(r):
    lane = iota(r[0].shape, 1)
    t0 = jnp.where(lane < 48, r[0], jnp.where(lane < 96, r[1], r[2]))
    t1 = jnp.where(
        lane < 16, r[2], jnp.where(lane < 64, r[3], jnp.where(lane < 112, r[4], r[5]))
    )
    t2 = jnp.where(lane < 32, r[5], jnp.where(lane < 80, r[6], r[7]))
    return t0, t1, t2


class Step:
    def __init__(self, ext, res):
        self.ext, self.res = ext, res
        self.gx, self.gy = lax.axis_index("gx"), lax.axis_index("gy")

    def put(self, field, t, x, first=8):
        self.ext[field, t, first : first + x.shape[0]] = x

    def mid(self, field, t, first=8, rows=HT):
        return self.ext[field, t, first : first + rows]

    def right(self, field, t, x, k=1, first=8):
        after = t if isinstance(t, int) and t in (5, 6) else t + 1
        lane = iota(x.shape, 1)
        y = self.mid(field, after, first, x.shape[0])
        return roll(jnp.where(lane < k, y, x), -k, 1)

    def left(self, field, t, x, k=1, first=8):
        before = t if isinstance(t, int) and t in (0, 6) else t - 1
        lane = iota(x.shape, 1)
        y = self.mid(field, before, first, x.shape[0])
        return roll(jnp.where(lane >= LANES - k, y, x), k, 1)

    def place(self, t, planes, part):
        def put(field, x, ring=False):
            if part == "halo":
                self.put(field, t, x, 56)
                if ring:
                    self.put(field, t, x, 0)
            else:
                self.put(field, t, x)
                if ring:
                    self.put(field, t, x[0:8], 64)
                    if part == "all":
                        self.put(field, t, x[48:56], 0)

        wet = planes(WET)
        put(WETS, wet)
        put(QUARTER, 0.25 * wet)
        sums = []
        for q in range(3):
            heat = planes(q) * wet
            put(T0 + q, heat, ring=True)
            b = heat - 0.1 * heat * heat
            sums.append(sums[-1] + b if sums else b)
        mean = (sums[0] + sums[1] + sums[2]) * (1.0 / 3.0)
        for q in range(3):
            push = 0.15 * (sums[q] - mean)
            u, v = planes(3 + q) * wet, planes(6 + q) * wet
            put(U0 + q, u, ring=True)
            put(V0 + q, v)
            u, v = 0.1 * u, 0.1 * v
            put(XE + q, u - push)
            put(XW + q, u + push)
            put(YN + q, v - push, ring=True)
            put(YS + q, v + push, ring=True)
        put(E0, planes(9) * wet)
        east, north = planes(10) * wet, planes(11) * wet
        depth = 0.25 * planes(12)
        put(P0, east)
        put(Q0, north)
        put(DEPTH, depth)
        put(DP, depth * east)
        put(DQ, depth * north, ring=True)

    def tracer(self, t, first, rows):
        mid = functools.partial(self.mid, t=t, rows=rows)
        wet = mid(WETS, first=first)
        for q in range(3):
            f = T0 + q
            x = mid(f, first=first)
            xe, xw = self.right(f, t, x, 1, first), self.left(f, t, x, 1, first)
            xee, xww = self.right(f, t, x, 2, first), self.left(f, t, x, 2, first)
            xn, xs = mid(f, first=first + 1), mid(f, first=first - 1)
            xnn, xss = mid(f, first=first + 2), mid(f, first=first - 2)
            dx = (3.2 / 12.0) * (xw - xe) + (0.4 / 12.0) * (xee - xww)
            dy = (3.2 / 12.0) * (xs - xn) + (0.4 / 12.0) * (xnn - xss)
            ring = 0.1 * ((xe + xw) + (xn + xs))
            u, v = mid(U0 + q, first=first), mid(V0 + q, first=first)
            new = 0.6 * x + ring + (u * dx + v * dy)
            self.res[t, 48 * q + first - 8 : 48 * q + first - 8 + rows] = wet * new

    def motion(self, t, first, rows):
        row = iota((rows, LANES), 0) + (first - 8)
        north = self.gx * BLOCK + row - jnp.where(row >= 52, HT, 0)
        turn = 0.15 * (2.0 * (north.astype(F32) + 0.5) / LAT - 1.0)
        mid = functools.partial(self.mid, t=t, rows=rows)
        wet = mid(WETS, first=first)
        kept = min(rows, 56 - first)
        gain_x = gain_y = None
        for q in range(3):
            u, v = mid(U0 + q, first=first), mid(V0 + q, first=first)
            xe, xw = mid(XE + q, first=first), mid(XW + q, first=first)
            side_x = self.right(XE + q, t, xe, 1, first) + self.left(XW + q, t, xw, 1, first)
            side_y = mid(YN + q, first=first + 1) + mid(YS + q, first=first - 1)
            ring_u = 0.1 * (mid(U0 + q, first=first + 1) + mid(U0 + q, first=first - 1))
            ring_v = 0.1 * (
                self.right(V0 + q, t, v, 1, first) + self.left(V0 + q, t, v, 1, first)
            )
            new_u = wet * ((0.6 * u + turn * v) + (side_x + ring_u))
            new_v = wet * ((0.6 * v - turn * u) + (side_y + ring_v))
            spot = 144 + 48 * q + first - 8
            self.res[t, spot : spot + kept] = new_u[:kept]
            self.res[t, spot + 144 : spot + 144 + kept] = new_v[:kept]
            du, dv = new_u - u, new_v - v
            gain_x = du if gain_x is None else gain_x + du
            gain_y = dv if gain_y is None else gain_y + dv
        self.put(GX, t, gain_x * (1.0 / 3.0), first)
        self.put(GY, t, gain_y * (1.0 / 3.0), first)

    def passes(self, strips):
        mid, put = self.mid, self.put
        for last in (False, True):
            for t in strips:
                flux = mid(DP, t)
                div = (self.right(DP, t, flux) - self.left(DP, t, flux)) + (
                    mid(DQ, t, 9) - mid(DQ, t, 7)
                )
                new = mid(E0, t) - mid(WETS, t) * div
                put(E0, t, new)
                put(E0, t, new[48:56], 0)
                put(E0, t, new[0:8], 64)
                if last:
                    self.res[t, 432:480] = new[:48]
            for t in strips:
                e, quarter = mid(E0, t), mid(QUARTER, t)
                ex = self.right(E0, t, e) - self.left(E0, t, e)
                ey = mid(E0, t, 9) - mid(E0, t, 7)
                new_p = (mid(P0, t) + mid(GX, t)) - quarter * ex
                new_q = (mid(Q0, t) + mid(GY, t)) - quarter * ey
                if last:
                    self.res[t, 480:528] = new_p[:48]
                    self.res[t, 528:576] = new_q[:48]
                else:
                    cross = mid(DEPTH, t) * new_q
                    put(P0, t, new_p)
                    put(Q0, t, new_q)
                    put(DP, t, mid(DEPTH, t) * new_p)
                    put(DQ, t, cross)
                    put(DQ, t, cross[48:56], 0)
                    put(DQ, t, cross[0:8], 64)


def cut_pieces(rounds, idx, res, send):
    spots = []
    for c in range(8 * rounds):
        off = 48 * idx[3, c]
        inner = off & 127
        spots.append((off >> 7, inner, (48 * c + 256 - inner) & 127))

    def cut(q):
        pair = 2 * q
        for h in range(rounds):
            done = []
            for start, n in ((64 * q, 64), (512 + 8 * q, 8)):
                rows = pl.ds(start, n) if isinstance(q, int) else pl.ds(pl.multiple_of(start, 8), n)
                lanes = iota((n, LANES), 1)
                moved = []
                for tile, inner, shift in spots[8 * h : 8 * h + 8]:
                    x = jnp.where(lanes >= inner, res[tile, rows], res[tile + 1, rows])
                    moved.append(pltpu.roll(x, shift, 1))
                done.append(pack_tiles(moved))
            mains, rests = done
            for i in range(3):
                base = PIECE * h + 36 * i
                send[pair, base + 32 : base + 40] = rests[i]
                send[pair + 1, base + 28 : base + 36] = rests[i]
            for i in range(3):
                base = PIECE * h + 36 * i
                send[pair, base : base + 32] = mains[i][:32]
                send[pair + 1, base : base + 32] = mains[i][32:]

    if rounds == 1:
        for q in range(8):
            cut(q)
    else:
        pl.loop(0, 8)(cut)


def interior_kernel(*refs):
    tab, raw = refs[0], refs[2:10]
    ext, res, idx, most, edge, col_e, col_w = refs[10:]
    place_tables(tab, idx, most)
    step = Step(ext, res)

    @pl.loop(0, 6)
    def fill(t):
        lanes = pl.ds(pl.multiple_of(t * LANES, LANES), LANES)
        step.place(t, lambda p: read_plane(raw, p, slice(None), lanes), "own")

    lane = iota((BLOCK, LANES), 1)
    to_east = to_west = jnp.zeros((BLOCK, LANES), F32)
    for p in range(PLANES):
        here = (lane >= 4 * p) & (lane < 4 * p + 4)
        east = read_plane(raw, p, slice(None), slice(640, 768))
        west = read_plane(raw, p, slice(None), slice(0, 128))
        edge[p, 0:48] = jnp.where(lane < 64, roll(east, 60, 1), roll(west, 68, 1))
        to_east = jnp.where(here, roll(east, 4 * p + 4, 1), to_east)
        to_west = jnp.where(here, roll(west, 4 * p, 1), to_west)
    col_e[...] = to_east
    col_w[...] = to_west

    @pl.loop(1, 5)
    def inner(t):
        step.tracer(t, 16, 32)
        step.motion(t, 16, 32)


def middle_kernel(row_a, row_b, ext_in, res_in, edge_in, ext, res, edge):
    step = Step(ext, res)
    even_row = step.gx % 2 == 0
    lane = iota((8, LANES), 1)
    for t in range(6):
        lanes = slice(LANES * t, LANES * t + LANES)

        def planes(p, t=t, lanes=lanes):
            rows = slice(8 * (p % 7), 8 * (p % 7) + 8)
            a, b = row_a[rows, lanes], row_b[rows, lanes]
            x = halo_tile(jnp.where(even_row, a, b), jnp.where(even_row, b, a), p)
            if t == 0:
                edge[p, 48:56] = roll(x, 68, 1)
            if t == 5:
                edge[p, 48:56] = jnp.where(lane < 64, roll(x, 60, 1), edge[p, 48:56])
            return x

        step.place(t, planes, "halo")

    @pl.loop(1, 5)
    def rims(t):
        step.tracer(t, 8, 8)
        step.tracer(t, 48, 8)
        step.motion(t, 8, 8)
        step.motion(t, 48, 16)

    for t in (0, 5):
        step.tracer(t, 8, 48)
        step.motion(t, 8, 56)
    step.passes(range(6))


def finish_kernel(col_a, col_b, idx, edge, ext_in, res_in, ext, res, send, table, sem):
    copy = pltpu.make_async_copy(idx, table, sem)
    copy.start()
    step = Step(ext, res)
    even = step.gy % 2 == 0
    a, b = col_a[...], col_b[...]
    from_east, from_west = jnp.where(even, a, b), jnp.where(even, b, a)
    lane = iota((HT, LANES), 1)

    def planes(p):
        near = jnp.where(lane < 64, roll(from_east, 60 - 4 * p, 1), roll(from_west, 64 - 4 * p, 1))
        return jnp.where((lane >= 60) & (lane < 68), near, edge[p])

    step.place(6, planes, "all")
    step.tracer(6, 8, 48)
    step.motion(6, 8, 56)
    step.passes((6,))
    lane = iota((BLOCK, LANES), 1)
    for r in range(0, 576, BLOCK):
        rows = slice(r, r + BLOCK)
        x = res[6, rows]
        res[0, rows] = jnp.where(lane < 4, roll(x, 60, 1), res[0, rows])
        res[5, rows] = jnp.where(lane >= 124, roll(x, 68, 1), res[5, rows])
    copy.wait()
    cut_pieces(1, table, res, send)


def cut_kernel(idx, res, send):
    cut_pieces(2, idx, res, send)


def route_kernel(rounds, idx, got, send):
    lane = iota((36, LANES), 1)

    @pl.loop(0, 2)
    def targets(part):
        for j in range(8):
            d = part * 8 + j
            moved = []
            for s in range(SLOTS):
                slot = d * SLOTS + s
                first, after, inner = idx[0, slot], idx[1, slot], idx[2, slot]
                if rounds > 1:
                    first, after = (
                        x + PIECE * (x // PIECE) + PIECE * idx[6, slot] for x in (first, after)
                    )
                near = got[pl.ds(first, 36), :]
                far = got[pl.ds(after, 36), :]
                x = jnp.where(lane >= inner, near, far)
                moved.append(pltpu.roll(x, (48 * s + 256 - inner) & 127, 1))
            for i, x in enumerate(pack_tiles(moved)):
                send[d, 36 * i : 36 * i + 36] = x


def settle_kernel(idx, got, heat, zonal, merid, height, east, north):
    used = jnp.broadcast_to(idx[5:6, :], (8, LANES))
    lane = iota((8, LANES), 1)
    low = iota((8, LANES), 0) < 4
    outs = (heat, zonal, merid, height, east, north)

    def put(tile_row, i, x):
        x = jnp.where(lane + LANES * i < used, x, 0.0)
        plane, rows = tile_row // 6, slice(8 * (tile_row % 6), 8 * (tile_row % 6) + 8)
        lanes = slice(LANES * i, LANES * i + LANES)
        if plane < 9:
            outs[plane // 3][plane % 3, rows, lanes] = x
        else:
            outs[plane - 6][rows, lanes] = x

    for i in range(3):
        for k in range(ROW_DEVICES):
            for t in range(4):
                put(4 * k + t, i, got[k, 36 * i + 8 * t : 36 * i + 8 * t + 8, :])
        for q in range(8):
            a = got[2 * q, 36 * i + 32 : 36 * i + 40, :]
            b = got[2 * q + 1, 36 * i + 28 : 36 * i + 36, :]
            put(64 + q, i, jnp.where(low, a, b))


def f32(*shape):
    return jax.ShapeDtypeStruct(shape, F32)


def cost(us):
    return pl.CostEstimate(flops=us * 1_000_000, bytes_accessed=us * 2_000_000, transcendentals=0)


VM = pl.BlockSpec(memory_space=pltpu.VMEM)
SM = pl.BlockSpec(memory_space=pltpu.SMEM)


def shards(heat, zonal, merid, height, east, north, depth, marine, sequence):
    raw = (heat, zonal, merid, height, east, north, depth, marine)
    tab = sequence.reshape(GRID_ROWS, LANES)

    def call(kernel, operands, ins, outs, shapes, mega=8, us=0, **more):
        more = {"in_specs": ins, "out_specs": outs, **more}
        return pl.pallas_call(
            kernel,
            out_shape=shapes,
            compiler_params=pltpu.CompilerParams(vmem_limit_bytes=mega << 20 if mega < 64 else 67_043_328),
            cost_estimate=cost(us) if us else None,
            **more,
        )(*operands)

    strips = [pltpu.VMEM(x.shape[:-2] + (8, 768), x.dtype) for _ in range(2) for x in raw]
    row_a, row_b = call(
        edge_kernel,
        tuple(pltpu.with_memory_space_constraint(x, pltpu.HBM) for x in raw),
        [pl.BlockSpec(memory_space=pltpu.HBM)] * 8,
        (VM, VM),
        (f32(56, 768), f32(56, 768)),
        mega=4,
        scratch_shapes=strips + [pltpu.SemaphoreType.DMA((16,))],
    )
    fields = (f32(FIELDS, STRIPS, STRIP, LANES), f32(STRIPS, 576, LANES))
    ints = jax.ShapeDtypeStruct((8, LANES), I32), jax.ShapeDtypeStruct((1, 1), I32)
    rim = f32(PLANES, HT, LANES)
    side = f32(BLOCK, LANES)
    ext, res, idx, most, edge, col_e, col_w = call(
        interior_kernel,
        (tab, row_a) + raw,
        [VM] * 10,
        (VM,) * 7,
        fields + ints + (rim, side, side),
        us=3,
    )

    def swaps(axis, size, first, second):
        near = [(i, i ^ 1) for i in range(size)]
        far = [(i, i + 1) for i in range(1, size - 1, 2)]
        far += [(j, i) for i, j in far]
        second = lax.ppermute(second, axis, far)
        first = lax.ppermute(first, axis, near)
        return first, second

    row_a, row_b = swaps("gx", GRID_ROWS, row_a, row_b)
    col_a, col_b = call(
        column_kernel,
        (row_a, row_b, col_e, col_w),
        [VM] * 4,
        (VM, VM),
        (f32(56, 128), f32(56, 128)),
        mega=4,
    )
    ext, res, edge = call(
        middle_kernel,
        (row_a, row_b, ext, res, edge),
        [VM] * 5,
        (VM,) * 3,
        fields + (rim,),
        us=3,
        input_output_aliases={2: 0, 3: 1, 4: 2},
    )
    col_a, col_b = swaps("gy", ROW_DEVICES, col_a, col_b)
    _, res, send = call(
        finish_kernel,
        (col_a, col_b, idx, edge, ext, res),
        [VM] * 6,
        (VM,) * 3,
        fields + (f32(ROW_DEVICES, PIECE, LANES),),
        us=2,
        input_output_aliases={4: 0, 5: 1},
        scratch_shapes=[pltpu.SMEM((8, LANES), I32), pltpu.SemaphoreType.DMA],
    )

    def deliver(rounds, send):
        got = lax.all_to_all(send, "gy", 0, 0, tiled=True)
        got = got.reshape(ROW_DEVICES * rounds * PIECE, LANES)
        piece = f32(ROW_DEVICES, PIECE, LANES)
        send = call(functools.partial(route_kernel, rounds), (idx, got), [SM, VM], VM, piece)
        got = lax.all_to_all(send, "gy", 0, 0, tiled=True)
        shapes = (f32(3, 48, 384),) * 3 + (f32(48, 384),) * 3
        return call(settle_kernel, (idx, got), [VM, VM], (VM,) * 6, shapes)

    def crowded():
        both = f32(ROW_DEVICES, 2 * PIECE, LANES)
        return deliver(2, call(cut_kernel, (idx, res), [SM, VM], VM, both))

    return lax.cond(most[0, 0] > 8, crowded, lambda: deliver(1, send))


def solution(mesh):
    level, flat = P(None, "gx", "gy"), P("gx", "gy")
    return jax.shard_map(
        shards,
        mesh=mesh,
        in_specs=(level,) * 3 + (flat,) * 5 + (P(),),
        out_specs=(P(None, None, ("gx", "gy")),) * 3 + (P(None, ("gx", "gy")),) * 3,
        check_vma=False,
    )
```

```python
import functools

import jax
import jax.numpy as jnp
from jax import lax
from jax.experimental import pallas as pl
from jax.experimental.pallas import tpu as pltpu
from jax.sharding import PartitionSpec as P

BLOCK = 48
SLOTS = 8
ROW_DEVICES = 16
GRID_ROWS = 8
LAT = 384
PLANES = 14
WET = 13
LANES = 128
PIECE = 112

F32 = jnp.float32
I32 = jnp.int32


def iota(shape, dim):
    return lax.broadcasted_iota(I32, shape, dim)


def roll(x, shift, axis):
    return pltpu.roll(x, shift % x.shape[axis], axis)


def plane_of(refs, p):
    if p < 9:
        return refs[p // 3], (p % 3,)
    return refs[3 + p - 9], ()


def read_plane(refs, p, rows, lanes):
    ref, lead = plane_of(refs, p)
    x = ref[lead + (rows, lanes)]
    return x.astype(F32) if p == WET else x


def halo_tile(north, south, p):
    low = iota(north.shape, 0) < 4
    if p < 7:
        return jnp.where(low, north, roll(south, 4, 0))
    return jnp.where(low, roll(north, 4, 0), south)


def edge_kernel(*refs):
    raw = refs[:8]
    row_a, row_b = refs[8:10]
    parts, sem = refs[10:26], refs[26]
    copies = []
    for i, rows in enumerate((slice(0, 8), slice(40, 48))):
        for j, x in enumerate(raw):
            where = (slice(None),) * (len(x.shape) - 2) + (rows, slice(None))
            n = 8 * i + j
            copies.append(pltpu.make_async_copy(x.at[where], parts[n], sem.at[n]))
            copies[-1].start()
    for copy in copies:
        copy.wait()
    bottoms, tops = parts[:8], parts[8:]
    even = lax.axis_index("gx") % 2 == 0
    low = iota((8, 768), 0) < 4
    full = slice(None)
    for m in range(7):
        t0, t1 = (read_plane(tops, q, full, full) for q in (m, m + 7))
        b0, b1 = (read_plane(bottoms, q, full, full) for q in (m, m + 7))
        top = jnp.where(low, roll(t0, 4, 0), t1)
        bottom = jnp.where(low, b0, roll(b1, 4, 0))
        row_a[8 * m : 8 * m + 8] = jnp.where(even, top, bottom)
        row_b[8 * m : 8 * m + 8] = jnp.where(even, bottom, top)


def place_tables(tab_ref, idx, full):
    gx, gy = lax.axis_index("gx"), lax.axis_index("gy")
    square = (LANES, LANES)
    g = tab_ref[pl.ds(gx, 1), :].astype(F32)
    g_lane = jnp.broadcast_to(g, square)
    diagonal = iota(square, 0) == iota(square, 1)
    g_sub = jnp.sum(jnp.where(diagonal, g_lane, 0.0), axis=1, keepdims=True)
    g_sub = jnp.broadcast_to(g_sub, square)
    d_lane = jnp.floor(g_lane * (1.0 / 16.0))
    d_sub = jnp.floor(g_sub * (1.0 / 16.0))
    same = d_lane == d_sub
    rank_lane = jnp.sum(jnp.where(same & (g_sub < g_lane), 1.0, 0.0), axis=0, keepdims=True)
    rank_sub = jnp.sum(jnp.where(same & (g_lane < g_sub), 1.0, 0.0), axis=1, keepdims=True)
    first = (gx * ROW_DEVICES).astype(F32)
    source = jnp.floor(g * (1.0 / 16.0)) - first
    listed = g >= 0.0
    half = jnp.where(rank_lane >= 8.0, 1.0, 0.0)
    half = jnp.where(listed, half, 0.0)
    place = jnp.where(listed, source, 0.0)
    off = jnp.where(listed, 48.0 * (rank_lane - 8.0 * half), 0.0)
    tile = jnp.floor(off * (1.0 / LANES))
    own = (iota((1, LANES), 1) // SLOTS == gy) & listed
    used = jnp.sum(jnp.where(own, float(BLOCK), 0.0), axis=1, keepdims=True)
    used = jnp.broadcast_to(used, (1, LANES))
    me = (gx * ROW_DEVICES + gy).astype(F32)
    c_lane = iota(square, 1).astype(F32)
    mine = (d_sub == me) & (jnp.broadcast_to(rank_sub, square) == c_lane)
    order = jnp.sum(jnp.where(mine, g_sub - d_sub * 16.0, 0.0), axis=0, keepdims=True)
    count = jnp.zeros(square, F32)
    for r in range(GRID_ROWS):
        owner = jnp.floor(tab_ref[r : r + 1, :].astype(F32) * (1.0 / 16.0))
        count += jnp.where(jnp.broadcast_to(owner, square) == iota(square, 0).astype(F32), 1.0, 0.0)
    most = jnp.max(jnp.sum(count, axis=1, keepdims=True), axis=0, keepdims=True)
    most = jnp.broadcast_to(most, (1, LANES))
    sub = iota((8, LANES), 0)
    table = jnp.where(sub == 3, order, most)
    table = jnp.where(sub == 0, place * PIECE + 36.0 * tile, table)
    table = jnp.where(sub == 1, place * PIECE + 36.0 * jnp.minimum(tile + 1.0, 2.0), table)
    table = jnp.where(sub == 2, off - LANES * tile, table)
    table = jnp.where(sub == 5, used, table)
    table = jnp.where(sub == 6, half, table)
    idx[...] = table.astype(I32)
    full[...] = most[:, :1].astype(I32)


def column_kernel(row_a, row_b, col_e, col_w, col_a, col_b):
    gx, gy = lax.axis_index("gx"), lax.axis_index("gy")
    even_row, even = gx % 2 == 0, gy % 2 == 0
    lane = iota((8, LANES), 1)
    east = jnp.zeros((8, LANES), F32)
    west = jnp.zeros((8, LANES), F32)
    for p in range(PLANES):
        rows = slice(8 * (p % 7), 8 * (p % 7) + 8)
        here = (lane >= 4 * p) & (lane < 4 * p + 4)
        w, e = (
            halo_tile(jnp.where(even_row, a, b), jnp.where(even_row, b, a), p)
            for a, b in (
                (row_a[rows, i : i + LANES], row_b[rows, i : i + LANES]) for i in (0, 640)
            )
        )
        east = jnp.where(here, roll(e, 4 * p + 4, 1), east)
        west = jnp.where(here, roll(w, 4 * p, 1), west)
    e_own, w_own = col_e[...], col_w[...]
    col_a[0:48] = jnp.where(even, e_own, w_own)
    col_b[0:48] = jnp.where(even, w_own, e_own)
    col_a[48:56] = jnp.where(even, east, west)
    col_b[48:56] = jnp.where(even, west, east)


HT = 56
STRIP = 72
STRIPS = 7
T0, U0, V0 = 0, 3, 6
XE, XW, YN, YS = 9, 12, 15, 18
E0, P0, Q0, DEPTH, WETS, QUARTER, DP, DQ, GX, GY = range(21, 31)
FIELDS = 31


def pack_tiles(r):
    lane = iota(r[0].shape, 1)
    t0 = jnp.where(lane < 48, r[0], jnp.where(lane < 96, r[1], r[2]))
    t1 = jnp.where(
        lane < 16, r[2], jnp.where(lane < 64, r[3], jnp.where(lane < 112, r[4], r[5]))
    )
    t2 = jnp.where(lane < 32, r[5], jnp.where(lane < 80, r[6], r[7]))
    return t0, t1, t2


class Step:
    def __init__(self, ext, res, first=0):
        self.ext, self.res, self.zero = ext, res, first
        self.gx, self.gy = lax.axis_index("gx"), lax.axis_index("gy")

    def put(self, field, t, x, first=8):
        self.ext[field, t - self.zero, first : first + x.shape[0]] = x

    def mid(self, field, t, first=8, rows=HT):
        return self.ext[field, t - self.zero, first : first + rows]

    def right(self, field, t, x, k=1, first=8):
        after = t if isinstance(t, int) and t in (5, 6) else t + 1
        lane = iota(x.shape, 1)
        y = self.mid(field, after, first, x.shape[0])
        return roll(jnp.where(lane < k, y, x), -k, 1)

    def left(self, field, t, x, k=1, first=8):
        before = t if isinstance(t, int) and t in (0, 6) else t - 1
        lane = iota(x.shape, 1)
        y = self.mid(field, before, first, x.shape[0])
        return roll(jnp.where(lane >= LANES - k, y, x), k, 1)

    def place(self, t, planes, part):
        def put(field, x, ring=False):
            if part == "halo":
                self.put(field, t, x, 56)
                if ring:
                    self.put(field, t, x, 0)
            else:
                self.put(field, t, x)
                if ring:
                    self.put(field, t, x[0:8], 64)
                    if part == "all":
                        self.put(field, t, x[48:56], 0)

        wet = planes(WET)
        put(WETS, wet)
        put(QUARTER, 0.25 * wet)
        sums = []
        for q in range(3):
            heat = planes(q) * wet
            put(T0 + q, heat, ring=True)
            b = heat - 0.1 * heat * heat
            sums.append(sums[-1] + b if sums else b)
        mean = (sums[0] + sums[1] + sums[2]) * (1.0 / 3.0)
        for q in range(3):
            push = 0.15 * (sums[q] - mean)
            u, v = planes(3 + q) * wet, planes(6 + q) * wet
            put(U0 + q, u, ring=True)
            put(V0 + q, v)
            u, v = 0.1 * u, 0.1 * v
            put(XE + q, u - push)
            put(XW + q, u + push)
            put(YN + q, v - push, ring=True)
            put(YS + q, v + push, ring=True)
        put(E0, planes(9) * wet)
        east, north = planes(10) * wet, planes(11) * wet
        depth = 0.25 * planes(12)
        put(P0, east)
        put(Q0, north)
        put(DEPTH, depth)
        put(DP, depth * east)
        put(DQ, depth * north, ring=True)

    def tracer(self, t, first, rows):
        mid = functools.partial(self.mid, t=t, rows=rows)
        wet = mid(WETS, first=first)
        for q in range(3):
            f = T0 + q
            x = mid(f, first=first)
            xe, xw = self.right(f, t, x, 1, first), self.left(f, t, x, 1, first)
            xee, xww = self.right(f, t, x, 2, first), self.left(f, t, x, 2, first)
            xn, xs = mid(f, first=first + 1), mid(f, first=first - 1)
            xnn, xss = mid(f, first=first + 2), mid(f, first=first - 2)
            dx = (3.2 / 12.0) * (xw - xe) + (0.4 / 12.0) * (xee - xww)
            dy = (3.2 / 12.0) * (xs - xn) + (0.4 / 12.0) * (xnn - xss)
            ring = 0.1 * ((xe + xw) + (xn + xs))
            u, v = mid(U0 + q, first=first), mid(V0 + q, first=first)
            new = 0.6 * x + ring + (u * dx + v * dy)
            self.res[t - self.zero, 48 * q + first - 8 : 48 * q + first - 8 + rows] = wet * new

    def motion(self, t, first, rows):
        row = iota((rows, LANES), 0) + (first - 8)
        north = self.gx * BLOCK + row - jnp.where(row >= 52, HT, 0)
        turn = 0.15 * (2.0 * (north.astype(F32) + 0.5) / LAT - 1.0)
        mid = functools.partial(self.mid, t=t, rows=rows)
        wet = mid(WETS, first=first)
        kept = min(rows, 56 - first)
        gain_x = gain_y = None
        for q in range(3):
            u, v = mid(U0 + q, first=first), mid(V0 + q, first=first)
            xe, xw = mid(XE + q, first=first), mid(XW + q, first=first)
            side_x = self.right(XE + q, t, xe, 1, first) + self.left(XW + q, t, xw, 1, first)
            side_y = mid(YN + q, first=first + 1) + mid(YS + q, first=first - 1)
            ring_u = 0.1 * (mid(U0 + q, first=first + 1) + mid(U0 + q, first=first - 1))
            ring_v = 0.1 * (
                self.right(V0 + q, t, v, 1, first) + self.left(V0 + q, t, v, 1, first)
            )
            new_u = wet * ((0.6 * u + turn * v) + (side_x + ring_u))
            new_v = wet * ((0.6 * v - turn * u) + (side_y + ring_v))
            spot = 144 + 48 * q + first - 8
            self.res[t - self.zero, spot : spot + kept] = new_u[:kept]
            self.res[t - self.zero, spot + 144 : spot + 144 + kept] = new_v[:kept]
            du, dv = new_u - u, new_v - v
            gain_x = du if gain_x is None else gain_x + du
            gain_y = dv if gain_y is None else gain_y + dv
        self.put(GX, t, gain_x * (1.0 / 3.0), first)
        self.put(GY, t, gain_y * (1.0 / 3.0), first)

    def passes(self, strips):
        mid, put = self.mid, self.put
        for last in (False, True):
            for t in strips:
                flux = mid(DP, t)
                div = (self.right(DP, t, flux) - self.left(DP, t, flux)) + (
                    mid(DQ, t, 9) - mid(DQ, t, 7)
                )
                new = mid(E0, t) - mid(WETS, t) * div
                put(E0, t, new)
                put(E0, t, new[48:56], 0)
                put(E0, t, new[0:8], 64)
                if last:
                    self.res[t - self.zero, 432:480] = new[:48]
            for t in strips:
                e, quarter = mid(E0, t), mid(QUARTER, t)
                ex = self.right(E0, t, e) - self.left(E0, t, e)
                ey = mid(E0, t, 9) - mid(E0, t, 7)
                new_p = (mid(P0, t) + mid(GX, t)) - quarter * ex
                new_q = (mid(Q0, t) + mid(GY, t)) - quarter * ey
                if last:
                    self.res[t - self.zero, 480:528] = new_p[:48]
                    self.res[t - self.zero, 528:576] = new_q[:48]
                else:
                    cross = mid(DEPTH, t) * new_q
                    put(P0, t, new_p)
                    put(Q0, t, new_q)
                    put(DP, t, mid(DEPTH, t) * new_p)
                    put(DQ, t, cross)
                    put(DQ, t, cross[48:56], 0)
                    put(DQ, t, cross[0:8], 64)


def cut_pieces(rounds, idx, res, send):
    spots = []
    for c in range(8 * rounds):
        off = 48 * idx[3, c]
        inner = off & 127
        spots.append((off >> 7, inner, (48 * c + 256 - inner) & 127))

    def cut(q):
        pair = 2 * q
        for h in range(rounds):
            done = []
            for start, n in ((64 * q, 64), (512 + 8 * q, 8)):
                rows = pl.ds(start, n) if isinstance(q, int) else pl.ds(pl.multiple_of(start, 8), n)
                lanes = iota((n, LANES), 1)
                moved = []
                for tile, inner, shift in spots[8 * h : 8 * h + 8]:
                    x = jnp.where(lanes >= inner, res[tile, rows], res[tile + 1, rows])
                    moved.append(pltpu.roll(x, shift, 1))
                done.append(pack_tiles(moved))
            mains, rests = done
            for i in range(3):
                base = PIECE * h + 36 * i
                send[pair, base + 32 : base + 40] = rests[i]
                send[pair + 1, base + 28 : base + 36] = rests[i]
            for i in range(3):
                base = PIECE * h + 36 * i
                send[pair, base : base + 32] = mains[i][:32]
                send[pair + 1, base : base + 32] = mains[i][32:]

    if rounds == 1:
        for q in range(8):
            cut(q)
    else:
        pl.loop(0, 8)(cut)


def interior_kernel(*refs):
    tab, raw = refs[0], refs[2:10]
    ext, res, idx, most, edge, col_e, col_w = refs[10:]
    place_tables(tab, idx, most)
    step = Step(ext, res)

    @pl.loop(0, 6)
    def fill(t):
        lanes = pl.ds(pl.multiple_of(t * LANES, LANES), LANES)
        step.place(t, lambda p: read_plane(raw, p, slice(None), lanes), "own")

    lane = iota((BLOCK, LANES), 1)
    to_east = to_west = jnp.zeros((BLOCK, LANES), F32)
    for p in range(PLANES):
        here = (lane >= 4 * p) & (lane < 4 * p + 4)
        east = read_plane(raw, p, slice(None), slice(640, 768))
        west = read_plane(raw, p, slice(None), slice(0, 128))
        edge[p, 0:48] = jnp.where(lane < 64, roll(east, 60, 1), roll(west, 68, 1))
        to_east = jnp.where(here, roll(east, 4 * p + 4, 1), to_east)
        to_west = jnp.where(here, roll(west, 4 * p, 1), to_west)
    col_e[...] = to_east
    col_w[...] = to_west

    @pl.loop(1, 5)
    def inner(t):
        step.tracer(t, 16, 32)
        step.motion(t, 16, 32)


def middle_kernel(
    row_a, row_b, idx, ext_in, res_in, edge_in, ext, res, edge, send, table, sem
):
    copy = pltpu.make_async_copy(idx, table, sem)
    copy.start()
    step = Step(ext, res)
    even_row = step.gx % 2 == 0
    lane = iota((8, LANES), 1)
    for t in range(6):
        lanes = slice(LANES * t, LANES * t + LANES)

        def planes(p, t=t, lanes=lanes):
            rows = slice(8 * (p % 7), 8 * (p % 7) + 8)
            a, b = row_a[rows, lanes], row_b[rows, lanes]
            x = halo_tile(jnp.where(even_row, a, b), jnp.where(even_row, b, a), p)
            if t == 0:
                edge[p, 48:56] = roll(x, 68, 1)
            if t == 5:
                edge[p, 48:56] = jnp.where(lane < 64, roll(x, 60, 1), edge[p, 48:56])
            return x

        step.place(t, planes, "halo")

    @pl.loop(1, 5)
    def rims(t):
        step.tracer(t, 8, 8)
        step.tracer(t, 48, 8)
        step.motion(t, 8, 8)
        step.motion(t, 48, 16)

    for t in (0, 5):
        step.tracer(t, 8, 48)
        step.motion(t, 8, 56)
    step.passes(range(6))
    copy.wait()
    cut_pieces(1, table, res, send)


def finish_kernel(col_a, col_b, idx, edge, send_in, send, res, ext, table, sem):
    copy = pltpu.make_async_copy(idx, table, sem)
    copy.start()
    step = Step(ext, res, 6)
    even = step.gy % 2 == 0
    a, b = col_a[...], col_b[...]
    from_east, from_west = jnp.where(even, a, b), jnp.where(even, b, a)
    lane = iota((HT, LANES), 1)

    def planes(p):
        near = jnp.where(lane < 64, roll(from_east, 60 - 4 * p, 1), roll(from_west, 64 - 4 * p, 1))
        return jnp.where((lane >= 60) & (lane < 68), near, edge[p])

    step.place(6, planes, "all")
    step.tracer(6, 8, 48)
    step.motion(6, 8, 56)
    step.passes((6,))
    copy.wait()

    last = jnp.int32(8)
    for c in range(8):
        last = jnp.where(table[3, c] == 15, c, last)
    off = 48 * jnp.minimum(last, 7) + 44
    rows = pl.ds(36 * (off >> 7), 36)
    inner = off & 127
    west = jnp.where(table[3, 0] == 0, 4, 0)
    east = jnp.where(last < 8, 4, 0)
    lane = iota((36, LANES), 1)
    on_west, on_east = lane < west, (lane >= inner) & (lane < inner + east)
    for k in range(ROW_DEVICES):
        x = jnp.concatenate(
            [res[0, 32 * k : 32 * k + 32], res[0, 512 + 4 * k : 516 + 4 * k]], axis=0
        )
        send[k, 0:36] = jnp.where(on_west, roll(x, 60, 1), send[k, 0:36])
        moved = pltpu.roll(x, (inner + 72) & 127, 1)
        send[k, rows, :] = jnp.where(on_east, moved, send[k, rows, :])


def cut_kernel(idx, res, rim, send, whole):
    for t in range(6):
        whole[t] = res[t]
    for r in range(0, 576, BLOCK):
        rows = slice(r, r + BLOCK)
        lane = iota((BLOCK, LANES), 1)
        x = rim[0, rows]
        whole[0, rows] = jnp.where(lane < 4, roll(x, 60, 1), res[0, rows])
        whole[5, rows] = jnp.where(lane >= 124, roll(x, 68, 1), res[5, rows])
    cut_pieces(2, idx, whole, send)


def route_kernel(rounds, idx, got, send):
    lane = iota((36, LANES), 1)

    def targets(part):
        for j in range(8):
            d = part * 8 + j
            moved = []
            for s in range(SLOTS):
                slot = d * SLOTS + s
                first, after, inner = idx[0, slot], idx[1, slot], idx[2, slot]
                if rounds > 1:
                    first, after = (
                        x + PIECE * (x // PIECE) + PIECE * idx[6, slot] for x in (first, after)
                    )
                near = got[pl.ds(first, 36), :]
                far = got[pl.ds(after, 36), :]
                x = jnp.where(lane >= inner, near, far)
                moved.append(pltpu.roll(x, (48 * s + 256 - inner) & 127, 1))
            for i, x in enumerate(pack_tiles(moved)):
                send[d, 36 * i : 36 * i + 36] = x

    if rounds == 1:
        for part in range(2):
            targets(part)
    else:
        pl.loop(0, 2)(targets)


def settle_kernel(idx, got, heat, zonal, merid, height, east, north):
    used = jnp.broadcast_to(idx[5:6, :], (8, LANES))
    lane = iota((8, LANES), 1)
    low = iota((8, LANES), 0) < 4
    outs = (heat, zonal, merid, height, east, north)

    def put(tile_row, i, x):
        x = jnp.where(lane + LANES * i < used, x, 0.0)
        plane, rows = tile_row // 6, slice(8 * (tile_row % 6), 8 * (tile_row % 6) + 8)
        lanes = slice(LANES * i, LANES * i + LANES)
        if plane < 9:
            outs[plane // 3][plane % 3, rows, lanes] = x
        else:
            outs[plane - 6][rows, lanes] = x

    for i in range(3):
        for k in range(ROW_DEVICES):
            for t in range(4):
                put(4 * k + t, i, got[k, 36 * i + 8 * t : 36 * i + 8 * t + 8, :])
        for q in range(8):
            a = got[2 * q, 36 * i + 32 : 36 * i + 40, :]
            b = got[2 * q + 1, 36 * i + 28 : 36 * i + 36, :]
            put(64 + q, i, jnp.where(low, a, b))


def f32(*shape):
    return jax.ShapeDtypeStruct(shape, F32)


def cost(us):
    return pl.CostEstimate(flops=us * 1_000_000, bytes_accessed=us * 2_000_000, transcendentals=0)


VM = pl.BlockSpec(memory_space=pltpu.VMEM)
SM = pl.BlockSpec(memory_space=pltpu.SMEM)


def shards(heat, zonal, merid, height, east, north, depth, marine, sequence):
    raw = (heat, zonal, merid, height, east, north, depth, marine)
    tab = sequence.reshape(GRID_ROWS, LANES)

    def call(kernel, operands, ins, outs, shapes, mega=8, us=0, **more):
        more = {"in_specs": ins, "out_specs": outs, **more}
        return pl.pallas_call(
            kernel,
            out_shape=shapes,
            compiler_params=pltpu.CompilerParams(vmem_limit_bytes=mega << 20 if mega < 64 else 67_043_328),
            cost_estimate=cost(us) if us else None,
            **more,
        )(*operands)

    strips = [pltpu.VMEM(x.shape[:-2] + (8, 768), x.dtype) for _ in range(2) for x in raw]
    row_a, row_b = call(
        edge_kernel,
        tuple(pltpu.with_memory_space_constraint(x, pltpu.HBM) for x in raw),
        [pl.BlockSpec(memory_space=pltpu.HBM)] * 8,
        (VM, VM),
        (f32(56, 768), f32(56, 768)),
        mega=4,
        scratch_shapes=strips + [pltpu.SemaphoreType.DMA((16,))],
    )
    fields = (f32(FIELDS, STRIPS, STRIP, LANES), f32(STRIPS, 576, LANES))
    ints = jax.ShapeDtypeStruct((8, LANES), I32), jax.ShapeDtypeStruct((1, 1), I32)
    rim = f32(PLANES, HT, LANES)
    side = f32(BLOCK, LANES)
    ext, res, idx, most, edge, col_e, col_w = call(
        interior_kernel,
        (tab, row_a) + raw,
        [VM] * 10,
        (VM,) * 7,
        fields + ints + (rim, side, side),
        us=3,
    )

    def swaps(axis, size, first, second):
        near = [(i, i ^ 1) for i in range(size)]
        far = [(i, i + 1) for i in range(1, size - 1, 2)]
        far += [(j, i) for i, j in far]
        second = lax.ppermute(second, axis, far)
        first = lax.ppermute(first, axis, near)
        return first, second

    row_a, row_b = swaps("gx", GRID_ROWS, row_a, row_b)
    col_a, col_b = call(
        column_kernel,
        (row_a, row_b, col_e, col_w),
        [VM] * 4,
        (VM, VM),
        (f32(56, 128), f32(56, 128)),
        mega=4,
    )
    piece = f32(ROW_DEVICES, PIECE, LANES)
    table = [pltpu.SMEM((8, LANES), I32), pltpu.SemaphoreType.DMA]
    ext, res, edge, send = call(
        middle_kernel,
        (row_a, row_b, idx, ext, res, edge),
        [VM] * 6,
        (VM,) * 4,
        fields + (rim, piece),
        us=3,
        input_output_aliases={3: 0, 4: 1, 5: 2},
        scratch_shapes=table,
    )
    col_a, col_b = swaps("gy", ROW_DEVICES, col_a, col_b)
    send, outer = call(
        finish_kernel,
        (col_a, col_b, idx, edge, send),
        [VM] * 5,
        (VM,) * 2,
        (piece, f32(1, 576, LANES)),
        us=2,
        input_output_aliases={4: 0},
        scratch_shapes=[pltpu.VMEM((FIELDS, 1, STRIP, LANES), F32)] + table,
    )

    def deliver(rounds, send):
        got = lax.all_to_all(send, "gy", 0, 0, tiled=True)
        got = got.reshape(ROW_DEVICES * rounds * PIECE, LANES)
        send = call(functools.partial(route_kernel, rounds), (idx, got), [SM, VM], VM, piece)
        got = lax.all_to_all(send, "gy", 0, 0, tiled=True)
        shapes = (f32(3, 48, 384),) * 3 + (f32(48, 384),) * 3
        return call(settle_kernel, (idx, got), [VM, VM], (VM,) * 6, shapes)

    def crowded():
        both = f32(ROW_DEVICES, 2 * PIECE, LANES)
        whole = [pltpu.VMEM((STRIPS, 576, LANES), F32)]
        ins = [SM, VM, VM]
        return deliver(2, call(cut_kernel, (idx, res, outer), ins, VM, both, scratch_shapes=whole))

    return lax.cond(most[0, 0] > 8, crowded, lambda: deliver(1, send))


def solution(mesh):
    level, flat = P(None, "gx", "gy"), P("gx", "gy")
    return jax.shard_map(
        shards,
        mesh=mesh,
        in_specs=(level,) * 3 + (flat,) * 5 + (P(),),
        out_specs=(P(None, None, ("gx", "gy")),) * 3 + (P(None, ("gx", "gy")),) * 3,
        check_vma=False,
    )
```

```python
import functools

import jax
import jax.numpy as jnp
from jax import lax
from jax.experimental import pallas as pl
from jax.experimental.pallas import tpu as pltpu
from jax.sharding import PartitionSpec as P

BLOCK = 48
SLOTS = 8
ROW_DEVICES = 16
GRID_ROWS = 8
LAT = 384
PLANES = 14
WET = 13
LANES = 128
PIECE = 112

F32 = jnp.float32
I32 = jnp.int32


def iota(shape, dim):
    return lax.broadcasted_iota(I32, shape, dim)


def roll(x, shift, axis):
    return pltpu.roll(x, shift % x.shape[axis], axis)


def plane_of(refs, p):
    if p < 9:
        return refs[p // 3], (p % 3,)
    return refs[3 + p - 9], ()


def read_plane(refs, p, rows, lanes):
    ref, lead = plane_of(refs, p)
    x = ref[lead + (rows, lanes)]
    return x.astype(F32) if p == WET else x


def halo_tile(north, south, p):
    low = iota(north.shape, 0) < 4
    if p < 7:
        return jnp.where(low, north, roll(south, 4, 0))
    return jnp.where(low, roll(north, 4, 0), south)


EDGES = (
    (slice(0, 8), slice(None)),
    (slice(40, 48), slice(None)),
    (slice(None), slice(0, 128)),
    (slice(None), slice(640, 768)),
)


def edge_kernel(*refs):
    raw = refs[:8]
    row_a, row_b, col_a, col_b = refs[8:12]
    parts, sem = refs[12:44], refs[44]
    copies = []
    for i in (2, 3, 0, 1):
        for j, x in enumerate(raw):
            where = (slice(None),) * (len(x.shape) - 2) + EDGES[i]
            n = 8 * i + j
            copies.append(pltpu.make_async_copy(x.at[where], parts[n], sem.at[n]))
            copies[-1].start(priority=1)
    for copy in copies:
        copy.wait()
    bottoms, tops, lefts, rights = (parts[8 * i : 8 * i + 8] for i in range(4))
    even = lax.axis_index("gx") % 2 == 0
    low = iota((8, 768), 0) < 4
    full = slice(None)
    for m in range(7):
        t0, t1 = (read_plane(tops, q, full, full) for q in (m, m + 7))
        b0, b1 = (read_plane(bottoms, q, full, full) for q in (m, m + 7))
        top = jnp.where(low, roll(t0, 4, 0), t1)
        bottom = jnp.where(low, b0, roll(b1, 4, 0))
        row_a[8 * m : 8 * m + 8] = jnp.where(even, top, bottom)
        row_b[8 * m : 8 * m + 8] = jnp.where(even, bottom, top)
    even = lax.axis_index("gy") % 2 == 0
    lane = iota((BLOCK, LANES), 1)
    to_east = to_west = jnp.zeros((BLOCK, LANES), F32)
    for p in range(PLANES):
        here = (lane >= 4 * p) & (lane < 4 * p + 4)
        to_east = jnp.where(here, roll(read_plane(rights, p, full, full), 4 * p + 4, 1), to_east)
        to_west = jnp.where(here, roll(read_plane(lefts, p, full, full), 4 * p, 1), to_west)
    col_a[...] = jnp.where(even, to_east, to_west)
    col_b[...] = jnp.where(even, to_west, to_east)


def place_tables(tab_ref, idx, full):
    gx, gy = lax.axis_index("gx"), lax.axis_index("gy")
    square = (LANES, LANES)
    g = tab_ref[pl.ds(gx, 1), :].astype(F32)
    g_lane = jnp.broadcast_to(g, square)
    diagonal = iota(square, 0) == iota(square, 1)
    g_sub = jnp.sum(jnp.where(diagonal, g_lane, 0.0), axis=1, keepdims=True)
    g_sub = jnp.broadcast_to(g_sub, square)
    d_lane = jnp.floor(g_lane * (1.0 / 16.0))
    d_sub = jnp.floor(g_sub * (1.0 / 16.0))
    same = d_lane == d_sub
    rank_lane = jnp.sum(jnp.where(same & (g_sub < g_lane), 1.0, 0.0), axis=0, keepdims=True)
    rank_sub = jnp.sum(jnp.where(same & (g_lane < g_sub), 1.0, 0.0), axis=1, keepdims=True)
    first = (gx * ROW_DEVICES).astype(F32)
    source = jnp.floor(g * (1.0 / 16.0)) - first
    listed = g >= 0.0
    half = jnp.where(rank_lane >= 8.0, 1.0, 0.0)
    half = jnp.where(listed, half, 0.0)
    place = jnp.where(listed, source, 0.0)
    off = jnp.where(listed, 48.0 * (rank_lane - 8.0 * half), 0.0)
    tile = jnp.floor(off * (1.0 / LANES))
    own = (iota((1, LANES), 1) // SLOTS == gy) & listed
    used = jnp.sum(jnp.where(own, float(BLOCK), 0.0), axis=1, keepdims=True)
    used = jnp.broadcast_to(used, (1, LANES))
    me = (gx * ROW_DEVICES + gy).astype(F32)
    c_lane = iota(square, 1).astype(F32)
    mine = (d_sub == me) & (jnp.broadcast_to(rank_sub, square) == c_lane)
    order = jnp.sum(jnp.where(mine, g_sub - d_sub * 16.0, 0.0), axis=0, keepdims=True)
    count = jnp.zeros(square, F32)
    for r in range(GRID_ROWS):
        owner = jnp.floor(tab_ref[r : r + 1, :].astype(F32) * (1.0 / 16.0))
        count += jnp.where(jnp.broadcast_to(owner, square) == iota(square, 0).astype(F32), 1.0, 0.0)
    most = jnp.max(jnp.sum(count, axis=1, keepdims=True), axis=0, keepdims=True)
    most = jnp.broadcast_to(most, (1, LANES))
    sub = iota((8, LANES), 0)
    table = jnp.where(sub == 3, order, most)
    table = jnp.where(sub == 0, place * PIECE + 36.0 * tile, table)
    table = jnp.where(sub == 1, place * PIECE + 36.0 * jnp.minimum(tile + 1.0, 2.0), table)
    table = jnp.where(sub == 2, off - LANES * tile, table)
    table = jnp.where(sub == 5, used, table)
    table = jnp.where(sub == 6, half, table)
    idx[...] = table.astype(I32)
    full[...] = most[:, :1].astype(I32)


def corner_kernel(col_a, col_b, after, cor_a, cor_b):
    even_row = lax.axis_index("gx") % 2 == 0
    even = lax.axis_index("gy") % 2 == 0
    lane = iota((8, LANES), 1)

    def rows(first):
        a, b = col_a[first : first + 8], col_b[first : first + 8]
        east, west = jnp.where(even, a, b), jnp.where(even, b, a)
        return jnp.where(lane < 64, east, roll(west, 64, 1))

    top, bottom = roll(rows(40), 4, 0), rows(0)
    cor_a[...] = jnp.where(even_row, top, bottom)
    cor_b[...] = jnp.where(even_row, bottom, top)


HT = 56
STRIP = 72
STRIPS = 7
T0, U0, V0 = 0, 3, 6
XE, XW, YN, YS = 9, 12, 15, 18
E0, P0, Q0, DEPTH, WETS, QUARTER, DP, DQ, GX, GY = range(21, 31)
FIELDS = 31


def pack_tiles(r):
    lane = iota(r[0].shape, 1)
    t0 = jnp.where(lane < 48, r[0], jnp.where(lane < 96, r[1], r[2]))
    t1 = jnp.where(
        lane < 16, r[2], jnp.where(lane < 64, r[3], jnp.where(lane < 112, r[4], r[5]))
    )
    t2 = jnp.where(lane < 32, r[5], jnp.where(lane < 80, r[6], r[7]))
    return t0, t1, t2


class Step:
    def __init__(self, ext, res, first=0):
        self.ext, self.res, self.zero = ext, res, first
        self.gx, self.gy = lax.axis_index("gx"), lax.axis_index("gy")

    def put(self, field, t, x, first=8):
        self.ext[field, t - self.zero, first : first + x.shape[0]] = x

    def mid(self, field, t, first=8, rows=HT):
        return self.ext[field, t - self.zero, first : first + rows]

    def right(self, field, t, x, k=1, first=8):
        after = t if isinstance(t, int) and t in (5, 6) else t + 1
        lane = iota(x.shape, 1)
        y = self.mid(field, after, first, x.shape[0])
        return roll(jnp.where(lane < k, y, x), -k, 1)

    def left(self, field, t, x, k=1, first=8):
        before = t if isinstance(t, int) and t in (0, 6) else t - 1
        lane = iota(x.shape, 1)
        y = self.mid(field, before, first, x.shape[0])
        return roll(jnp.where(lane >= LANES - k, y, x), k, 1)

    def place(self, t, planes, part):
        def put(field, x, ring=False):
            if part == "halo":
                self.put(field, t, x, 56)
                if ring:
                    self.put(field, t, x, 0)
            else:
                self.put(field, t, x)
                if ring:
                    self.put(field, t, x[0:8], 64)
                    if part == "all":
                        self.put(field, t, x[48:56], 0)

        wet = planes(WET)
        put(WETS, wet)
        put(QUARTER, 0.25 * wet)
        sums = []
        for q in range(3):
            heat = planes(q) * wet
            put(T0 + q, heat, ring=True)
            b = heat - 0.1 * heat * heat
            sums.append(sums[-1] + b if sums else b)
        mean = (sums[0] + sums[1] + sums[2]) * (1.0 / 3.0)
        for q in range(3):
            push = 0.15 * (sums[q] - mean)
            u, v = planes(3 + q) * wet, planes(6 + q) * wet
            put(U0 + q, u, ring=True)
            put(V0 + q, v)
            u, v = 0.1 * u, 0.1 * v
            put(XE + q, u - push)
            put(XW + q, u + push)
            put(YN + q, v - push, ring=True)
            put(YS + q, v + push, ring=True)
        put(E0, planes(9) * wet)
        east, north = planes(10) * wet, planes(11) * wet
        depth = 0.25 * planes(12)
        put(P0, east)
        put(Q0, north)
        put(DEPTH, depth)
        put(DP, depth * east)
        put(DQ, depth * north, ring=True)

    def tracer(self, t, first, rows):
        mid = functools.partial(self.mid, t=t, rows=rows)
        wet = mid(WETS, first=first)
        for q in range(3):
            f = T0 + q
            x = mid(f, first=first)
            xe, xw = self.right(f, t, x, 1, first), self.left(f, t, x, 1, first)
            xee, xww = self.right(f, t, x, 2, first), self.left(f, t, x, 2, first)
            xn, xs = mid(f, first=first + 1), mid(f, first=first - 1)
            xnn, xss = mid(f, first=first + 2), mid(f, first=first - 2)
            dx = (3.2 / 12.0) * (xw - xe) + (0.4 / 12.0) * (xee - xww)
            dy = (3.2 / 12.0) * (xs - xn) + (0.4 / 12.0) * (xnn - xss)
            ring = 0.1 * ((xe + xw) + (xn + xs))
            u, v = mid(U0 + q, first=first), mid(V0 + q, first=first)
            new = 0.6 * x + ring + (u * dx + v * dy)
            self.res[t - self.zero, 48 * q + first - 8 : 48 * q + first - 8 + rows] = wet * new

    def motion(self, t, first, rows):
        row = iota((rows, LANES), 0) + (first - 8)
        north = self.gx * BLOCK + row - jnp.where(row >= 52, HT, 0)
        turn = 0.15 * (2.0 * (north.astype(F32) + 0.5) / LAT - 1.0)
        mid = functools.partial(self.mid, t=t, rows=rows)
        wet = mid(WETS, first=first)
        kept = min(rows, 56 - first)
        gain_x = gain_y = None
        for q in range(3):
            u, v = mid(U0 + q, first=first), mid(V0 + q, first=first)
            xe, xw = mid(XE + q, first=first), mid(XW + q, first=first)
            side_x = self.right(XE + q, t, xe, 1, first) + self.left(XW + q, t, xw, 1, first)
            side_y = mid(YN + q, first=first + 1) + mid(YS + q, first=first - 1)
            ring_u = 0.1 * (mid(U0 + q, first=first + 1) + mid(U0 + q, first=first - 1))
            ring_v = 0.1 * (
                self.right(V0 + q, t, v, 1, first) + self.left(V0 + q, t, v, 1, first)
            )
            new_u = wet * ((0.6 * u + turn * v) + (side_x + ring_u))
            new_v = wet * ((0.6 * v - turn * u) + (side_y + ring_v))
            spot = 144 + 48 * q + first - 8
            self.res[t - self.zero, spot : spot + kept] = new_u[:kept]
            self.res[t - self.zero, spot + 144 : spot + 144 + kept] = new_v[:kept]
            du, dv = new_u - u, new_v - v
            gain_x = du if gain_x is None else gain_x + du
            gain_y = dv if gain_y is None else gain_y + dv
        self.put(GX, t, gain_x * (1.0 / 3.0), first)
        self.put(GY, t, gain_y * (1.0 / 3.0), first)

    def passes(self, strips):
        mid, put = self.mid, self.put
        for last in (False, True):
            for t in strips:
                flux = mid(DP, t)
                div = (self.right(DP, t, flux) - self.left(DP, t, flux)) + (
                    mid(DQ, t, 9) - mid(DQ, t, 7)
                )
                new = mid(E0, t) - mid(WETS, t) * div
                put(E0, t, new)
                put(E0, t, new[48:56], 0)
                put(E0, t, new[0:8], 64)
                if last:
                    self.res[t - self.zero, 432:480] = new[:48]
            for t in strips:
                e, quarter = mid(E0, t), mid(QUARTER, t)
                ex = self.right(E0, t, e) - self.left(E0, t, e)
                ey = mid(E0, t, 9) - mid(E0, t, 7)
                new_p = (mid(P0, t) + mid(GX, t)) - quarter * ex
                new_q = (mid(Q0, t) + mid(GY, t)) - quarter * ey
                if last:
                    self.res[t - self.zero, 480:528] = new_p[:48]
                    self.res[t - self.zero, 528:576] = new_q[:48]
                else:
                    cross = mid(DEPTH, t) * new_q
                    put(P0, t, new_p)
                    put(Q0, t, new_q)
                    put(DP, t, mid(DEPTH, t) * new_p)
                    put(DQ, t, cross)
                    put(DQ, t, cross[48:56], 0)
                    put(DQ, t, cross[0:8], 64)


def cut_pieces(rounds, idx, res, send):
    spots = []
    for c in range(8 * rounds):
        off = 48 * idx[3, c]
        inner = off & 127
        spots.append((off >> 7, inner, (48 * c + 256 - inner) & 127))

    def cut(q):
        pair = 2 * q
        for h in range(rounds):
            done = []
            for start, n in ((64 * q, 64), (512 + 8 * q, 8)):
                rows = pl.ds(start, n) if isinstance(q, int) else pl.ds(pl.multiple_of(start, 8), n)
                lanes = iota((n, LANES), 1)
                moved = []
                for tile, inner, shift in spots[8 * h : 8 * h + 8]:
                    x = jnp.where(lanes >= inner, res[tile, rows], res[tile + 1, rows])
                    moved.append(pltpu.roll(x, shift, 1))
                done.append(pack_tiles(moved))
            mains, rests = done
            for i in range(3):
                base = PIECE * h + 36 * i
                send[pair, base + 32 : base + 40] = rests[i]
                send[pair + 1, base + 28 : base + 36] = rests[i]
            for i in range(3):
                base = PIECE * h + 36 * i
                send[pair, base : base + 32] = mains[i][:32]
                send[pair + 1, base : base + 32] = mains[i][32:]

    if rounds == 1:
        for q in range(8):
            cut(q)
    else:
        pl.loop(0, 8)(cut)


def interior_kernel(*refs):
    tab, raw = refs[0], refs[2:10]
    ext, res, idx, most, edge = refs[10:]
    place_tables(tab, idx, most)
    step = Step(ext, res)

    @pl.loop(0, 6)
    def fill(t):
        lanes = pl.ds(pl.multiple_of(t * LANES, LANES), LANES)
        step.place(t, lambda p: read_plane(raw, p, slice(None), lanes), "own")

    lane = iota((BLOCK, LANES), 1)
    for p in range(PLANES):
        east = read_plane(raw, p, slice(None), slice(640, 768))
        west = read_plane(raw, p, slice(None), slice(0, 128))
        edge[p, 0:48] = jnp.where(lane < 64, roll(east, 60, 1), roll(west, 68, 1))

    @pl.loop(1, 5)
    def inner(t):
        step.tracer(t, 16, 32)
        step.motion(t, 16, 32)


def middle_kernel(
    row_a, row_b, idx, ext_in, res_in, edge_in, ext, res, edge, send, table, sem
):
    copy = pltpu.make_async_copy(idx, table, sem)
    copy.start()
    step = Step(ext, res)
    even_row = step.gx % 2 == 0
    lane = iota((8, LANES), 1)
    for t in range(6):
        lanes = slice(LANES * t, LANES * t + LANES)

        def planes(p, t=t, lanes=lanes):
            rows = slice(8 * (p % 7), 8 * (p % 7) + 8)
            a, b = row_a[rows, lanes], row_b[rows, lanes]
            x = halo_tile(jnp.where(even_row, a, b), jnp.where(even_row, b, a), p)
            if t == 0:
                edge[p, 48:56] = roll(x, 68, 1)
            if t == 5:
                edge[p, 48:56] = jnp.where(lane < 64, roll(x, 60, 1), edge[p, 48:56])
            return x

        step.place(t, planes, "halo")

    @pl.loop(1, 5)
    def rims(t):
        step.tracer(t, 8, 8)
        step.tracer(t, 48, 8)
        step.motion(t, 8, 8)
        step.motion(t, 48, 16)

    for t in (0, 5):
        step.tracer(t, 8, 48)
        step.motion(t, 8, 56)
    step.passes(range(6))
    copy.wait()
    cut_pieces(1, table, res, send)


def finish_kernel(col_a, col_b, cor_a, cor_b, idx, edge, send_in, send, res, ext, table, sem):
    copy = pltpu.make_async_copy(idx, table, sem)
    copy.start()
    step = Step(ext, res, 6)
    even = step.gy % 2 == 0
    even_row = step.gx % 2 == 0
    a, b = cor_a[...], cor_b[...]
    north, south = jnp.where(even_row, a, b), jnp.where(even_row, b, a)
    corner = jnp.where(iota((8, LANES), 0) < 4, north, roll(south, 4, 0))
    a, b = col_a[...], col_b[...]
    from_east = jnp.concatenate([jnp.where(even, a, b), corner], axis=0)
    from_west = jnp.concatenate([jnp.where(even, b, a), roll(corner, 64, 1)], axis=0)
    lane = iota((HT, LANES), 1)

    def planes(p):
        near = jnp.where(lane < 64, roll(from_east, 60 - 4 * p, 1), roll(from_west, 64 - 4 * p, 1))
        return jnp.where((lane >= 60) & (lane < 68), near, edge[p])

    step.place(6, planes, "all")
    step.tracer(6, 8, 48)
    step.motion(6, 8, 56)
    step.passes((6,))
    copy.wait()

    last = jnp.int32(8)
    for c in range(8):
        last = jnp.where(table[3, c] == 15, c, last)
    off = 48 * jnp.minimum(last, 7) + 44
    rows = pl.ds(36 * (off >> 7), 36)
    inner = off & 127
    west = jnp.where(table[3, 0] == 0, 4, 0)
    east = jnp.where(last < 8, 4, 0)
    lane = iota((36, LANES), 1)
    on_west, on_east = lane < west, (lane >= inner) & (lane < inner + east)
    for k in range(ROW_DEVICES):
        x = jnp.concatenate(
            [res[0, 32 * k : 32 * k + 32], res[0, 512 + 4 * k : 516 + 4 * k]], axis=0
        )
        send[k, 0:36] = jnp.where(on_west, roll(x, 60, 1), send[k, 0:36])
        moved = pltpu.roll(x, (inner + 72) & 127, 1)
        send[k, rows, :] = jnp.where(on_east, moved, send[k, rows, :])


def cut_kernel(idx, res, rim, send, whole):
    for t in range(6):
        whole[t] = res[t]
    for r in range(0, 576, BLOCK):
        rows = slice(r, r + BLOCK)
        lane = iota((BLOCK, LANES), 1)
        x = rim[0, rows]
        whole[0, rows] = jnp.where(lane < 4, roll(x, 60, 1), res[0, rows])
        whole[5, rows] = jnp.where(lane >= 124, roll(x, 68, 1), res[5, rows])
    cut_pieces(2, idx, whole, send)


def route_kernel(rounds, idx, got, send):
    lane = iota((36, LANES), 1)

    def targets(part):
        for j in range(8):
            d = part * 8 + j
            moved = []
            for s in range(SLOTS):
                slot = d * SLOTS + s
                first, after, inner = idx[0, slot], idx[1, slot], idx[2, slot]
                if rounds > 1:
                    first, after = (
                        x + PIECE * (x // PIECE) + PIECE * idx[6, slot] for x in (first, after)
                    )
                near = got[pl.ds(first, 36), :]
                far = got[pl.ds(after, 36), :]
                x = jnp.where(lane >= inner, near, far)
                moved.append(pltpu.roll(x, (48 * s + 256 - inner) & 127, 1))
            for i, x in enumerate(pack_tiles(moved)):
                send[d, 36 * i : 36 * i + 36] = x

    if rounds == 1:
        for part in range(2):
            targets(part)
    else:
        pl.loop(0, 2)(targets)


def settle_kernel(idx, got, heat, zonal, merid, height, east, north):
    used = jnp.broadcast_to(idx[5:6, :], (8, LANES))
    lane = iota((8, LANES), 1)
    low = iota((8, LANES), 0) < 4
    outs = (heat, zonal, merid, height, east, north)

    def put(tile_row, i, x):
        x = jnp.where(lane + LANES * i < used, x, 0.0)
        plane, rows = tile_row // 6, slice(8 * (tile_row % 6), 8 * (tile_row % 6) + 8)
        lanes = slice(LANES * i, LANES * i + LANES)
        if plane < 9:
            outs[plane // 3][plane % 3, rows, lanes] = x
        else:
            outs[plane - 6][rows, lanes] = x

    for i in range(3):
        for k in range(ROW_DEVICES):
            for t in range(4):
                put(4 * k + t, i, got[k, 36 * i + 8 * t : 36 * i + 8 * t + 8, :])
        for q in range(8):
            a = got[2 * q, 36 * i + 32 : 36 * i + 40, :]
            b = got[2 * q + 1, 36 * i + 28 : 36 * i + 36, :]
            put(64 + q, i, jnp.where(low, a, b))


def f32(*shape):
    return jax.ShapeDtypeStruct(shape, F32)


def cost(us):
    return pl.CostEstimate(flops=us * 1_000_000, bytes_accessed=us * 2_000_000, transcendentals=0)


VM = pl.BlockSpec(memory_space=pltpu.VMEM)
SM = pl.BlockSpec(memory_space=pltpu.SMEM)


def shards(heat, zonal, merid, height, east, north, depth, marine, sequence):
    raw = (heat, zonal, merid, height, east, north, depth, marine)
    tab = sequence.reshape(GRID_ROWS, LANES)

    def call(kernel, operands, ins, outs, shapes, mega=8, us=0, **more):
        more = {"in_specs": ins, "out_specs": outs, **more}
        return pl.pallas_call(
            kernel,
            out_shape=shapes,
            compiler_params=pltpu.CompilerParams(vmem_limit_bytes=mega << 20 if mega < 64 else 67_043_328),
            cost_estimate=cost(us) if us else None,
            **more,
        )(*operands)

    strips = [pltpu.VMEM(x.shape[:-2] + (8, 768), x.dtype) for _ in range(2) for x in raw]
    strips += [pltpu.VMEM(x.shape[:-2] + (BLOCK, LANES), x.dtype) for _ in range(2) for x in raw]
    row_a, row_b, col_a, col_b = call(
        edge_kernel,
        tuple(pltpu.with_memory_space_constraint(x, pltpu.HBM) for x in raw),
        [pl.BlockSpec(memory_space=pltpu.HBM)] * 8,
        (VM,) * 4,
        (f32(56, 768), f32(56, 768), f32(BLOCK, LANES), f32(BLOCK, LANES)),
        mega=4,
        scratch_shapes=strips + [pltpu.SemaphoreType.DMA((32,))],
    )
    fields = (f32(FIELDS, STRIPS, STRIP, LANES), f32(STRIPS, 576, LANES))
    ints = jax.ShapeDtypeStruct((8, LANES), I32), jax.ShapeDtypeStruct((1, 1), I32)
    rim = f32(PLANES, HT, LANES)
    ext, res, idx, most, edge = call(
        interior_kernel, (tab, row_a) + raw, [VM] * 10, (VM,) * 5, fields + ints + (rim,), us=3
    )

    full = (most > 8).astype(I32)

    def swaps(axis, size, first, second):
        near = [(i, i ^ 1) for i in range(size)]
        far = [(i, i + 1) for i in range(1, size - 1, 2)]
        far += [(j, i) for i, j in far]
        second = lax.ppermute(second, axis, far)
        first = lax.ppermute(first, axis, near)
        return first, second

    col_a, col_b = swaps("gy", ROW_DEVICES, col_a, col_b)
    row_a, row_b = swaps("gx", GRID_ROWS, row_a, row_b)
    cor_a, cor_b = call(
        corner_kernel,
        (col_a, col_b, full),
        [VM] * 3,
        (VM, VM),
        (f32(8, LANES), f32(8, LANES)),
        mega=4,
    )
    piece = f32(ROW_DEVICES, PIECE, LANES)
    table = [pltpu.SMEM((8, LANES), I32), pltpu.SemaphoreType.DMA]
    ext, res, edge, send = call(
        middle_kernel,
        (row_a, row_b, idx, ext, res, edge),
        [VM] * 6,
        (VM,) * 4,
        fields + (rim, piece),
        us=3,
        input_output_aliases={3: 0, 4: 1, 5: 2},
        scratch_shapes=table,
    )
    cor_a, cor_b = swaps("gx", GRID_ROWS, cor_a, cor_b)
    send, outer = call(
        finish_kernel,
        (col_a, col_b, cor_a, cor_b, idx, edge, send),
        [VM] * 7,
        (VM,) * 2,
        (piece, f32(1, 576, LANES)),
        us=2,
        input_output_aliases={6: 0},
        scratch_shapes=[pltpu.VMEM((FIELDS, 1, STRIP, LANES), F32)] + table,
    )

    def deliver(rounds, send):
        got = lax.all_to_all(send, "gy", 0, 0, tiled=True)
        got = got.reshape(ROW_DEVICES * rounds * PIECE, LANES)
        send = call(functools.partial(route_kernel, rounds), (idx, got), [SM, VM], VM, piece)
        got = lax.all_to_all(send, "gy", 0, 0, tiled=True)
        shapes = (f32(3, 48, 384),) * 3 + (f32(48, 384),) * 3
        return call(settle_kernel, (idx, got), [VM, VM], (VM,) * 6, shapes)

    def crowded():
        both = f32(ROW_DEVICES, 2 * PIECE, LANES)
        whole = [pltpu.VMEM((STRIPS, 576, LANES), F32)]
        ins = [SM, VM, VM]
        return deliver(2, call(cut_kernel, (idx, res, outer), ins, VM, both, scratch_shapes=whole))

    return lax.cond(full[0, 0] > 0, crowded, lambda: deliver(1, send))


def solution(mesh):
    level, flat = P(None, "gx", "gy"), P("gx", "gy")
    return jax.shard_map(
        shards,
        mesh=mesh,
        in_specs=(level,) * 3 + (flat,) * 5 + (P(),),
        out_specs=(P(None, None, ("gx", "gy")),) * 3 + (P(None, ("gx", "gy")),) * 3,
        check_vma=False,
    )
```
